32 devices in a mesh: drift: 16 (over z, x, core), radius: 2 (over y).
Axes of the slice: x: 2, y: 2, z: 4, core: 2. Of those that a mesh axis runs over, the one named last changes fastest.
Arguments:
- ions: float32 [256, 128, 256], P('drift', 'radius'), may hold values from 0 to 2
- potential_guess: float32 [256, 128, 256], P('drift', 'radius'), may hold values from -6 to 6
- permittivity: float32 [256, 128, 256], P('drift', 'radius'), may hold values from 0.5 to 2
- recombination: float32 [128, 256], P('radius'), may hold values from 0.1 to 1
- rate_index: int32 [128, 256], P('radius'), may hold values from 0 to 15
- gap_mask: int32 [128, 256], P('radius'), may hold values 0 or 1
- rate_table: float32 [16], replicated, may hold values from 0.2 to 2
Outputs:
- charge: float32 [256, 128, 256], P('drift', 'radius')
- potential: float32 [256, 128, 256], P('drift', 'radius')
- distortion: float32 [2, 256, 128, 256], P(None, 'drift', 'radius')
The draws below stay inside these ranges and needn't reach their ends.
All inputs are finite; a program needn't handle non-finite values. No bound on the sum of `gap_mask` on one device may be relied on, other than what follows from the above.
Results may differ from the reference program's by a relative error of at most 0.0003.
Values sent between devices are 32-bit elements; how exact they have to be, the bound alone decides.
No kernel may reach another device: no remote copies, remote signals or barrier semaphores. Data moves between devices by JAX's collectives and lax.ppermute only.
A program may use at most 64 MiB of HBM per device.

```python
import math
import jax
import jax.numpy as jnp

CZ = 16
NA = 256
RATES = 16
TRANSITS = 2
SWEEPS = 4
NZ = 256
NR = 128


def place_ends(result, own_key, least, high):
    extent = result.shape
    index_at = [jax.random.randint(jax.random.fold_in(own_key, axis), (), 0, extent[axis]) for axis in range(len(extent))]
    result = result.at[tuple(index_at)].set(least)
    longest = extent.index(max(extent))
    index_at[longest] = (index_at[longest] + 1) % extent[longest]
    return result.at[tuple(index_at)].set(high)


def steps_of(stream_key, dims, shards, least, largest):
    loudness = 1.0
    for axis_at, shards_of in shards:
        steps = jax.random.uniform(jax.random.fold_in(jax.random.fold_in(stream_key, 6), axis_at), (shards_of,), jnp.float32, least / len(shards), largest / len(shards))
        loudness = loudness * jnp.repeat(jnp.exp(steps), dims[axis_at] // shards_of).reshape((-1,) + (1,) * (len(dims) - 1 - axis_at))
    return loudness


def scatter_about(rng, dims, spread, limit, shards=(), kind=jnp.bfloat16):
    array = jax.random.normal(rng, dims, jnp.float32) * spread
    if len(shards) > 0:
        array = steps_of(rng, dims, shards, -0.22, 0.18) * array
    return jnp.clip(array, min=-limit, max=limit).astype(kind)


def setup_inputs(seed: int = 0) -> dict:
    key_list = jax.random.split(jax.random.key(seed), 8)
    ions = jnp.clip(2.0 * jax.random.uniform(key_list[0], (NZ, NR, NA), jnp.float32) ** steps_of(key_list[0], (NZ, NR, NA), ((0, 16), (1, 2)), -0.2, 0.2), 0.0, 2.0)
    potential_guess = scatter_about(key_list[1], (NZ, NR, NA), 1.0, 6.0, ((0, 16), (1, 2)), jnp.float32)
    permittivity = jnp.clip(jnp.exp(math.log(2.0) - 1.3862944 * jax.random.uniform(key_list[2], (NZ, NR, NA), jnp.float32) ** steps_of(key_list[2], (NZ, NR, NA), ((0, 16), (1, 2)), -0.2, 0.2)), 0.5, 2.0)
    recombination = jnp.clip(jnp.exp(math.log(1.0) - 2.3025851 * jax.random.uniform(key_list[3], (NR, NA), jnp.float32) ** steps_of(key_list[3], (NR, NA), ((0, 2),), -0.2, 0.2)), 0.1, 1.0)
    rate_index = place_ends(jax.random.randint(key_list[4], (NR, NA), 0, RATES), jax.random.fold_in(key_list[4], 1), 0, RATES - 1).astype(jnp.int32)
    gap_mask = place_ends((jax.random.randint(key_list[5], (NR, NA), 0, 4) < 1).astype(jnp.int32), jax.random.fold_in(key_list[5], 1), 0, 1)
    rate_table = jnp.clip(jnp.exp(jax.random.uniform(key_list[6], (RATES,), jnp.float32, math.log(0.2), math.log(2.0))), 0.2, 2.0)
    return dict(ions=ions, potential_guess=potential_guess, permittivity=permittivity, recombination=recombination, rate_index=rate_index, gap_mask=gap_mask, rate_table=rate_table)


def relax(phi_x, rho_x, eps_x, rpos_x, inside_x, half):
    phi_a = jnp.pad(phi_x, ((0, 0), (0, 0), (1, 1)))
    eps_a = jnp.pad(eps_x, ((0, 0), (0, 0), (1, 1)))
    center = eps_x[1:-1, 1:-1]
    radial = rpos_x[1:-1][:, None]
    z_up = 0.5 * (center + eps_x[2:, 1:-1])
    z_down = 0.5 * (center + eps_x[:-2, 1:-1])
    r_up = 0.5 * (center + eps_x[1:-1, 2:]) * ((radial + half) / radial)
    r_down = 0.5 * (center + eps_x[1:-1, :-2]) * ((radial - half) / radial)
    a_up = 0.5 * (center + eps_a[1:-1, 1:-1, 2:]) / (radial * radial)
    a_down = 0.5 * (center + eps_a[1:-1, 1:-1, :-2]) / (radial * radial)
    total = z_up * phi_x[2:, 1:-1] + z_down * phi_x[:-2, 1:-1]
    total = total + r_up * phi_x[1:-1, 2:] + r_down * phi_x[1:-1, :-2]
    total = total + a_up * phi_a[1:-1, 1:-1, 2:] + a_down * phi_a[1:-1, 1:-1, :-2]
    diag = z_up + z_down + r_up + r_down + a_up + a_down
    inner = inside_x[1:-1, 1:-1]
    safe = jnp.where(inner > 0, diag, 1.0)
    return (rho_x[1:-1, 1:-1] + total) / safe * inner


def padded(field):
    return jnp.pad(field, ((1, 1), (1, 1), (0, 0)))


def reference(ions, potential_guess, permittivity, recombination, rate_index, gap_mask, rate_table):
    inject = rate_table[rate_index] * (1 - gap_mask).astype(jnp.float32)
    charge = ions
    for step in range(TRANSITS):
        shifted = jnp.concatenate([jnp.zeros((CZ, NR, NA), jnp.float32), charge[:-CZ]], axis=0)
        charge = shifted / (1.0 + recombination * shifted) + inject
    rpos_x = ((NR + jnp.arange(-1, NR + 1)).astype(jnp.float32) + 0.5) / NR
    inside_x = padded(jnp.ones((NZ, NR, 1), jnp.float32))
    half = 0.5 / NR
    rho_x = padded(charge)
    eps_x = padded(permittivity)
    potential = potential_guess
    for sweep in range(SWEEPS):
        potential = relax(padded(potential), rho_x, eps_x, rpos_x, inside_x, half)
    radial_ext = jnp.pad(potential, ((0, 0), (1, 1), (0, 0)))
    azimuth_ext = jnp.pad(potential, ((0, 0), (0, 0), (1, 1)))
    radial = rpos_x[1:-1][:, None]
    field_r = -(radial_ext[:, 2:] - radial_ext[:, :-2]) * 0.5
    field_a = -(azimuth_ext[:, :, 2:] - azimuth_ext[:, :, :-2]) * 0.5 / radial
    scale = 1.0 / (8.0 * 1.09)
    ratios = jnp.stack([(field_r + 0.3 * field_a) * scale, (field_a - 0.3 * field_r) * scale])
    distortion = jnp.cumsum(ratios, axis=1)
    return charge, potential, distortion
```

```python
import jax
import jax.numpy as jnp
from jax import lax
from jax.experimental import pallas as pl
from jax.experimental.pallas import tpu as pltpu
from jax.sharding import PartitionSpec as P

SWEEPS = 4
ROWS = 8
VMEM = pltpu.MemorySpace.VMEM


def shifted(block, axis, distance):
    count = lax.axis_size(axis)
    route = [(i, i + distance) for i in range(count) if 0 <= i + distance < count]
    return lax.ppermute(block, axis, route)


def edges(block):
    band = block.shape[-2]
    if lax.axis_size("radius") == 2:
        start = jnp.where(lax.axis_index("radius") == 0, band - ROWS, 0)
        return (lax.dynamic_slice_in_dim(block, start, ROWS, axis=block.ndim - 2),)
    tail = lax.slice_in_dim(block, band - ROWS, band, axis=block.ndim - 2)
    head = lax.slice_in_dim(block, 0, ROWS, axis=block.ndim - 2)
    return (tail, head)


def radial(blocks):
    if len(blocks) == 1:
        got = lax.ppermute(blocks[0], "radius", [(0, 1), (1, 0)])
        return got, got
    return shifted(blocks[0], "radius", 1), shifted(blocks[1], "radius", -1)


def transit(slab, rec, inj):
    return slab / (1.0 + rec * slab) + inj


def roll(x, amount, axis):
    return pltpu.roll(x, amount % x.shape[axis], axis)


def lane_pair(x, lane):
    return roll(x, -1, 1), roll(x, 1, 1)


def relax_kernel(
    phi, eps, moved, moved_lo, moved_hi, raw_lo, raw_hi, below, above, far, corner_lo, corner_hi, pads,
    charge_out, potential_out, window_out, sums_out,
    p0, p1, ex, bx, wzu, wzd, wru, wrd, wau, wad, geo,
):
    layers, band, sector = phi.shape
    depth = SWEEPS
    zs = layers + 2 * depth
    rows = band + 2 * ROWS
    d, drifts = lax.axis_index("drift"), lax.axis_size("drift")
    r, bands = lax.axis_index("radius"), lax.axis_size("radius")
    total_r = band * bands
    has_lo, has_hi = r > 0, r < bands - 1
    own = slice(ROWS, ROWS + band)
    top = slice(ROWS + band, rows)
    tiles = rows // ROWS

    def blank(cond, value):
        return jnp.where(cond, value, 0.0)

    n = layers
    for dst, src, base, at_lo, at_hi in ((p0, phi, 0, 0, 0), (ex, eps, n, depth, depth)):
        dst[0:depth, own] = below[at_lo : at_lo + depth]
        dst[depth : depth + n, own] = src[...]
        dst[depth + n : zs, own] = above[at_hi : at_hi + depth]
        for side, raw, corner, has in ((slice(0, ROWS), raw_lo, corner_lo, has_lo), (top, raw_hi, corner_hi, has_hi)):
            dst[0:depth, side] = blank(has, corner[at_lo : at_lo + depth])
            dst[depth : depth + n, side] = blank(has, raw[base : base + n])
            up = 3 * depth - 1 + at_hi
            dst[depth + n : zs, side] = blank(has, corner[up : up + depth])

    row = lax.broadcasted_iota(jnp.int32, (rows, sector), 0) - ROWS + r * band
    lane = lax.broadcasted_iota(jnp.int32, (rows, sector), 1)
    rpos = ((total_r + row).astype(jnp.float32) + 0.5) / total_r
    half = 0.5 / total_r
    inside = (row >= 0) & (row < total_r)
    geo[0] = (rpos + half) / rpos
    geo[1] = (rpos - half) / rpos
    geo[2] = 1.0 / (rpos * rpos)
    geo[3] = jnp.where(inside, 1.0, 0.0)
    geo[4] = jnp.where(lane == sector - 1, 0.0, 1.0)
    geo[5] = jnp.where(lane == 0, 0.0, 1.0)
    geo[6, own] = pads[0]
    geo[7, own] = pads[1]
    for side, raw, has in ((slice(0, ROWS), raw_lo, has_lo), (top, raw_hi, has_hi)):
        geo[6, side] = blank(has, raw[3 * n])
        geo[7, side] = blank(has, raw[3 * n + 1])

    def drift_charge(ions, at, slab):
        rec, inj = geo[6, at], geo[7, at]
        once = transit(ions, rec, inj)
        return transit(jnp.where(slab >= 1, once, 0.0), rec, inj)

    @pl.loop(0, n)
    def _(z):
        value = drift_charge(moved[z], own, d)
        charge_out[z] = value
        bx[depth + z, own] = value
        bx[depth + z, 0:ROWS] = drift_charge(blank(has_lo, moved_lo[z]), slice(0, ROWS), d)
        bx[depth + z, top] = drift_charge(blank(has_hi, moved_hi[z]), top, d)

    for k in range(depth - 1):
        for z, ions, slab, at in ((1 + k, far, d - 1, k), (depth + n + k, below, d + 1, 2 * depth + k)):
            bx[z, own] = drift_charge(ions[at], own, slab)
            spot = 5 * depth - 1 + k if ions is far else 2 * depth + k
            bx[z, 0:ROWS] = drift_charge(blank(has_lo, corner_lo[spot]), slice(0, ROWS), slab)
            bx[z, top] = drift_charge(blank(has_hi, corner_hi[spot]), top, slab)

    sub = lax.broadcasted_iota(jnp.int32, (ROWS, sector), 0)

    def row_pairs(ref, z):
        x = [ref[z, t * ROWS : (t + 1) * ROWS] for t in range(tiles)]
        up = [roll(v, -1, 0) for v in x]
        down = [roll(v, 1, 0) for v in x]
        for t in range(tiles):
            higher = jnp.where(sub == ROWS - 1, up[(t + 1) % tiles], up[t])
            lower = jnp.where(sub == 0, down[(t - 1) % tiles], down[t])
            yield t, slice(t * ROWS, (t + 1) * ROWS), x[t], higher, lower

    @pl.loop(1, zs - 1)
    def _(z):
        zg = d * n - depth + z
        alive = jnp.where((zg >= 0) & (zg < drifts * n), 1.0, 0.0)
        for t, at, e, e_up, e_down in row_pairs(ex, z):
            right, left = lane_pair(e, None)
            not_last, not_first = geo[4, at], geo[5, at]
            inv_r2 = geo[2, at]
            zu = e + ex[z + 1, at]
            zd = e + ex[z - 1, at]
            ru = (e + e_up) * geo[0, at]
            rd = (e + e_down) * geo[1, at]
            au = (e + right * not_last) * inv_r2
            ad = (e + left * not_first) * inv_r2
            diag = ((zu + zd) + (ru + rd)) + (au + ad)
            keep = geo[3, at] * alive
            inv = jnp.where(keep > 0, 1.0 / diag, 0.0)
            wzu[z, at] = zu * inv
            wzd[z, at] = zd * inv
            wru[z, at] = ru * inv
            wrd[z, at] = rd * inv
            wau[z, at] = au * inv * not_last
            wad[z, at] = ad * inv * not_first
            bx[z, at] = bx[z, at] * (inv + inv)

    sums_out[...] = jnp.zeros_like(sums_out)
    for sweep in range(1, SWEEPS + 1):
        src, dst = (p0, p1) if sweep % 2 else (p1, p0)
        last = sweep == SWEEPS

        @pl.loop(sweep, zs - sweep)
        def _(z, src=src, dst=dst, last=last):
            for t, at, p, p_up, p_down in row_pairs(src, z):
                right, left = lane_pair(p, None)
                total = bx[z, at] + (wzu[z, at] * src[z + 1, at] + wzd[z, at] * src[z - 1, at])
                total = total + (wru[z, at] * p_up + wrd[z, at] * p_down)
                total = total + (wau[z, at] * right + wad[z, at] * left)
                if last:
                    window_out[z - depth, at] = total
                    sums_out[at] += total
                    if 0 < t < tiles - 1:
                        potential_out[z - depth, (t - 1) * ROWS : t * ROWS] = total
                else:
                    dst[z, at] = total


def integrate_kernel(window, prefix, out, run):
    layers, rows, sector = window.shape
    band = rows - 2 * ROWS
    r, bands = lax.axis_index("radius"), lax.axis_size("radius")
    total_r = band * bands
    tiles = rows // ROWS
    run[...] = prefix[...]
    sub = lax.broadcasted_iota(jnp.int32, (ROWS, sector), 0)
    lane = lax.broadcasted_iota(jnp.int32, (ROWS, sector), 1)
    scale = 1.0 / (8.0 * 1.09)

    @pl.loop(0, layers)
    def _(z):
        x = []
        for t in range(tiles):
            at = slice(t * ROWS, (t + 1) * ROWS)
            value = run[at] + window[z, at]
            run[at] = value
            x.append(value)
        up = [roll(v, -1, 0) for v in x]
        down = [roll(v, 1, 0) for v in x]
        for t in range(1, tiles - 1):
            row = sub + ((t - 1) * ROWS + r * band)
            rpos = ((total_r + row).astype(jnp.float32) + 0.5) / total_r
            higher = jnp.where(sub == ROWS - 1, up[t + 1], up[t])
            lower = jnp.where(sub == 0, down[t - 1], down[t])
            right = jnp.where(lane == sector - 1, 0.0, roll(x[t], -1, 1))
            left = jnp.where(lane == 0, 0.0, roll(x[t], 1, 1))
            er = (lower - higher) * 0.5
            ea = (left - right) * (0.5 / rpos)
            at = slice((t - 1) * ROWS, t * ROWS)
            out[0, z, at] = (er + 0.3 * ea) * scale
            out[1, z, at] = (ea - 0.3 * er) * scale


def sums_below(sums):
    count, mine = lax.axis_size("drift"), lax.axis_index("drift")
    assert count & (count - 1) == 0
    total, below, step = sums, jnp.zeros_like(sums), 1
    while step < count:
        other = lax.ppermute(total, "drift", [(i, i ^ step) for i in range(count)])
        below = below + jnp.where((mine & step) > 0, other, 0.0)
        total = total + other
        step *= 2
    return below


def body(ions, potential_guess, permittivity, recombination, rate_index, gap_mask, rate_table):
    layers, band, sector = ions.shape
    rows = band + 2 * ROWS
    zs = layers + 2 * SWEEPS
    f32 = jnp.float32
    levels = jnp.arange(rate_table.shape[0], dtype=jnp.int32)
    picked = jnp.sum(jnp.where(rate_index[:, :, None] == levels, rate_table, 0.0), axis=2)
    inject = picked * (1 - gap_mask).astype(f32)
    pads = jnp.stack([recombination, inject])

    up_block = jnp.concatenate(
        [potential_guess[layers - SWEEPS :], permittivity[layers - SWEEPS :], ions[: SWEEPS - 1]]
    )
    down_block = jnp.concatenate([potential_guess[:SWEEPS], permittivity[:SWEEPS]])
    below = shifted(up_block, "drift", 1)
    above = shifted(down_block, "drift", -1)
    far = shifted(ions[layers - SWEEPS + 1 :], "drift", 3)
    raw_lo, raw_hi = radial(
        tuple(jnp.concatenate(parts) for parts in zip(edges(potential_guess), edges(permittivity), edges(ions), edges(pads)))
    )
    swapped = len(edges(pads)) == 1
    moved_lo = shifted(raw_lo[2 * layers : 3 * layers], "drift", 2)
    moved_hi = moved_lo if swapped else shifted(raw_hi[2 * layers : 3 * layers], "drift", 2)
    moved = shifted(ions, "drift", 2)
    corner_lo, corner_hi = radial(
        tuple(jnp.concatenate(parts) for parts in zip(edges(below), edges(above), edges(far)))
    )
    plane = lambda *shape: jax.ShapeDtypeStruct(shape, f32)
    box = pltpu.VMEM((zs, rows, sector), f32)
    charge, potential, window, sums = pl.pallas_call(
        relax_kernel,
        out_shape=(
            plane(layers, band, sector),
            plane(layers, band, sector),
            plane(layers, rows, sector),
            plane(rows, sector),
        ),
        in_specs=[pl.BlockSpec(memory_space=VMEM)] * 13,
        out_specs=[pl.BlockSpec(memory_space=VMEM)] * 4,
        scratch_shapes=[box] * 10 + [pltpu.VMEM((8, rows, sector), f32)],
        name="relax",
    )(
        potential_guess, permittivity, moved, moved_lo, moved_hi, raw_lo, raw_hi, below, above, far,
        corner_lo, corner_hi, pads,
    )
    below_sums = sums_below(sums)
    distortion = pl.pallas_call(
        integrate_kernel,
        out_shape=plane(2, layers, band, sector),
        in_specs=[pl.BlockSpec(memory_space=VMEM)] * 2,
        out_specs=pl.BlockSpec(memory_space=VMEM),
        scratch_shapes=[pltpu.VMEM((rows, sector), f32)],
        name="integrate",
    )(window, below_sums)
    return charge, potential, distortion


def solution(mesh):
    return jax.shard_map(
        body,
        mesh=mesh,
        in_specs=(
            P("drift", "radius", None),
            P("drift", "radius", None),
            P("drift", "radius", None),
            P("radius", None),
            P("radius", None),
            P("radius", None),
            P(),
        ),
        out_specs=(
            P("drift", "radius", None),
            P("drift", "radius", None),
            P(None, "drift", "radius", None),
        ),
        check_vma=False,
    )
```

```python
import functools

import jax
import jax.numpy as jnp
from jax import lax
from jax.experimental import pallas as pl
from jax.experimental.pallas import tpu as pltpu
from jax.sharding import PartitionSpec as P

SWEEPS = 4
ROWS = 8
F32 = jnp.float32
IN_VMEM = pl.BlockSpec(memory_space=pltpu.VMEM)
ANYWHERE = pl.BlockSpec(memory_space=pl.ANY)


def plane(*shape):
    return jax.ShapeDtypeStruct(shape, F32)


def near(*shape):
    return pltpu.VMEM(shape, F32)


def fetched(x):
    return pltpu.with_memory_space_constraint(x, pltpu.VMEM)


def shifted(block, axis, distance):
    count = lax.axis_size(axis)
    route = [(i, i + distance) for i in range(count) if 0 <= i + distance < count]
    return lax.ppermute(block, axis, route)


def edges(block):
    band = block.shape[-2]
    if lax.axis_size("radius") == 2:
        start = jnp.where(lax.axis_index("radius") == 0, band - ROWS, 0)
        return (lax.dynamic_slice_in_dim(block, start, ROWS, axis=block.ndim - 2),)
    tail = lax.slice_in_dim(block, band - ROWS, band, axis=block.ndim - 2)
    head = lax.slice_in_dim(block, 0, ROWS, axis=block.ndim - 2)
    return (tail, head)


def radial(blocks):
    if len(blocks) == 1:
        return [lax.ppermute(blocks[0], "radius", [(0, 1), (1, 0)])]
    return [shifted(blocks[0], "radius", 1), shifted(blocks[1], "radius", -1)]


def transit(slab, rec, inj):
    return slab / (1.0 + rec * slab) + inj


def drift_charge(ions, rec, inj, slab):
    once = transit(ions, rec, inj)
    return transit(jnp.where(slab >= 1, once, 0.0), rec, inj)


def roll(x, amount, axis):
    return pltpu.roll(x, amount % x.shape[axis], axis)


def row_tiles(load, tiles, sub):
    x = [load(slice(t * ROWS, (t + 1) * ROWS)) for t in range(tiles)]
    up = [roll(v, -1, 0) for v in x]
    down = [roll(v, 1, 0) for v in x]
    for t in range(tiles):
        higher = jnp.where(sub == ROWS - 1, up[(t + 1) % tiles], up[t])
        lower = jnp.where(sub == 0, down[(t - 1) % tiles], down[t])
        yield t, slice(t * ROWS, (t + 1) * ROWS), x[t], higher, lower


def pack_kernel(split, phi, eps, ions, rec, index, gap, table, up, down, far, first, second, *rest):
    sides, pads, sems = rest[:-2], rest[-2], rest[-1]
    layers, band, sector = phi.shape
    depth = SWEEPS
    copies = [
        (ions.at[0:split], first),
        (phi.at[layers - depth :], up.at[0:depth]),
        (eps.at[layers - depth :], up.at[depth : 2 * depth]),
        (ions.at[0 : depth - 1], up.at[2 * depth :]),
        (phi.at[0:depth], down.at[0:depth]),
        (eps.at[0:depth], down.at[depth:]),
        (ions.at[layers - depth + 1 :], far),
        (ions.at[split:], second),
    ]
    if len(sides) == 1:
        starts = [pl.multiple_of(jnp.where(lax.axis_index("radius") == 0, band - ROWS, 0), ROWS)]
    else:
        starts = [band - ROWS, 0]
    for start, side in zip(starts, sides):
        rows = pl.ds(start, ROWS)
        for k, src in enumerate((phi, eps, ions)):
            copies.append((src.at[:, rows], side.at[k * layers : (k + 1) * layers]))
    running = [pltpu.make_async_copy(src, dst, sems.at[k]) for k, (src, dst) in enumerate(copies)]
    for copy in running:
        copy.start()
    levels = table.shape[0]
    for t in range(band // ROWS):
        at = slice(t * ROWS, (t + 1) * ROWS)
        which = index[at]
        picked = jnp.zeros((ROWS, sector), F32)
        for k in range(levels):
            picked = jnp.where(which == k, table[k], picked)
        pads[0, at] = rec[at]
        pads[1, at] = picked * (1 - gap[at]).astype(F32)
    for start, side in zip(starts, sides):
        rows = pl.ds(start, ROWS)
        side[3 * layers] = pads[0, rows]
        side[3 * layers + 1] = pads[1, rows]
    for copy in running:
        copy.wait()


def coupling_kernel(sides, phi, eps, below, above, far, pads, *refs):
    raws, corners, moveds = refs[:sides], refs[sides : 2 * sides], refs[2 * sides : 3 * sides]
    p0, w, bx, ex, geo = refs[3 * sides :]
    layers, band, sector = phi.shape
    depth, n = SWEEPS, layers
    zs = n + 2 * depth
    rows = band + 2 * ROWS
    d, drifts = lax.axis_index("drift"), lax.axis_size("drift")
    r, bands = lax.axis_index("radius"), lax.axis_size("radius")
    total_r = band * bands
    own, top = slice(ROWS, ROWS + band), slice(ROWS + band, rows)
    ends = ((slice(0, ROWS), 0, r > 0), (top, sides - 1, r < bands - 1))
    tiles = rows // ROWS
    sub = lax.broadcasted_iota(jnp.int32, (ROWS, sector), 0)

    def blank(cond, value):
        return jnp.where(cond, value, 0.0)

    for dst, src, base, start in ((p0, phi, 0, 0), (ex, eps, n, depth)):
        dst[0:depth, own] = below[start : start + depth]
        dst[depth : depth + n, own] = src[...]
        dst[depth + n : zs, own] = above[start : start + depth]
        for at, side, has in ends:
            dst[0:depth, at] = blank(has, corners[side][start : start + depth])
            dst[depth : depth + n, at] = blank(has, raws[side][base : base + n])
            up = 3 * depth - 1 + start
            dst[depth + n : zs, at] = blank(has, corners[side][up : up + depth])

    row = lax.broadcasted_iota(jnp.int32, (rows, sector), 0) - ROWS + r * band
    lane = lax.broadcasted_iota(jnp.int32, (rows, sector), 1)
    rpos = ((total_r + row).astype(F32) + 0.5) / total_r
    half = 0.5 / total_r
    geo[0] = (rpos + half) / rpos
    geo[1] = (rpos - half) / rpos
    geo[2] = 1.0 / (rpos * rpos)
    geo[3] = jnp.where((row >= 0) & (row < total_r), 1.0, 0.0)
    geo[4] = jnp.where(lane == sector - 1, 0.0, 1.0)
    geo[5] = jnp.where(lane == 0, 0.0, 1.0)
    for k in range(2):
        geo[6 + k, own] = pads[k]
        for at, side, has in ends:
            geo[6 + k, at] = blank(has, raws[side][3 * n + k])

    @pl.loop(0, n)
    def _(z):
        for at, side, has in ends:
            bx[depth + z, at] = drift_charge(blank(has, moveds[side][z]), geo[6, at], geo[7, at], d)

    for k in range(depth - 1):
        for z, ions, slab, spot, corner in (
            (1 + k, far, d - 1, k, 5 * depth - 1 + k),
            (depth + n + k, below, d + 1, 2 * depth + k, 2 * depth + k),
        ):
            bx[z, own] = drift_charge(ions[spot], geo[6, own], geo[7, own], slab)
            for at, side, has in ends:
                bx[z, at] = drift_charge(blank(has, corners[side][corner]), geo[6, at], geo[7, at], slab)

    @pl.loop(1, zs - 1)
    def _(z):
        zg = d * n - depth + z
        alive = jnp.where((zg >= 0) & (zg < drifts * n), 1.0, 0.0)
        outer = (z < depth) | (z >= depth + n)
        for t, at, e, e_up, e_down in row_tiles(lambda s: ex[z, s], tiles, sub):
            not_last, not_first = geo[4, at], geo[5, at]
            right, left = roll(e, -1, 1), roll(e, 1, 1)
            inv_r2 = geo[2, at]
            zu = e + ex[z + 1, at]
            zd = e + ex[z - 1, at]
            ru = (e + e_up) * geo[0, at]
            rd = (e + e_down) * geo[1, at]
            au = (e + right * not_last) * inv_r2
            ad = (e + left * not_first) * inv_r2
            diag = ((zu + zd) + (ru + rd)) + (au + ad)
            inv = jnp.where(geo[3, at] * alive > 0, 1.0 / diag, 0.0)
            for k, value in enumerate((zu, zd, ru, rd)):
                w[k, z, at] = value * inv
            w[4, z, at] = au * inv * not_last
            w[5, z, at] = ad * inv * not_first
            twice = inv + inv
            if t in (0, tiles - 1):
                bx[z, at] = bx[z, at] * twice
            else:
                bx[z, at] = jnp.where(outer, bx[z, at] * twice, twice)


def sweep_layer(z, src, w, b, tiles, sub, put):
    for t, at, p, p_up, p_down in row_tiles(lambda s: src[z, s], tiles, sub):
        right, left = roll(p, -1, 1), roll(p, 1, 1)
        total = b(t, at) + (w[0, z, at] * src[z + 1, at] + w[1, z, at] * src[z - 1, at])
        total = total + (w[2, z, at] * p_up + w[3, z, at] * p_down)
        total = total + (w[4, z, at] * right + w[5, z, at] * left)
        put(t, at, total)


def relax_kernel(first, last, moved, p0, w, bx, pads, *refs):
    depth = SWEEPS
    n = w.shape[1] - 2 * depth
    zs = w.shape[1]
    has_state = first > 0
    whole = last == n
    if has_state:
        carried, sums_in, *refs = refs
    charge_out, window_out, sums_out, *refs = refs
    if not whole:
        state_out, *refs = refs
    p1, p2, p3, b = refs
    rows, sector = p0.shape[1:]
    tiles = rows // ROWS
    d = lax.axis_index("drift")
    sub = lax.broadcasted_iota(jnp.int32, (ROWS, sector), 0)
    phis = (p0, p1, p2, p3)

    @pl.loop(0, last - first)
    def _(k):
        value = drift_charge(moved[k], pads[0], pads[1], d)
        charge_out[k] = value
        z = depth + first + k
        b[z, ROWS : rows - ROWS] = value * bx[z, ROWS : rows - ROWS]
        b[z, 0:ROWS] = bx[z, 0:ROWS]
        b[z, rows - ROWS :] = bx[z, rows - ROWS :]

    lows = [z for z in range(1, depth)] if not has_state else []
    if has_state:
        for s in range(1, depth):
            for k in range(2):
                phis[s][depth + first - s - 1 + k] = carried[s - 1, k]
        for k in range(depth - 1):
            b[depth + first - depth + 1 + k] = carried[depth - 1 + k // 2, k % 2]
        sums_out[...] = sums_in[...]
    else:
        sums_out[...] = jnp.zeros_like(sums_out)
    for z in lows:
        b[z] = bx[z]
    if whole:
        for z in range(depth + n, zs - 1):
            b[z] = bx[z]
    top = zs - 1 if whole else depth + last
    for s in range(1, depth + 1):
        start = depth + first - s + 1 if has_state else s
        stop = top - s + 1

        @pl.loop(start, stop)
        def _(z, s=s, start=start):
            def put(t, at, total):
                if s < depth:
                    phis[s][z, at] = total
                else:
                    window_out[z - start, at] = total
                    sums_out[at] += total

            sweep_layer(z, phis[s - 1], w, lambda t, at: b[z, at], tiles, sub, put)

    if not whole:
        for s in range(1, depth):
            for k in range(2):
                state_out[s - 1, k] = phis[s][depth + last - s - 1 + k]
        for k in range(depth - 1):
            state_out[depth - 1 + k // 2, k % 2] = b[depth + last - depth + 1 + k]


def local_kernel(cut, window_a, window_b, charge_a, charge_b, charge, potential, out, run):
    layers, band, sector = potential.shape
    rows = band + 2 * ROWS
    tiles = rows // ROWS
    charge[0:cut] = charge_a[...]
    charge[cut:] = charge_b[...]
    run[...] = jnp.zeros_like(run)
    done = window_a.shape[0]
    for window, base in ((window_a, 0), (window_b, done)):

        @pl.loop(0, window.shape[0])
        def _(k, window=window, base=base):
            for t in range(tiles):
                at = slice(t * ROWS, (t + 1) * ROWS)
                value = window[k, at]
                run[at] += value
                if 0 < t < tiles - 1:
                    potential[base + k, (t - 1) * ROWS : t * ROWS] = value

            def put(at, first, second):
                out[0, base + k, at] = first
                out[1, base + k, at] = second

            ratios_of(run, put)


def ratios_of(field, put):
    rows, sector = field.shape
    band = rows - 2 * ROWS
    r, bands = lax.axis_index("radius"), lax.axis_size("radius")
    total_r = band * bands
    tiles = rows // ROWS
    sub = lax.broadcasted_iota(jnp.int32, (ROWS, sector), 0)
    lane = lax.broadcasted_iota(jnp.int32, (ROWS, sector), 1)
    scale = 1.0 / (8.0 * 1.09)
    for t, at, x, higher, lower in row_tiles(lambda s: field[s], tiles, sub):
        if 0 < t < tiles - 1:
            row = sub + ((t - 1) * ROWS + r * band)
            rpos = ((total_r + row).astype(F32) + 0.5) / total_r
            right = jnp.where(lane == sector - 1, 0.0, roll(x, -1, 1))
            left = jnp.where(lane == 0, 0.0, roll(x, 1, 1))
            er = (lower - higher) * (0.5 * scale)
            ea = (left - right) * (0.5 * scale / rpos)
            put(slice((t - 1) * ROWS, t * ROWS), er + 0.3 * ea, ea - 0.3 * er)


def offset_kernel(local, prefix, out, shift, stage, sems):
    layers = local.shape[1]
    copies = []

    def put(at, first, second):
        shift[0, at] = first
        shift[1, at] = second

    ratios_of(prefix, put)
    parts = sems.shape[0]
    each = layers // parts
    for k in range(parts):
        for c in range(2):
            stage[c, k * each : (k + 1) * each] = local[c, k * each : (k + 1) * each] + shift[c]
        copy = pltpu.make_async_copy(
            stage.at[:, k * each : (k + 1) * each], out.at[:, k * each : (k + 1) * each], sems.at[k]
        )
        copy.start()
        copies.append(copy)
    for copy in copies:
        copy.wait()


def sums_below(sums):
    count, mine = lax.axis_size("drift"), lax.axis_index("drift")
    assert count & (count - 1) == 0
    total, below, step = sums, jnp.zeros_like(sums), 1
    while step < count:
        other = lax.ppermute(total, "drift", [(i, i ^ step) for i in range(count)])
        below = below + jnp.where((mine & step) > 0, other, 0.0)
        total = total + other
        step *= 2
    return below


def body(ions, potential_guess, permittivity, recombination, rate_index, gap_mask, rate_table):
    layers, band, sector = ions.shape
    rows = band + 2 * ROWS
    depth = SWEEPS
    zs = layers + 2 * depth
    split = (5 * layers) // 8
    sides = 1 if lax.axis_size("radius") == 2 else 2

    packed = pl.pallas_call(
        functools.partial(pack_kernel, split),
        out_shape=(
            near(3 * depth - 1, band, sector),
            near(2 * depth, band, sector),
            near(depth - 1, band, sector),
            near(split, band, sector),
            near(layers - split, band, sector),
            *[near(3 * layers + 2, ROWS, sector)] * sides,
            plane(2, band, sector),
        ),
        in_specs=[ANYWHERE] * 3 + [IN_VMEM] * 3 + [pl.BlockSpec(memory_space=pltpu.SMEM)],
        out_specs=[IN_VMEM] * (6 + sides),
        scratch_shapes=[pltpu.SemaphoreType.DMA((8 + 3 * sides,))],
        name="pack",
        compiler_params=pltpu.CompilerParams(vmem_limit_bytes=14 << 20),
    )(potential_guess, permittivity, ions, recombination, rate_index, gap_mask, rate_table)
    up_block, down_block, far_block, first_ions, second_ions, *rest = packed
    side_blocks, pads = rest[:-1], rest[-1]

    below = shifted(up_block, "drift", 1)
    above = shifted(down_block, "drift", -1)
    far = shifted(far_block, "drift", 3)
    raws = radial(side_blocks)
    moveds = [shifted(raw[2 * layers : 3 * layers], "drift", 2) for raw in raws]
    moved_first = shifted(first_ions, "drift", 2)
    moved_second = shifted(second_ions, "drift", 2)
    corners = radial([jnp.concatenate(parts) for parts in zip(edges(below), edges(above), edges(far))])

    p0, w, bx = pl.pallas_call(
        functools.partial(coupling_kernel, sides),
        out_shape=(plane(zs, rows, sector), plane(6, zs, rows, sector), plane(zs, rows, sector)),
        in_specs=[IN_VMEM] * (6 + 3 * sides),
        out_specs=[IN_VMEM] * 3,
        scratch_shapes=[near(zs, rows, sector), near(8, rows, sector)],
        name="couplings",
        compiler_params=pltpu.CompilerParams(vmem_limit_bytes=30 << 20),
    )(potential_guess, permittivity, below, above, far, pads, *raws, *corners, *moveds)
    p0, w, bx, pads = fetched(p0), fetched(w), fetched(bx), fetched(pads)

    own_done = split - depth + 1
    boxes = [near(zs, rows, sector)] * 4
    charge_a, window_a, sums_a, state = pl.pallas_call(
        functools.partial(relax_kernel, 0, split),
        out_shape=(
            plane(split, band, sector),
            plane(own_done, rows, sector),
            plane(rows, sector),
            plane(depth - 1 + depth // 2, 2, rows, sector),
        ),
        in_specs=[IN_VMEM] * 5,
        out_specs=[IN_VMEM] * 4,
        scratch_shapes=boxes,
        name="relax_first",
        compiler_params=pltpu.CompilerParams(vmem_limit_bytes=22 << 20),
    )(moved_first, p0, w, bx, pads)
    charge_b, window_b, sums = pl.pallas_call(
        functools.partial(relax_kernel, split, layers),
        out_shape=(
            near(layers - split, band, sector),
            near(layers - own_done, rows, sector),
            near(rows, sector),
        ),
        in_specs=[IN_VMEM] * 7,
        out_specs=[IN_VMEM] * 3,
        scratch_shapes=boxes,
        name="relax_second",
        compiler_params=pltpu.CompilerParams(vmem_limit_bytes=22 << 20),
    )(moved_second, p0, w, bx, pads, fetched(state), fetched(sums_a))

    charge, potential, local = pl.pallas_call(
        functools.partial(local_kernel, split),
        out_shape=(plane(layers, band, sector), plane(layers, band, sector), plane(2, layers, band, sector)),
        in_specs=[IN_VMEM] * 4,
        out_specs=[IN_VMEM] * 3,
        scratch_shapes=[near(rows, sector)],
        name="local",
        compiler_params=pltpu.CompilerParams(vmem_limit_bytes=22 << 20),
    )(window_a, window_b, charge_a, charge_b)
    below_sums = sums_below(sums)
    distortion = pl.pallas_call(
        offset_kernel,
        out_shape=plane(2, layers, band, sector),
        in_specs=[IN_VMEM] * 2,
        out_specs=ANYWHERE,
        scratch_shapes=[near(2, band, sector), near(2, layers, band, sector), pltpu.SemaphoreType.DMA((4,))],
        name="offset",
        compiler_params=pltpu.CompilerParams(vmem_limit_bytes=20 << 20),
    )(fetched(local), below_sums)
    return charge, potential, distortion


def solution(mesh):
    return jax.shard_map(
        body,
        mesh=mesh,
        in_specs=(
            P("drift", "radius", None),
            P("drift", "radius", None),
            P("drift", "radius", None),
            P("radius", None),
            P("radius", None),
            P("radius", None),
            P(),
        ),
        out_specs=(
            P("drift", "radius", None),
            P("drift", "radius", None),
            P(None, "drift", "radius", None),
        ),
        check_vma=False,
    )
```

```python
import functools

import jax
import jax.numpy as jnp
from jax import lax
from jax.experimental import pallas as pl
from jax.experimental.pallas import tpu as pltpu
from jax.sharding import PartitionSpec as P

SWEEPS = 4
ROWS = 8
F32 = jnp.float32
IN_VMEM = pl.BlockSpec(memory_space=pltpu.VMEM)
ANYWHERE = pl.BlockSpec(memory_space=pl.ANY)


def plane(*shape):
    return jax.ShapeDtypeStruct(shape, F32)


def near(*shape):
    return pltpu.VMEM(shape, F32)


def fetched(x):
    return pltpu.with_memory_space_constraint(x, pltpu.VMEM)


def shifted(block, axis, distance):
    count = lax.axis_size(axis)
    route = [(i, i + distance) for i in range(count) if 0 <= i + distance < count]
    return lax.ppermute(block, axis, route)


def edges(block):
    band = block.shape[-2]
    if lax.axis_size("radius") == 2:
        start = jnp.where(lax.axis_index("radius") == 0, band - ROWS, 0)
        return (lax.dynamic_slice_in_dim(block, start, ROWS, axis=block.ndim - 2),)
    tail = lax.slice_in_dim(block, band - ROWS, band, axis=block.ndim - 2)
    head = lax.slice_in_dim(block, 0, ROWS, axis=block.ndim - 2)
    return (tail, head)


def radial(blocks):
    if len(blocks) == 1:
        return [lax.ppermute(blocks[0], "radius", [(0, 1), (1, 0)])]
    return [shifted(blocks[0], "radius", 1), shifted(blocks[1], "radius", -1)]


def transit(slab, rec, inj):
    return slab / (1.0 + rec * slab) + inj


def drift_charge(ions, rec, inj, slab):
    once = transit(ions, rec, inj)
    return transit(jnp.where(slab >= 1, once, 0.0), rec, inj)


def roll(x, amount, axis):
    return pltpu.roll(x, amount % x.shape[axis], axis)


def row_tiles(load, tiles, sub):
    x = [load(slice(t * ROWS, (t + 1) * ROWS)) for t in range(tiles)]
    up = [roll(v, -1, 0) for v in x]
    down = [roll(v, 1, 0) for v in x]
    for t in range(tiles):
        higher = jnp.where(sub == ROWS - 1, up[(t + 1) % tiles], up[t])
        lower = jnp.where(sub == 0, down[(t - 1) % tiles], down[t])
        yield t, slice(t * ROWS, (t + 1) * ROWS), x[t], higher, lower


def run_all(copies, sems):
    running = [pltpu.make_async_copy(src, dst, sems.at[k]) for k, (src, dst) in enumerate(copies)]
    for copy in running:
        copy.start()
    return running


def send_kernel(phi, eps, ions, up, down, far, *rest):
    sides, sems = rest[:-1], rest[-1]
    layers, band, _ = phi.shape
    depth = SWEEPS
    if len(sides) == 1:
        starts = [pl.multiple_of(jnp.where(lax.axis_index("radius") == 0, band - ROWS, 0), ROWS)]
    else:
        starts = [band - ROWS, 0]
    copies = []
    for start, side in zip(starts, sides):
        for k, src in enumerate((phi, eps, ions)):
            copies.append((src.at[:, pl.ds(start, ROWS)], side.at[k * layers : (k + 1) * layers]))
    copies += [
        (phi.at[layers - depth :], up.at[0:depth]),
        (eps.at[layers - depth :], up.at[depth : 2 * depth]),
        (ions.at[0 : depth - 1], up.at[2 * depth :]),
        (phi.at[0:depth], down.at[0:depth]),
        (eps.at[0:depth], down.at[depth:]),
        (ions.at[layers - depth + 1 :], far),
    ]
    for copy in run_all(copies, sems):
        copy.wait()


def parts_kernel(split, ions, rec, index, gap, table, first, second, pads, sems):
    band, sector = rec.shape
    copies = run_all([(ions.at[0:split], first), (ions.at[split:], second)], sems)
    levels = table.shape[0]
    for t in range(band // ROWS):
        at = slice(t * ROWS, (t + 1) * ROWS)
        which = index[at]
        picked = jnp.zeros((ROWS, sector), F32)
        for k in range(levels):
            picked = jnp.where(which == k, table[k], picked)
        pads[0, at] = rec[at]
        pads[1, at] = picked * (1 - gap[at]).astype(F32)
    for copy in copies:
        copy.wait()


def coupling_kernel(sides, phi, eps, below, above, far, pads, *refs):
    raws, corners, moveds = refs[:sides], refs[sides : 2 * sides], refs[2 * sides : 3 * sides]
    p0, w, bx, ex, geo = refs[3 * sides :]
    layers, band, sector = phi.shape
    depth, n = SWEEPS, layers
    zs = n + 2 * depth
    rows = band + 2 * ROWS
    d, drifts = lax.axis_index("drift"), lax.axis_size("drift")
    r, bands = lax.axis_index("radius"), lax.axis_size("radius")
    total_r = band * bands
    own, top = slice(ROWS, ROWS + band), slice(ROWS + band, rows)
    ends = ((slice(0, ROWS), 0, r > 0), (top, sides - 1, r < bands - 1))
    tiles = rows // ROWS
    sub = lax.broadcasted_iota(jnp.int32, (ROWS, sector), 0)

    def blank(cond, value):
        return jnp.where(cond, value, 0.0)

    for dst, src, base, start in ((p0, phi, 0, 0), (ex, eps, n, depth)):
        dst[0:depth, own] = below[start : start + depth]
        dst[depth : depth + n, own] = src[...]
        dst[depth + n : zs, own] = above[start : start + depth]
        for at, side, has in ends:
            dst[0:depth, at] = blank(has, corners[side][start : start + depth])
            dst[depth : depth + n, at] = blank(has, raws[side][base : base + n])
            up = 3 * depth - 1 + start
            dst[depth + n : zs, at] = blank(has, corners[side][up : up + depth])

    row = lax.broadcasted_iota(jnp.int32, (rows, sector), 0) - ROWS + r * band
    lane = lax.broadcasted_iota(jnp.int32, (rows, sector), 1)
    rpos = ((total_r + row).astype(F32) + 0.5) / total_r
    half = 0.5 / total_r
    geo[0] = (rpos + half) / rpos
    geo[1] = (rpos - half) / rpos
    geo[2] = 1.0 / (rpos * rpos)
    geo[3] = jnp.where((row >= 0) & (row < total_r), 1.0, 0.0)
    geo[4] = jnp.where(lane == sector - 1, 0.0, 1.0)
    geo[5] = jnp.where(lane == 0, 0.0, 1.0)
    for k in range(2):
        geo[6 + k, own] = pads[k]
        for at, side, has in ends:
            geo[6 + k, at] = blank(has, corners[side][6 * depth - 2 + k])

    @pl.loop(0, n)
    def _(z):
        for at, side, has in ends:
            bx[depth + z, at] = drift_charge(blank(has, moveds[side][z]), geo[6, at], geo[7, at], d)

    for k in range(depth - 1):
        for z, ions, slab, spot, corner in (
            (1 + k, far, d - 1, k, 5 * depth - 1 + k),
            (depth + n + k, below, d + 1, 2 * depth + k, 2 * depth + k),
        ):
            bx[z, own] = drift_charge(ions[spot], geo[6, own], geo[7, own], slab)
            for at, side, has in ends:
                bx[z, at] = drift_charge(blank(has, corners[side][corner]), geo[6, at], geo[7, at], slab)

    @pl.loop(1, zs - 1)
    def _(z):
        zg = d * n - depth + z
        alive = jnp.where((zg >= 0) & (zg < drifts * n), 1.0, 0.0)
        outer = (z < depth) | (z >= depth + n)
        for t, at, e, e_up, e_down in row_tiles(lambda s: ex[z, s], tiles, sub):
            not_last, not_first = geo[4, at], geo[5, at]
            right, left = roll(e, -1, 1), roll(e, 1, 1)
            inv_r2 = geo[2, at]
            zu = e + ex[z + 1, at]
            zd = e + ex[z - 1, at]
            ru = (e + e_up) * geo[0, at]
            rd = (e + e_down) * geo[1, at]
            au = (e + right * not_last) * inv_r2
            ad = (e + left * not_first) * inv_r2
            diag = ((zu + zd) + (ru + rd)) + (au + ad)
            inv = jnp.where(geo[3, at] * alive > 0, 1.0 / diag, 0.0)
            for k, value in enumerate((zu, zd, ru, rd)):
                w[k, z, at] = value * inv
            w[4, z, at] = au * inv * not_last
            w[5, z, at] = ad * inv * not_first
            twice = inv + inv
            if t in (0, tiles - 1):
                bx[z, at] = bx[z, at] * twice
            else:
                bx[z, at] = jnp.where(outer, bx[z, at] * twice, twice)


def sweep_layer(z, src, w, b, tiles, sub, put):
    for t, at, p, p_up, p_down in row_tiles(lambda s: src[z, s], tiles, sub):
        right, left = roll(p, -1, 1), roll(p, 1, 1)
        total = b(t, at) + (w[0, z, at] * src[z + 1, at] + w[1, z, at] * src[z - 1, at])
        total = total + (w[2, z, at] * p_up + w[3, z, at] * p_down)
        total = total + (w[4, z, at] * right + w[5, z, at] * left)
        put(t, at, total)


def relax_kernel(first, last, moved, p0, w, bx, pads, *refs):
    depth = SWEEPS
    n = w.shape[1] - 2 * depth
    zs = w.shape[1]
    has_state = first > 0
    whole = last == n
    if has_state:
        carried, sums_in, *refs = refs
    charge_out, window_out, sums_out, *refs = refs
    if not whole:
        state_out, *refs = refs
    p1, p2, p3, b = refs
    rows, sector = p0.shape[1:]
    tiles = rows // ROWS
    d = lax.axis_index("drift")
    sub = lax.broadcasted_iota(jnp.int32, (ROWS, sector), 0)
    phis = (p0, p1, p2, p3)

    @pl.loop(0, last - first)
    def _(k):
        value = drift_charge(moved[k], pads[0], pads[1], d)
        charge_out[k] = value
        z = depth + first + k
        b[z, ROWS : rows - ROWS] = value * bx[z, ROWS : rows - ROWS]
        b[z, 0:ROWS] = bx[z, 0:ROWS]
        b[z, rows - ROWS :] = bx[z, rows - ROWS :]

    lows = [z for z in range(1, depth)] if not has_state else []
    if has_state:
        for s in range(1, depth):
            for k in range(2):
                phis[s][depth + first - s - 1 + k] = carried[s - 1, k]
        for k in range(depth - 1):
            b[depth + first - depth + 1 + k] = carried[depth - 1 + k // 2, k % 2]
        sums_out[...] = sums_in[...]
    else:
        sums_out[...] = jnp.zeros_like(sums_out)
    for z in lows:
        b[z] = bx[z]
    if whole:
        for z in range(depth + n, zs - 1):
            b[z] = bx[z]
    top = zs - 1 if whole else depth + last
    for s in range(1, depth + 1):
        start = depth + first - s + 1 if has_state else s
        stop = top - s + 1

        @pl.loop(start, stop)
        def _(z, s=s, start=start):
            def put(t, at, total):
                if s < depth:
                    phis[s][z, at] = total
                else:
                    window_out[z - start, at] = total
                    sums_out[at] += total

            sweep_layer(z, phis[s - 1], w, lambda t, at: b[z, at], tiles, sub, put)

    if not whole:
        for s in range(1, depth):
            for k in range(2):
                state_out[s - 1, k] = phis[s][depth + last - s - 1 + k]
        for k in range(depth - 1):
            state_out[depth - 1 + k // 2, k % 2] = b[depth + last - depth + 1 + k]


def local_kernel(cut, window_a, window_b, charge_a, charge_b, charge, potential, out, run):
    _, band, _ = potential.shape
    rows = band + 2 * ROWS
    tiles = rows // ROWS
    charge[0:cut] = charge_a[...]
    charge[cut:] = charge_b[...]
    run[...] = jnp.zeros_like(run)
    done = window_a.shape[0]
    for window, base in ((window_a, 0), (window_b, done)):

        @pl.loop(0, window.shape[0])
        def _(k, window=window, base=base):
            for t in range(tiles):
                at = slice(t * ROWS, (t + 1) * ROWS)
                value = window[k, at]
                run[at] += value
                if 0 < t < tiles - 1:
                    potential[base + k, (t - 1) * ROWS : t * ROWS] = value

            def put(at, first, second):
                out[0, base + k, at] = first
                out[1, base + k, at] = second

            ratios_of(run, put)


def ratios_of(field, put):
    rows, sector = field.shape
    band = rows - 2 * ROWS
    r, bands = lax.axis_index("radius"), lax.axis_size("radius")
    total_r = band * bands
    tiles = rows // ROWS
    sub = lax.broadcasted_iota(jnp.int32, (ROWS, sector), 0)
    lane = lax.broadcasted_iota(jnp.int32, (ROWS, sector), 1)
    scale = 1.0 / (8.0 * 1.09)
    for t, at, x, higher, lower in row_tiles(lambda s: field[s], tiles, sub):
        if 0 < t < tiles - 1:
            row = sub + ((t - 1) * ROWS + r * band)
            rpos = ((total_r + row).astype(F32) + 0.5) / total_r
            right = jnp.where(lane == sector - 1, 0.0, roll(x, -1, 1))
            left = jnp.where(lane == 0, 0.0, roll(x, 1, 1))
            er = (lower - higher) * (0.5 * scale)
            ea = (left - right) * (0.5 * scale / rpos)
            put(slice((t - 1) * ROWS, t * ROWS), er + 0.3 * ea, ea - 0.3 * er)


def offset_kernel(local, prefix, out, shift, stage, sems):
    layers = local.shape[1]
    copies = []

    def put(at, first, second):
        shift[0, at] = first
        shift[1, at] = second

    ratios_of(prefix, put)
    parts = sems.shape[0]
    each = layers // parts
    for k in range(parts):
        for c in range(2):
            stage[c, k * each : (k + 1) * each] = local[c, k * each : (k + 1) * each] + shift[c]
        copy = pltpu.make_async_copy(
            stage.at[:, k * each : (k + 1) * each], out.at[:, k * each : (k + 1) * each], sems.at[k]
        )
        copy.start()
        copies.append(copy)
    for copy in copies:
        copy.wait()


def sums_below(sums):
    count, mine = lax.axis_size("drift"), lax.axis_index("drift")
    assert count & (count - 1) == 0
    total, below, step = sums, jnp.zeros_like(sums), 1
    while step < count:
        other = lax.ppermute(total, "drift", [(i, i ^ step) for i in range(count)])
        below = below + jnp.where((mine & step) > 0, other, 0.0)
        total = total + other
        step *= 2
    return below


def body(ions, potential_guess, permittivity, recombination, rate_index, gap_mask, rate_table):
    layers, band, sector = ions.shape
    rows = band + 2 * ROWS
    depth = SWEEPS
    zs = layers + 2 * depth
    split = (3 * layers) // 4
    sides = 1 if lax.axis_size("radius") == 2 else 2

    far_off = [pltpu.with_memory_space_constraint(x, pltpu.HBM) for x in (potential_guess, permittivity, ions)]
    up_block, down_block, far_block, *side_blocks = pl.pallas_call(
        send_kernel,
        out_shape=(
            plane(3 * depth - 1, band, sector),
            plane(2 * depth, band, sector),
            plane(depth - 1, band, sector),
            *[plane(3 * layers, ROWS, sector)] * sides,
        ),
        in_specs=[ANYWHERE] * 3,
        out_specs=[IN_VMEM] * (3 + sides),
        scratch_shapes=[pltpu.SemaphoreType.DMA((6 + 3 * sides,))],
        name="send",
        compiler_params=pltpu.CompilerParams(vmem_limit_bytes=6 << 20),
    )(*far_off)
    raws = radial(side_blocks)
    below = shifted(up_block, "drift", 1)
    above = shifted(down_block, "drift", -1)
    far = shifted(far_block, "drift", 3)
    first_ions, second_ions, pads = pl.pallas_call(
        functools.partial(parts_kernel, split),
        out_shape=(
            plane(split, band, sector),
            plane(layers - split, band, sector),
            plane(2, band, sector),
        ),
        in_specs=[ANYWHERE] + [IN_VMEM] * 3 + [pl.BlockSpec(memory_space=pltpu.SMEM)],
        out_specs=[IN_VMEM] * 3,
        scratch_shapes=[pltpu.SemaphoreType.DMA((2,))],
        name="parts",
        compiler_params=pltpu.CompilerParams(vmem_limit_bytes=4 << 20),
    )(far_off[2], recombination, rate_index, gap_mask, rate_table)
    raws, first_ions = lax.optimization_barrier((raws, first_ions))
    moveds = [shifted(raw[2 * layers :], "drift", 2) for raw in raws]
    moved_first = shifted(first_ions, "drift", 2)
    corners = radial(
        [jnp.concatenate(parts) for parts in zip(edges(below), edges(above), edges(far), edges(pads))]
    )
    corners, second_ions = lax.optimization_barrier((corners, second_ions))
    moved_second = shifted(second_ions, "drift", 2)

    p0, w, bx = pl.pallas_call(
        functools.partial(coupling_kernel, sides),
        out_shape=(plane(zs, rows, sector), plane(6, zs, rows, sector), plane(zs, rows, sector)),
        in_specs=[IN_VMEM] * (6 + 3 * sides),
        out_specs=[IN_VMEM] * 3,
        scratch_shapes=[near(zs, rows, sector), near(8, rows, sector)],
        name="couplings",
        compiler_params=pltpu.CompilerParams(vmem_limit_bytes=30 << 20),
    )(potential_guess, permittivity, below, above, far, pads, *raws, *corners, *moveds)
    p0, w, bx, pads = fetched(p0), fetched(w), fetched(bx), fetched(pads)

    own_done = split - depth + 1
    boxes = [near(zs, rows, sector)] * 4
    charge_a, window_a, sums_a, state = pl.pallas_call(
        functools.partial(relax_kernel, 0, split),
        out_shape=(
            plane(split, band, sector),
            plane(own_done, rows, sector),
            plane(rows, sector),
            plane(depth - 1 + depth // 2, 2, rows, sector),
        ),
        in_specs=[IN_VMEM] * 5,
        out_specs=[IN_VMEM] * 4,
        scratch_shapes=boxes,
        name="relax_first",
        compiler_params=pltpu.CompilerParams(vmem_limit_bytes=22 << 20),
    )(moved_first, p0, w, bx, pads)
    charge_b, window_b, sums = pl.pallas_call(
        functools.partial(relax_kernel, split, layers),
        out_shape=(
            near(layers - split, band, sector),
            near(layers - own_done, rows, sector),
            near(rows, sector),
        ),
        in_specs=[IN_VMEM] * 7,
        out_specs=[IN_VMEM] * 3,
        scratch_shapes=boxes,
        name="relax_second",
        compiler_params=pltpu.CompilerParams(vmem_limit_bytes=22 << 20),
    )(moved_second, p0, w, bx, pads, fetched(state), fetched(sums_a))

    charge, potential, local = pl.pallas_call(
        functools.partial(local_kernel, split),
        out_shape=(plane(layers, band, sector), plane(layers, band, sector), plane(2, layers, band, sector)),
        in_specs=[IN_VMEM] * 4,
        out_specs=[IN_VMEM] * 3,
        scratch_shapes=[near(rows, sector)],
        name="local",
        compiler_params=pltpu.CompilerParams(vmem_limit_bytes=22 << 20),
    )(window_a, window_b, charge_a, charge_b)
    below_sums = sums_below(sums)
    distortion = pl.pallas_call(
        offset_kernel,
        out_shape=plane(2, layers, band, sector),
        in_specs=[IN_VMEM] * 2,
        out_specs=ANYWHERE,
        scratch_shapes=[near(2, band, sector), near(2, layers, band, sector), pltpu.SemaphoreType.DMA((4,))],
        name="offset",
        compiler_params=pltpu.CompilerParams(vmem_limit_bytes=20 << 20),
    )(fetched(local), below_sums)
    return charge, potential, distortion


def solution(mesh):
    return jax.shard_map(
        body,
        mesh=mesh,
        in_specs=(
            P("drift", "radius", None),
            P("drift", "radius", None),
            P("drift", "radius", None),
            P("radius", None),
            P("radius", None),
            P("radius", None),
            P(),
        ),
        out_specs=(
            P("drift", "radius", None),
            P("drift", "radius", None),
            P(None, "drift", "radius", None),
        ),
        check_vma=False,
    )
```

```python
import functools

import jax
import jax.numpy as jnp
from jax import lax
from jax.experimental import pallas as pl
from jax.experimental.pallas import tpu as pltpu
from jax.sharding import PartitionSpec as P

SWEEPS = 4
ROWS = 8
F32 = jnp.float32
IN_VMEM = pl.BlockSpec(memory_space=pltpu.VMEM)
ANYWHERE = pl.BlockSpec(memory_space=pl.ANY)


def plane(*shape):
    return jax.ShapeDtypeStruct(shape, F32)


def near(*shape):
    return pltpu.VMEM(shape, F32)


def fetched(x):
    return pltpu.with_memory_space_constraint(x, pltpu.VMEM)


def shifted(block, axis, distance):
    count = lax.axis_size(axis)
    route = [(i, i + distance) for i in range(count) if 0 <= i + distance < count]
    return lax.ppermute(block, axis, route)


def transit(slab, rec, inj):
    return slab / (1.0 + rec * slab) + inj


def drift_charge(ions, rec, inj, slab):
    once = transit(ions, rec, inj)
    return transit(jnp.where(slab >= 1, once, 0.0), rec, inj)


def roll(x, amount, axis):
    return pltpu.roll(x, amount % x.shape[axis], axis)


def row_tiles(load, tiles, sub):
    x = [load(slice(t * ROWS, (t + 1) * ROWS)) for t in range(tiles)]
    up = [roll(v, -1, 0) for v in x]
    down = [roll(v, 1, 0) for v in x]
    for t in range(tiles):
        higher = jnp.where(sub == ROWS - 1, up[(t + 1) % tiles], up[t])
        lower = jnp.where(sub == 0, down[(t - 1) % tiles], down[t])
        yield t, slice(t * ROWS, (t + 1) * ROWS), x[t], higher, lower


def run_all(copies, sems):
    running = [pltpu.make_async_copy(src, dst, sems.at[k]) for k, (src, dst) in enumerate(copies)]
    for copy in running:
        copy.start()
    return running


def sides_of(count, band):
    if count == 1:
        return [pl.multiple_of(jnp.where(lax.axis_index("radius") == 0, band - ROWS, 0), ROWS)]
    return [band - ROWS, 0]


def rows_kernel(phi, eps, ions, rec, index, gap, table, *rest):
    blocks, pads, sems = rest[:-2], rest[-2], rest[-1]
    layers, band, sector = phi.shape
    starts = sides_of(len(blocks), band)
    copies = []
    for start, block in zip(starts, blocks):
        for k, src in enumerate((phi, eps, ions)):
            copies.append((src.at[:, pl.ds(start, ROWS)], block.at[k * layers : (k + 1) * layers]))
    running = run_all(copies, sems)
    for t in range(band // ROWS):
        at = slice(t * ROWS, (t + 1) * ROWS)
        which = index[at]
        picked = jnp.zeros((ROWS, sector), F32)
        for k in range(table.shape[0]):
            picked = jnp.where(which == k, table[k], picked)
        pads[0, at] = rec[at]
        pads[1, at] = picked * (1 - gap[at]).astype(F32)
    for start, block in zip(starts, blocks):
        for k in range(2):
            block[3 * layers + k] = pads[k, pl.ds(start, ROWS)]
    for copy in running:
        copy.wait()


def halo_kernel(sides, phi, eps, ions, *refs):
    raws, (up, down, far, sems) = refs[:sides], refs[sides:]
    layers, band, _ = phi.shape
    depth = SWEEPS
    copies = []
    for dst, at, k, start, count in (
        (up, 0, 0, layers - depth, depth),
        (up, depth, 1, layers - depth, depth),
        (up, 2 * depth, 2, 0, depth - 1),
        (down, 0, 0, 0, depth),
        (down, depth, 1, 0, depth),
        (far, 0, 2, layers - depth + 1, depth - 1),
    ):
        src = (phi, eps, ions)[k]
        copies.append((src.at[start : start + count], dst.at[at : at + count, 0:band]))
        for side, raw in enumerate(raws):
            rows = slice(band + side * ROWS, band + (side + 1) * ROWS)
            first = k * layers + start
            copies.append((raw.at[first : first + count], dst.at[at : at + count, rows]))
    for copy in run_all(copies, sems):
        copy.wait()


class Window:
    def __init__(self, sides, band):
        r, bands = lax.axis_index("radius"), lax.axis_size("radius")
        self.band, self.rows = band, band + 2 * ROWS
        self.own = slice(ROWS, ROWS + band)
        self.ends = (
            (slice(0, ROWS), 0, r > 0),
            (slice(ROWS + band, self.rows), sides - 1, r < bands - 1),
        )

    def pieces(self, own, outer):
        yield self.own, own()
        for at, side, has in self.ends:
            yield at, jnp.where(has, outer(side), 0.0)

    def of_halo(self, ref, index):
        band = self.band
        return self.pieces(
            lambda: ref[index, 0:band],
            lambda side: ref[index, band + side * ROWS : band + (side + 1) * ROWS],
        )


def coupling_rows(z, ex, z_up, z_down, geo, alive, tiles, sub, put):
    for t, at, e, e_up, e_down in row_tiles(lambda s: ex(z, s), tiles, sub):
        not_last, not_first = geo[4, at], geo[5, at]
        right, left = roll(e, -1, 1), roll(e, 1, 1)
        inv_r2 = geo[2, at]
        zu = e + ex(z_up, at)
        zd = e + ex(z_down, at)
        ru = (e + e_up) * geo[0, at]
        rd = (e + e_down) * geo[1, at]
        au = (e + right * not_last) * inv_r2
        ad = (e + left * not_first) * inv_r2
        diag = ((zu + zd) + (ru + rd)) + (au + ad)
        inv = jnp.where(geo[3, at] * alive > 0, 1.0 / diag, 0.0)
        put(at, (zu * inv, zd * inv, ru * inv, rd * inv, au * inv * not_last, ad * inv * not_first), inv + inv)


def inner_coupling_kernel(sides, phi, eps, pads, *refs):
    raws, (p0, ex, w, inv2, geo) = refs[:sides], refs[sides:]
    layers, band, sector = phi.shape
    win = Window(sides, band)
    rows, tiles = win.rows, win.rows // ROWS
    r, bands = lax.axis_index("radius"), lax.axis_size("radius")
    total_r = band * bands
    sub = lax.broadcasted_iota(jnp.int32, (ROWS, sector), 0)

    row = lax.broadcasted_iota(jnp.int32, (rows, sector), 0) - ROWS + r * band
    lane = lax.broadcasted_iota(jnp.int32, (rows, sector), 1)
    rpos = ((total_r + row).astype(F32) + 0.5) / total_r
    half = 0.5 / total_r
    geo[0] = (rpos + half) / rpos
    geo[1] = (rpos - half) / rpos
    geo[2] = 1.0 / (rpos * rpos)
    geo[3] = jnp.where((row >= 0) & (row < total_r), 1.0, 0.0)
    geo[4] = jnp.where(lane == sector - 1, 0.0, 1.0)
    geo[5] = jnp.where(lane == 0, 0.0, 1.0)
    for k in range(2):
        for at, value in win.pieces(lambda k=k: pads[k], lambda side, k=k: raws[side][3 * layers + k]):
            geo[6 + k, at] = value

    @pl.loop(0, layers)
    def _(z):
        for dst, src, base in ((p0, phi, 0), (ex, eps, layers)):
            for at, value in win.pieces(lambda: src[z], lambda side: raws[side][base + z]):
                dst[z, at] = value

    @pl.loop(1, layers - 1)
    def _(z):
        def put(at, values, twice):
            for k, value in enumerate(values):
                w[k, z, at] = value
            inv2[z, at] = twice

        coupling_rows(z, lambda i, s: ex[i, s], z + 1, z - 1, geo, 1.0, tiles, sub, put)


def sweep_layer(src, src_up, src_down, w, b, tiles, sub, put):
    for t, at, p, p_up, p_down in row_tiles(src, tiles, sub):
        right, left = roll(p, -1, 1), roll(p, 1, 1)
        total = b(at) + (w(0, at) * src_up(at) + w(1, at) * src_down(at))
        total = total + (w(2, at) * p_up + w(3, at) * p_down)
        total = total + (w(4, at) * right + w(5, at) * left)
        put(at, total)


def inner_relax_kernel(sides, moved, p0, w, inv2, geo, *refs):
    rows_moved = refs[:sides]
    charge_out, window_out, sums_out, state, b_out, p1, p2, p3, b = refs[sides:]
    layers, band, sector = moved.shape
    depth = SWEEPS
    win = Window(sides, band)
    tiles = win.rows // ROWS
    d = lax.axis_index("drift")
    sub = lax.broadcasted_iota(jnp.int32, (ROWS, sector), 0)
    phis = (p0, p1, p2, p3)

    @pl.loop(0, layers)
    def _(z):
        inner = (z > 0) & (z < layers - 1)
        for at, ions in win.pieces(lambda: moved[z], lambda side: rows_moved[side][z]):
            value = drift_charge(ions, geo[6, at], geo[7, at], d)
            if at is win.own:
                charge_out[z] = value
            b[z, at] = jnp.where(inner, value * inv2[z, at], value)

    sums_out[...] = jnp.zeros_like(sums_out)
    for s in range(1, depth + 1):
        src = phis[s - 1]

        @pl.loop(s, layers - s)
        def _(z, s=s, src=src):
            def put(at, total):
                if s < depth:
                    phis[s][z, at] = total
                else:
                    window_out[z - depth, at] = total
                    sums_out[at] += total

            sweep_layer(
                lambda at: src[z, at],
                lambda at: src[z + 1, at],
                lambda at: src[z - 1, at],
                lambda k, at: w[k, z, at],
                lambda at: b[z, at],
                tiles,
                sub,
                put,
            )

    for s in range(1, depth):
        for k in range(2):
            state[0, s - 1, k] = phis[s][s + k]
            state[1, s - 1, k] = phis[s][layers - s - 2 + k]
    for k in range(depth):
        b_out[0, k] = b[k]
        b_out[1, k] = b[layers - depth + k]


def outer_relax_kernel(sides, below, above, far, p0, ex, w, geo, state, b_in, sums_in, *refs):
    low_out, high_out, sums_out, ph, eh, wb, bb, q = refs
    layers, rows, sector = p0.shape
    depth, n = SWEEPS, layers
    zs = n + 2 * depth
    band = rows - 2 * ROWS
    win = Window(sides, band)
    tiles = rows // ROWS
    d, drifts = lax.axis_index("drift"), lax.axis_size("drift")
    sub = lax.broadcasted_iota(jnp.int32, (ROWS, sector), 0)

    for k in range(depth):
        for ref, dst in ((below, 0), (above, 1)):
            for at, value in win.of_halo(ref, k):
                ph[dst, k, at] = value
            for at, value in win.of_halo(ref, depth + k):
                eh[dst, k if dst == 0 else 2 + k, at] = value
    for k in range(2):
        eh[0, depth + k] = ex[k]
        eh[1, k] = ex[n - 2 + k]

    for k in range(depth - 1):
        for side, at_layer, ref, index, slab in ((0, k, far, k, d - 1), (1, k + 1, below, 2 * depth + k, d + 1)):
            for at, ions in win.of_halo(ref, index):
                bb[side, at_layer, at] = drift_charge(ions, geo[6, at], geo[7, at], slab)
    bb[0, depth - 1] = b_in[0, 0]
    bb[1, 0] = b_in[1, depth - 1]
    for side in range(2):

        @pl.loop(0, depth)
        def _(k, side=side):
            zg = d * n - depth + (k + 1 if side == 0 else depth + n - 1 + k)
            alive = jnp.where((zg >= 0) & (zg < drifts * n), 1.0, 0.0)

            def put(at, values, twice):
                for j, value in enumerate(values):
                    wb[j, side, k, at] = value
                bb[side, k, at] = bb[side, k, at] * twice

            coupling_rows(k + 1, lambda i, s: eh[side, i, s], k + 2, k, geo, alive, tiles, sub, put)

    def phi_at(s, e):
        if s == 0:
            if e < depth:
                return lambda at: ph[0, e, at]
            if e >= depth + n:
                return lambda at: ph[1, e - depth - n, at]
            return lambda at: p0[e - depth, at]
        z = e - depth
        if s <= z < n - s:
            if z < n // 2:
                return lambda at: state[0, s - 1, z - s, at]
            return lambda at: state[1, s - 1, z - (n - s - 2), at]
        side = 0 if e < zs // 2 else 1
        return lambda at: q[s - 1, side, (e - s) if side == 0 else e - (zs - s - depth), at]

    sums_out[...] = sums_in[...]
    for s in range(1, depth + 1):
        for side in range(2):
            for k in range(depth):
                e = s + k if side == 0 else zs - s - depth + k
                z = e - depth
                if 0 < z < n - 1:
                    w_at = lambda j, at, z=z: w[j, z, at]
                    b_at = lambda at, z=z: b_in[0, z, at] if z < n // 2 else b_in[1, z - (n - depth), at]
                else:
                    at_layer = e - 1 if side == 0 else e - (zs - depth - 1)
                    w_at = lambda j, at, side=side, i=at_layer: wb[j, side, i, at]
                    b_at = lambda at, side=side, i=at_layer: bb[side, i, at]

                def put(at, total, s=s, side=side, k=k):
                    if s < depth:
                        q[s - 1, side, k, at] = total
                    else:
                        (low_out, high_out)[side][k, at] = total
                        sums_out[at] += total

                sweep_layer(phi_at(s - 1, e), phi_at(s - 1, e + 1), phi_at(s - 1, e - 1), w_at, b_at, tiles, sub, put)


def local_kernel(low, inner, high, potential, out, run):
    _, band, _ = potential.shape
    rows = band + 2 * ROWS
    tiles = rows // ROWS
    run[...] = jnp.zeros_like(run)
    base = 0
    for window in (low, inner, high):

        @pl.loop(0, window.shape[0])
        def _(k, window=window, base=base):
            for t in range(tiles):
                at = slice(t * ROWS, (t + 1) * ROWS)
                value = window[k, at]
                run[at] += value
                if 0 < t < tiles - 1:
                    potential[base + k, (t - 1) * ROWS : t * ROWS] = value

            def put(at, first, second):
                out[0, base + k, at] = first
                out[1, base + k, at] = second

            ratios_of(run, put)

        base += window.shape[0]


def ratios_of(field, put):
    rows, sector = field.shape
    band = rows - 2 * ROWS
    r, bands = lax.axis_index("radius"), lax.axis_size("radius")
    total_r = band * bands
    tiles = rows // ROWS
    sub = lax.broadcasted_iota(jnp.int32, (ROWS, sector), 0)
    lane = lax.broadcasted_iota(jnp.int32, (ROWS, sector), 1)
    scale = 1.0 / (8.0 * 1.09)
    for t, at, x, higher, lower in row_tiles(lambda s: field[s], tiles, sub):
        if 0 < t < tiles - 1:
            row = sub + ((t - 1) * ROWS + r * band)
            rpos = ((total_r + row).astype(F32) + 0.5) / total_r
            right = jnp.where(lane == sector - 1, 0.0, roll(x, -1, 1))
            left = jnp.where(lane == 0, 0.0, roll(x, 1, 1))
            er = (lower - higher) * (0.5 * scale)
            ea = (left - right) * (0.5 * scale / rpos)
            put(slice((t - 1) * ROWS, t * ROWS), er + 0.3 * ea, ea - 0.3 * er)


def offset_kernel(local, prefix, out, shift, stage, sems):
    layers = local.shape[1]
    copies = []

    def put(at, first, second):
        shift[0, at] = first
        shift[1, at] = second

    ratios_of(prefix, put)
    parts = sems.shape[0]
    each = layers // parts
    for k in range(parts):
        for c in range(2):
            stage[c, k * each : (k + 1) * each] = local[c, k * each : (k + 1) * each] + shift[c]
        copy = pltpu.make_async_copy(
            stage.at[:, k * each : (k + 1) * each], out.at[:, k * each : (k + 1) * each], sems.at[k]
        )
        copy.start()
        copies.append(copy)
    for copy in copies:
        copy.wait()


def sums_below(sums):
    count, mine = lax.axis_size("drift"), lax.axis_index("drift")
    assert count & (count - 1) == 0
    total, below, step = sums, jnp.zeros_like(sums), 1
    while step < count:
        other = lax.ppermute(total, "drift", [(i, i ^ step) for i in range(count)])
        below = below + jnp.where((mine & step) > 0, other, 0.0)
        total = total + other
        step *= 2
    return below


def kernel(function, out_shape, in_specs, out_specs=None, scratch=(), mb=16):
    return pl.pallas_call(
        function,
        out_shape=out_shape,
        in_specs=in_specs,
        out_specs=out_specs if out_specs is not None else [IN_VMEM] * len(out_shape),
        scratch_shapes=list(scratch),
        compiler_params=pltpu.CompilerParams(vmem_limit_bytes=mb << 20),
    )


def body(ions, potential_guess, permittivity, recombination, rate_index, gap_mask, rate_table):
    layers, band, sector = ions.shape
    rows = band + 2 * ROWS
    depth = SWEEPS
    sides = 1 if lax.axis_size("radius") == 2 else 2
    sent = band + sides * ROWS
    dma = pltpu.SemaphoreType.DMA
    phi, eps, ions_far = [
        pltpu.with_memory_space_constraint(x, pltpu.HBM) for x in (potential_guess, permittivity, ions)
    ]

    moved = shifted(ions, "drift", 2)
    *blocks, pads = kernel(
        rows_kernel,
        [plane(3 * layers + 2, ROWS, sector)] * sides + [plane(2, band, sector)],
        [ANYWHERE] * 3 + [IN_VMEM] * 3 + [pl.BlockSpec(memory_space=pltpu.SMEM)],
        scratch=[dma((3 * sides,))],
        mb=4,
    )(phi, eps, ions_far, recombination, rate_index, gap_mask, rate_table)
    if sides == 1:
        raws = [lax.ppermute(blocks[0], "radius", [(0, 1), (1, 0)])]
    else:
        raws = [shifted(blocks[0], "radius", 1), shifted(blocks[1], "radius", -1)]
    up, down, beyond = kernel(
        functools.partial(halo_kernel, sides),
        [plane(3 * depth - 1, sent, sector), plane(2 * depth, sent, sector), plane(depth - 1, sent, sector)],
        [ANYWHERE] * 3 + [IN_VMEM] * sides,
        scratch=[dma((6 * (1 + sides),))],
        mb=6,
    )(phi, eps, ions_far, *raws)
    rows_moved = [shifted(raw[2 * layers : 3 * layers], "drift", 2) for raw in raws]
    below = shifted(up, "drift", 1)
    above = shifted(down, "drift", -1)
    far = shifted(beyond, "drift", 3)

    box = plane(layers, rows, sector)
    p0, ex, w, inv2, geo = kernel(
        functools.partial(inner_coupling_kernel, sides),
        [box, box, plane(6, layers, rows, sector), box, plane(8, rows, sector)],
        [IN_VMEM] * (3 + sides),
        mb=20,
    )(potential_guess, permittivity, pads, *raws)
    p0, ex, w, inv2, geo = [fetched(x) for x in (p0, ex, w, inv2, geo)]
    charge, inner, sums, state, b = kernel(
        functools.partial(inner_relax_kernel, sides),
        [
            plane(layers, band, sector),
            plane(layers - 2 * depth, rows, sector),
            plane(rows, sector),
            plane(2, depth - 1, 2, rows, sector),
            plane(2, depth, rows, sector),
        ],
        [IN_VMEM] * (5 + sides),
        scratch=[near(layers, rows, sector)] * 4,
        mb=16,
    )(moved, p0, w, inv2, geo, *rows_moved)
    low, high, sums = kernel(
        functools.partial(outer_relax_kernel, sides),
        [plane(depth, rows, sector), plane(depth, rows, sector), plane(rows, sector)],
        [IN_VMEM] * 10,
        scratch=[
            near(2, depth, rows, sector),
            near(2, depth + 2, rows, sector),
            near(6, 2, depth, rows, sector),
            near(2, depth, rows, sector),
            near(depth - 1, 2, depth, rows, sector),
        ],
        mb=16,
    )(below, above, far, p0, ex, w, geo, fetched(state), fetched(b), fetched(sums))
    potential, local = kernel(
        local_kernel,
        [plane(layers, band, sector), plane(2, layers, band, sector)],
        [IN_VMEM] * 3,
        scratch=[near(rows, sector)],
        mb=16,
    )(low, inner, high)
    below_sums = sums_below(sums)
    distortion = kernel(
        offset_kernel,
        plane(2, layers, band, sector),
        [IN_VMEM] * 2,
        ANYWHERE,
        [near(2, band, sector), near(2, layers, band, sector), dma((4,))],
        mb=12,
    )(fetched(local), below_sums)
    return charge, potential, distortion


def solution(mesh):
    return jax.shard_map(
        body,
        mesh=mesh,
        in_specs=(
            P("drift", "radius", None),
            P("drift", "radius", None),
            P("drift", "radius", None),
            P("radius", None),
            P("radius", None),
            P("radius", None),
            P(),
        ),
        out_specs=(
            P("drift", "radius", None),
            P("drift", "radius", None),
            P(None, "drift", "radius", None),
        ),
        check_vma=False,
    )
```

```python
import functools

import jax
import jax.numpy as jnp
from jax import lax
from jax.experimental import pallas as pl
from jax.experimental.pallas import tpu as pltpu
from jax.sharding import PartitionSpec as P

SWEEPS = 4
ROWS = 8
F32 = jnp.float32
IN_VMEM = pl.BlockSpec(memory_space=pltpu.VMEM)
ANYWHERE = pl.BlockSpec(memory_space=pl.ANY)


def plane(*shape):
    return jax.ShapeDtypeStruct(shape, F32)


def near(*shape):
    return pltpu.VMEM(shape, F32)


def fetched(x):
    return pltpu.with_memory_space_constraint(x, pltpu.VMEM)


def shifted(block, axis, distance):
    count = lax.axis_size(axis)
    route = [(i, i + distance) for i in range(count) if 0 <= i + distance < count]
    return lax.ppermute(block, axis, route)


def transit(slab, rec, inj):
    return slab / (1.0 + rec * slab) + inj


def drift_charge(ions, rec, inj, slab):
    once = transit(ions, rec, inj)
    return transit(jnp.where(slab >= 1, once, 0.0), rec, inj)


def roll(x, amount, axis):
    return pltpu.roll(x, amount % x.shape[axis], axis)


def row_tiles(load, tiles, sub):
    x = [load(slice(t * ROWS, (t + 1) * ROWS)) for t in range(tiles)]
    up = [roll(v, -1, 0) for v in x]
    down = [roll(v, 1, 0) for v in x]
    for t in range(tiles):
        higher = jnp.where(sub == ROWS - 1, up[(t + 1) % tiles], up[t])
        lower = jnp.where(sub == 0, down[(t - 1) % tiles], down[t])
        yield t, slice(t * ROWS, (t + 1) * ROWS), x[t], higher, lower


def run_all(copies, sems):
    running = [pltpu.make_async_copy(src, dst, sems.at[k]) for k, (src, dst) in enumerate(copies)]
    for copy in running:
        copy.start()
    return running


def sides_of(count, band):
    if count == 1:
        return [pl.multiple_of(jnp.where(lax.axis_index("radius") == 0, band - ROWS, 0), ROWS)]
    return [band - ROWS, 0]


def rows_kernel(phi, eps, ions, rec, index, gap, table, *rest):
    sides = (len(rest) - 7) // 2
    blocks, pads, stages = rest[:sides], rest[sides], rest[sides + 1 : 2 * sides + 1]
    rec_v, index_v, gap_v, table_s, sems, pad_sems = rest[2 * sides + 1 :]
    layers, band, sector = phi.shape
    ends = SWEEPS - 1
    starts = sides_of(sides, band)
    copies = []
    for start, block, stage in zip(starts, blocks, stages):
        rows = pl.ds(start, ROWS)
        copies.append((phi.at[:, rows], block.at[0:layers]))
        copies.append((eps.at[:, rows], block.at[layers : 2 * layers]))
        copies.append((ions.at[:, rows], stage))
    running = run_all(copies, sems)
    pad_copies = run_all([(rec, rec_v), (index, index_v), (gap, gap_v), (table, table_s)], pad_sems)
    for copy in pad_copies:
        copy.wait()
    for t in range(band // ROWS):
        at = slice(t * ROWS, (t + 1) * ROWS)
        which = index_v[at]
        picked = jnp.zeros((ROWS, sector), F32)
        for k in range(table_s.shape[0]):
            picked = jnp.where(which == k, table_s[k], picked)
        pads[0, at] = rec_v[at]
        pads[1, at] = picked * (1 - gap_v[at]).astype(F32)
    for copy in running:
        copy.wait()
    sub = lax.broadcasted_iota(jnp.int32, (ROWS, sector), 0)
    first_half = sub < ROWS // 2
    for side, (start, block, stage) in enumerate(zip(starts, blocks, stages)):
        tail = (lax.axis_index("radius") == 0) if sides == 1 else side == 0
        base = 2 * layers
        for j in range(layers // 2):
            one, two = stage[2 * j], stage[2 * j + 1]
            from_tail = jnp.where(first_half, roll(one, ROWS // 2, 0), two)
            from_head = jnp.where(first_half, one, roll(two, ROWS // 2, 0))
            block[base + j] = jnp.where(tail, from_tail, from_head)
        base += layers // 2
        for k in range(ends):
            block[base + k] = stage[k]
            block[base + ends + k] = stage[layers - ends + k]
        base += 2 * ends
        for k in range(2):
            block[base + k] = pads[k, pl.ds(start, ROWS)]


def halo_kernel(sides, phi, eps, ions, *refs):
    raws, (inner, outer, far, sems) = refs[:sides], refs[sides:]
    layers, band, _ = phi.shape
    depth = SWEEPS
    odd = lax.rem(lax.axis_index("drift"), 2) == 1
    low, high = 0, layers - depth
    near_at, far_at = jnp.where(odd, low, high), jnp.where(odd, high, low)
    ends = 2 * layers + layers // 2
    copies = []
    for dst, at, k, start, raw_at, count in (
        (inner, 0, 0, near_at, near_at, depth),
        (inner, depth, 1, near_at, layers + near_at, depth),
        (inner, 2 * depth, 2, 0, ends, depth - 1),
        (outer, 0, 0, far_at, far_at, depth),
        (outer, depth, 1, far_at, layers + far_at, depth),
        (far, 0, 2, layers - depth + 1, ends + depth - 1, depth - 1),
    ):
        src = (phi, eps, ions)[k]
        copies.append((src.at[pl.ds(start, count)], dst.at[at : at + count, 0:band]))
        for side, raw in enumerate(raws):
            rows = slice(band + side * ROWS, band + (side + 1) * ROWS)
            copies.append((raw.at[pl.ds(raw_at, count)], dst.at[at : at + count, rows]))
    for copy in run_all(copies, sems):
        copy.wait()


class Window:
    def __init__(self, sides, band):
        r, bands = lax.axis_index("radius"), lax.axis_size("radius")
        self.band, self.rows = band, band + 2 * ROWS
        self.own = slice(ROWS, ROWS + band)
        self.ends = (
            (slice(0, ROWS), 0, r > 0),
            (slice(ROWS + band, self.rows), sides - 1, r < bands - 1),
        )

    def pieces(self, own, outer):
        yield self.own, own()
        for at, side, has in self.ends:
            yield at, jnp.where(has, outer(side), 0.0)

    def of_halo(self, ref, index):
        band = self.band
        return self.pieces(
            lambda: ref[index, 0:band],
            lambda side: ref[index, band + side * ROWS : band + (side + 1) * ROWS],
        )


def coupling_rows(z, ex, z_up, z_down, geo, alive, tiles, sub, put):
    for t, at, e, e_up, e_down in row_tiles(lambda s: ex(z, s), tiles, sub):
        not_last, not_first = geo[4, at], geo[5, at]
        right, left = roll(e, -1, 1), roll(e, 1, 1)
        inv_r2 = geo[2, at]
        zu = e + ex(z_up, at)
        zd = e + ex(z_down, at)
        ru = (e + e_up) * geo[0, at]
        rd = (e + e_down) * geo[1, at]
        au = (e + right * not_last) * inv_r2
        ad = (e + left * not_first) * inv_r2
        diag = ((zu + zd) + (ru + rd)) + (au + ad)
        inv = jnp.where(geo[3, at] * alive > 0, 1.0 / diag, 0.0)
        put(at, (zu * inv, zd * inv, ru * inv, rd * inv, au * inv * not_last, ad * inv * not_first), inv + inv)


def inner_coupling_kernel(sides, phi, eps, pads, *refs):
    raws, (p0, ex, w, inv2, geo) = refs[:sides], refs[sides:]
    layers, band, sector = phi.shape
    win = Window(sides, band)
    rows, tiles = win.rows, win.rows // ROWS
    r, bands = lax.axis_index("radius"), lax.axis_size("radius")
    total_r = band * bands
    sub = lax.broadcasted_iota(jnp.int32, (ROWS, sector), 0)

    row = lax.broadcasted_iota(jnp.int32, (rows, sector), 0) - ROWS + r * band
    lane = lax.broadcasted_iota(jnp.int32, (rows, sector), 1)
    rpos = ((total_r + row).astype(F32) + 0.5) / total_r
    half = 0.5 / total_r
    geo[0] = (rpos + half) / rpos
    geo[1] = (rpos - half) / rpos
    geo[2] = 1.0 / (rpos * rpos)
    geo[3] = jnp.where((row >= 0) & (row < total_r), 1.0, 0.0)
    geo[4] = jnp.where(lane == sector - 1, 0.0, 1.0)
    geo[5] = jnp.where(lane == 0, 0.0, 1.0)
    for k in range(2):
        for at, value in win.pieces(lambda k=k: pads[k], lambda side, k=k: raws[side][2 * layers + layers // 2 + 2 * (SWEEPS - 1) + k]):
            geo[6 + k, at] = value

    @pl.loop(0, layers)
    def _(z):
        for dst, src, base in ((p0, phi, 0), (ex, eps, layers)):
            for at, value in win.pieces(lambda: src[z], lambda side: raws[side][base + z]):
                dst[z, at] = value

    @pl.loop(1, layers - 1)
    def _(z):
        def put(at, values, twice):
            for k, value in enumerate(values):
                w[k, z, at] = value
            inv2[z, at] = twice

        coupling_rows(z, lambda i, s: ex[i, s], z + 1, z - 1, geo, 1.0, tiles, sub, put)


def sweep_layer(src, src_up, src_down, w, b, tiles, sub, put):
    for t, at, p, p_up, p_down in row_tiles(src, tiles, sub):
        right, left = roll(p, -1, 1), roll(p, 1, 1)
        total = b(at) + (w(0, at) * src_up(at) + w(1, at) * src_down(at))
        total = total + (w(2, at) * p_up + w(3, at) * p_down)
        total = total + (w(4, at) * right + w(5, at) * left)
        put(at, total)


def inner_relax_kernel(sides, moved, p0, w, inv2, geo, *refs):
    rows_moved = refs[:sides]
    charge_out, swap, window_out, sums_out, state, b_out, p1, p2, p3, b, raw = refs[sides:]
    layers, band, sector = moved.shape
    depth = SWEEPS
    win = Window(sides, band)
    tiles = win.rows // ROWS
    d = lax.axis_index("drift")
    sub = lax.broadcasted_iota(jnp.int32, (ROWS, sector), 0)
    phis = (p0, p1, p2, p3)

    @pl.loop(0, layers // 2)
    def _(j):
        for half in range(2):
            z = 2 * j + half
            inner = (z > 0) & (z < layers - 1)
            for at, side, has in ((win.own, None, None), *win.ends):
                if side is None:
                    ions = moved[z]
                else:
                    ions = rows_moved[side][j]
                    if half == (0 if at is win.ends[0][0] else 1):
                        ions = roll(ions, ROWS // 2, 0)
                    ions = jnp.where(has, ions, 0.0)
                value = drift_charge(ions, geo[6, at], geo[7, at], d)
                if side is None:
                    charge_out[z] = value
                raw[z, at] = value
                b[z, at] = jnp.where(inner, value * inv2[z, at], value)

    odd = lax.rem(d, 2) == 1
    for k in range(depth - 1):
        swap[k] = raw[jnp.where(odd, k, layers - depth + 1 + k)]
    sums_out[...] = jnp.zeros_like(sums_out)
    for s in range(1, depth + 1):
        src = phis[s - 1]

        @pl.loop(s, layers - s, step=2)
        def _(first, s=s, src=src):
            for z in (first, first + 1):

                def put(at, total, z=z):
                    if s < depth:
                        phis[s][z, at] = total
                    else:
                        window_out[z - depth, at] = total
                        sums_out[at] += total

                sweep_layer(
                    lambda at, z=z: src[z, at],
                    lambda at, z=z: src[z + 1, at],
                    lambda at, z=z: src[z - 1, at],
                    lambda k, at, z=z: w[k, z, at],
                    lambda at, z=z: b[z, at],
                    tiles,
                    sub,
                    put,
                )

    for s in range(1, depth):
        for k in range(2):
            state[0, s - 1, k] = phis[s][s + k]
            state[1, s - 1, k] = phis[s][layers - s - 2 + k]
    for k in range(depth):
        b_out[0, k] = b[k]
        b_out[1, k] = b[layers - depth + k]


def outer_relax_kernel(sides, inner, outer, far, swapped, p0, ex, w, geo, state, b_in, sums_in, *refs):
    low_out, high_out, sums_out, ph, eh, wb, bb, q = refs
    layers, rows, sector = p0.shape
    depth, n = SWEEPS, layers
    zs = n + 2 * depth
    band = rows - 2 * ROWS
    win = Window(sides, band)
    tiles = rows // ROWS
    d, drifts = lax.axis_index("drift"), lax.axis_size("drift")
    sub = lax.broadcasted_iota(jnp.int32, (ROWS, sector), 0)

    odd = lax.rem(d, 2) == 1
    for k in range(depth):
        for ref, half, to in ((ph, 0, (k, k)), (eh, depth, (k, 2 + k))):
            for (at, one), (_, two) in zip(win.of_halo(inner, half + k), win.of_halo(outer, half + k)):
                ref[0, to[0], at] = jnp.where(odd, one, two)
                ref[1, to[1], at] = jnp.where(odd, two, one)
    for k in range(2):
        eh[0, depth + k] = ex[k]
        eh[1, k] = ex[n - 2 + k]

    for k in range(depth - 1):
        for (at, near_ions), (_, far_ions) in zip(win.of_halo(inner, 2 * depth + k), win.of_halo(far, k)):
            rec, inj = geo[6, at], geo[7, at]
            ready = swapped[k, at]
            bb[0, k, at] = jnp.where(odd, ready, drift_charge(far_ions, rec, inj, d - 1))
            bb[1, k + 1, at] = jnp.where(odd, drift_charge(near_ions, rec, inj, d + 1), ready)
    bb[0, depth - 1] = b_in[0, 0]
    bb[1, 0] = b_in[1, depth - 1]
    for side in range(2):

        @pl.loop(0, depth)
        def _(k, side=side):
            zg = d * n - depth + (k + 1 if side == 0 else depth + n - 1 + k)
            alive = jnp.where((zg >= 0) & (zg < drifts * n), 1.0, 0.0)

            def put(at, values, twice):
                for j, value in enumerate(values):
                    wb[j, side, k, at] = value
                bb[side, k, at] = bb[side, k, at] * twice

            coupling_rows(k + 1, lambda i, s: eh[side, i, s], k + 2, k, geo, alive, tiles, sub, put)

    def phi_at(s, e):
        if s == 0:
            if e < depth:
                return lambda at: ph[0, e, at]
            if e >= depth + n:
                return lambda at: ph[1, e - depth - n, at]
            return lambda at: p0[e - depth, at]
        z = e - depth
        if s <= z < n - s:
            if z < n // 2:
                return lambda at: state[0, s - 1, z - s, at]
            return lambda at: state[1, s - 1, z - (n - s - 2), at]
        side = 0 if e < zs // 2 else 1
        return lambda at: q[s - 1, side, (e - s) if side == 0 else e - (zs - s - depth), at]

    sums_out[...] = sums_in[...]
    for s in range(1, depth + 1):
        for side in range(2):
            for k in range(depth):
                e = s + k if side == 0 else zs - s - depth + k
                z = e - depth
                if 0 < z < n - 1:
                    w_at = lambda j, at, z=z: w[j, z, at]
                    b_at = lambda at, z=z: b_in[0, z, at] if z < n // 2 else b_in[1, z - (n - depth), at]
                else:
                    at_layer = e - 1 if side == 0 else e - (zs - depth - 1)
                    w_at = lambda j, at, side=side, i=at_layer: wb[j, side, i, at]
                    b_at = lambda at, side=side, i=at_layer: bb[side, i, at]

                def put(at, total, s=s, side=side, k=k):
                    if s < depth:
                        q[s - 1, side, k, at] = total
                    else:
                        (low_out, high_out)[side][k, at] = total
                        sums_out[at] += total

                sweep_layer(phi_at(s - 1, e), phi_at(s - 1, e + 1), phi_at(s - 1, e - 1), w_at, b_at, tiles, sub, put)


def local_kernel(low, inner, high, potential, out, run):
    _, band, _ = potential.shape
    rows = band + 2 * ROWS
    tiles = rows // ROWS
    run[...] = jnp.zeros_like(run)
    base = 0
    for window in (low, inner, high):

        @pl.loop(0, window.shape[0])
        def _(k, window=window, base=base):
            for t in range(tiles):
                at = slice(t * ROWS, (t + 1) * ROWS)
                value = window[k, at]
                run[at] += value
                if 0 < t < tiles - 1:
                    potential[base + k, (t - 1) * ROWS : t * ROWS] = value

            def put(at, first, second):
                out[0, base + k, at] = first
                out[1, base + k, at] = second

            ratios_of(run, put)

        base += window.shape[0]


def ratios_of(field, put):
    rows, sector = field.shape
    band = rows - 2 * ROWS
    r, bands = lax.axis_index("radius"), lax.axis_size("radius")
    total_r = band * bands
    tiles = rows // ROWS
    sub = lax.broadcasted_iota(jnp.int32, (ROWS, sector), 0)
    lane = lax.broadcasted_iota(jnp.int32, (ROWS, sector), 1)
    scale = 1.0 / (8.0 * 1.09)
    for t, at, x, higher, lower in row_tiles(lambda s: field[s], tiles, sub):
        if 0 < t < tiles - 1:
            row = sub + ((t - 1) * ROWS + r * band)
            rpos = ((total_r + row).astype(F32) + 0.5) / total_r
            right = jnp.where(lane == sector - 1, 0.0, roll(x, -1, 1))
            left = jnp.where(lane == 0, 0.0, roll(x, 1, 1))
            er = (lower - higher) * (0.5 * scale)
            ea = (left - right) * (0.5 * scale / rpos)
            put(slice((t - 1) * ROWS, t * ROWS), er + 0.3 * ea, ea - 0.3 * er)


def offset_kernel(local, prefix, out, shift, stage, sems):
    layers = local.shape[1]
    copies = []

    def put(at, first, second):
        shift[0, at] = first
        shift[1, at] = second

    ratios_of(prefix, put)
    parts = sems.shape[0]
    each = layers // parts
    for k in range(parts):
        for c in range(2):
            stage[c, k * each : (k + 1) * each] = local[c, k * each : (k + 1) * each] + shift[c]
        copy = pltpu.make_async_copy(
            stage.at[:, k * each : (k + 1) * each], out.at[:, k * each : (k + 1) * each], sems.at[k]
        )
        copy.start()
        copies.append(copy)
    for copy in copies:
        copy.wait()


def sums_below(sums):
    count, mine = lax.axis_size("drift"), lax.axis_index("drift")
    assert count & (count - 1) == 0
    total, below, step = sums, jnp.zeros_like(sums), 1
    while step < count:
        other = lax.ppermute(total, "drift", [(i, i ^ step) for i in range(count)])
        below = below + jnp.where((mine & step) > 0, other, 0.0)
        total = total + other
        step *= 2
    return below


def kernel(function, out_shape, in_specs, out_specs=None, scratch=(), mb=16):
    return pl.pallas_call(
        function,
        out_shape=out_shape,
        in_specs=in_specs,
        out_specs=out_specs if out_specs is not None else [IN_VMEM] * len(out_shape),
        scratch_shapes=list(scratch),
        compiler_params=pltpu.CompilerParams(vmem_limit_bytes=mb << 20),
    )


def body(ions, potential_guess, permittivity, recombination, rate_index, gap_mask, rate_table):
    layers, band, sector = ions.shape
    rows = band + 2 * ROWS
    depth = SWEEPS
    sides = 1 if lax.axis_size("radius") == 2 else 2
    sent = band + sides * ROWS
    dma = pltpu.SemaphoreType.DMA
    ends = depth - 1
    row_block = 2 * layers + layers // 2 + 2 * ends + 2
    far_args = (potential_guess, permittivity, ions, recombination, rate_index, gap_mask, rate_table)
    phi, eps, ions_far, *pad_args = [pltpu.with_memory_space_constraint(x, pltpu.HBM) for x in far_args]

    moved = shifted(ions, "drift", 2)
    *blocks, pads = kernel(
        rows_kernel,
        [plane(row_block, ROWS, sector)] * sides + [plane(2, band, sector)],
        [ANYWHERE] * 7,
        scratch=[near(layers, ROWS, sector)] * sides
        + [
            near(band, sector),
            pltpu.VMEM((band, sector), jnp.int32),
            pltpu.VMEM((band, sector), jnp.int32),
            pltpu.SMEM(rate_table.shape, F32),
            dma((3 * sides,)),
            dma((4,)),
        ],
        mb=5,
    )(phi, eps, ions_far, *pad_args)
    if sides == 1:
        raws = [lax.ppermute(blocks[0], "radius", [(0, 1), (1, 0)])]
    else:
        raws = [shifted(blocks[0], "radius", 1), shifted(blocks[1], "radius", -1)]
    to_core, to_chip, beyond = kernel(
        functools.partial(halo_kernel, sides),
        [plane(3 * depth - 1, sent, sector), plane(2 * depth, sent, sector), plane(depth - 1, sent, sector)],
        [ANYWHERE] * 3 + [IN_VMEM] * sides,
        scratch=[dma((6 * (1 + sides),))],
        mb=6,
    )(phi, eps, ions_far, *raws)
    count = lax.axis_size("drift")
    assert count % 2 == 0
    partners = [(i, i ^ 1) for i in range(count)]
    chips = [(i, i + 1 if i % 2 else i - 1) for i in range(1, count - 1)]
    rows_moved = [shifted(raw[2 * layers : 2 * layers + layers // 2], "drift", 2) for raw in raws]
    outer = lax.ppermute(to_chip, "drift", chips)
    far = lax.ppermute(beyond, "drift", [(i - 3, i) for i in range(4, count, 2)])
    inner = lax.ppermute(to_core, "drift", partners)

    box = plane(layers, rows, sector)
    p0, ex, w, inv2, geo = kernel(
        functools.partial(inner_coupling_kernel, sides),
        [box, box, plane(6, layers, rows, sector), box, plane(8, rows, sector)],
        [IN_VMEM] * (3 + sides),
        mb=20,
    )(potential_guess, permittivity, pads, *raws)
    p0, ex, w, inv2, geo = [fetched(x) for x in (p0, ex, w, inv2, geo)]
    charge, swap, middle, sums, state, b = kernel(
        functools.partial(inner_relax_kernel, sides),
        [
            plane(layers, band, sector),
            plane(depth - 1, rows, sector),
            plane(layers - 2 * depth, rows, sector),
            plane(rows, sector),
            plane(2, depth - 1, 2, rows, sector),
            plane(2, depth, rows, sector),
        ],
        [IN_VMEM] * (5 + sides),
        scratch=[near(layers, rows, sector)] * 5,
        mb=16,
    )(moved, p0, w, inv2, geo, *rows_moved)
    swapped = lax.ppermute(swap, "drift", partners)
    low, high, sums = kernel(
        functools.partial(outer_relax_kernel, sides),
        [plane(depth, rows, sector), plane(depth, rows, sector), plane(rows, sector)],
        [IN_VMEM] * 11,
        scratch=[
            near(2, depth, rows, sector),
            near(2, depth + 2, rows, sector),
            near(6, 2, depth, rows, sector),
            near(2, depth, rows, sector),
            near(depth - 1, 2, depth, rows, sector),
        ],
        mb=16,
    )(inner, outer, far, swapped, p0, ex, w, geo, fetched(state), fetched(b), fetched(sums))
    potential, local = kernel(
        local_kernel,
        [plane(layers, band, sector), plane(2, layers, band, sector)],
        [IN_VMEM] * 3,
        scratch=[near(rows, sector)],
        mb=16,
    )(low, middle, high)
    below_sums = sums_below(sums)
    distortion = kernel(
        offset_kernel,
        plane(2, layers, band, sector),
        [IN_VMEM] * 2,
        ANYWHERE,
        [near(2, band, sector), near(2, layers, band, sector), dma((4,))],
        mb=12,
    )(fetched(local), below_sums)
    return charge, potential, distortion


def solution(mesh):
    return jax.shard_map(
        body,
        mesh=mesh,
        in_specs=(
            P("drift", "radius", None),
            P("drift", "radius", None),
            P("drift", "radius", None),
            P("radius", None),
            P("radius", None),
            P("radius", None),
            P(),
        ),
        out_specs=(
            P("drift", "radius", None),
            P("drift", "radius", None),
            P(None, "drift", "radius", None),
        ),
        check_vma=False,
    )
```

```python
import functools

import jax
import jax.numpy as jnp
from jax import lax
from jax.experimental import pallas as pl
from jax.experimental.pallas import tpu as pltpu
from jax.sharding import PartitionSpec as P

SWEEPS = 4
ROWS = 8
F32 = jnp.float32
IN_VMEM = pl.BlockSpec(memory_space=pltpu.VMEM)
ANYWHERE = pl.BlockSpec(memory_space=pl.ANY)


def plane(*shape):
    return jax.ShapeDtypeStruct(shape, F32)


def near(*shape):
    return pltpu.VMEM(shape, F32)


def fetched(x):
    return pltpu.with_memory_space_constraint(x, pltpu.VMEM)


def shifted(block, axis, distance):
    count = lax.axis_size(axis)
    route = [(i, i + distance) for i in range(count) if 0 <= i + distance < count]
    return lax.ppermute(block, axis, route)


def transit(slab, rec, inj):
    return slab / (1.0 + rec * slab) + inj


def drift_charge(ions, rec, inj, slab):
    once = transit(ions, rec, inj)
    return transit(jnp.where(slab >= 1, once, 0.0), rec, inj)


def roll(x, amount, axis):
    return pltpu.roll(x, amount % x.shape[axis], axis)


def row_tiles(load, tiles, sub):
    x = [load(slice(t * ROWS, (t + 1) * ROWS)) for t in range(tiles)]
    up = [roll(v, -1, 0) for v in x]
    down = [roll(v, 1, 0) for v in x]
    for t in range(tiles):
        higher = jnp.where(sub == ROWS - 1, up[(t + 1) % tiles], up[t])
        lower = jnp.where(sub == 0, down[(t - 1) % tiles], down[t])
        yield t, slice(t * ROWS, (t + 1) * ROWS), x[t], higher, lower


def run_all(copies, sems):
    running = [pltpu.make_async_copy(src, dst, sems.at[k]) for k, (src, dst) in enumerate(copies)]
    for copy in running:
        copy.start()
    return running


def sides_of(count, band):
    if count == 1:
        return [pl.multiple_of(jnp.where(lax.axis_index("radius") == 0, band - ROWS, 0), ROWS)]
    return [0, band - ROWS]


def window_rows(sides, band):
    own = [t * ROWS for t in range(band // ROWS)]
    if sides == 1:
        return [*own, jnp.where(lax.axis_index("radius") == 0, band, -ROWS)]
    return [*own, band, -ROWS]


def rows_kernel(phi, eps, ions, rec, index, gap, table, *rest):
    sides = (len(rest) - 7) // 2
    blocks, pads, stages = rest[:sides], rest[sides], rest[sides + 1 : 2 * sides + 1]
    rec_v, index_v, gap_v, table_s, sems, pad_sems = rest[2 * sides + 1 :]
    layers, band, sector = phi.shape
    ends = SWEEPS - 1
    starts = sides_of(sides, band)
    copies = []
    for start, block, stage in zip(starts, blocks, stages):
        rows = pl.ds(start, ROWS)
        copies.append((phi.at[:, rows], block.at[0:layers]))
        copies.append((eps.at[:, rows], block.at[layers : 2 * layers]))
        copies.append((ions.at[:, rows], stage))
    running = run_all(copies, sems)
    pad_copies = run_all([(rec, rec_v), (index, index_v), (gap, gap_v), (table, table_s)], pad_sems)
    for copy in pad_copies:
        copy.wait()
    for t in range(band // ROWS):
        at = slice(t * ROWS, (t + 1) * ROWS)
        which = index_v[at]
        picked = jnp.zeros((ROWS, sector), F32)
        for k in range(table_s.shape[0]):
            picked = jnp.where(which == k, table_s[k], picked)
        pads[0, at] = rec_v[at]
        pads[1, at] = picked * (1 - gap_v[at]).astype(F32)
    for copy in running:
        copy.wait()
    sub = lax.broadcasted_iota(jnp.int32, (ROWS, sector), 0)
    first_half = sub < ROWS // 2
    for side, (start, block, stage) in enumerate(zip(starts, blocks, stages)):
        tail = (lax.axis_index("radius") == 0) if sides == 1 else side == 1
        base = 2 * layers
        for j in range(layers // 2):
            one, two = stage[2 * j], stage[2 * j + 1]
            from_tail = jnp.where(first_half, roll(one, ROWS // 2, 0), two)
            from_head = jnp.where(first_half, one, roll(two, ROWS // 2, 0))
            block[base + j] = jnp.where(tail, from_tail, from_head)
        base += layers // 2
        for k in range(ends):
            block[base + k] = stage[k]
            block[base + ends + k] = stage[layers - ends + k]
        base += 2 * ends
        for k in range(2):
            block[base + k] = pads[k, pl.ds(start, ROWS)]


def halo_kernel(sides, phi, eps, ions, *refs):
    raws, (inner, outer, far, sems) = refs[:sides], refs[sides:]
    layers, band, _ = phi.shape
    depth = SWEEPS
    odd = lax.rem(lax.axis_index("drift"), 2) == 1
    low, high = 0, layers - depth
    near_at, far_at = jnp.where(odd, low, high), jnp.where(odd, high, low)
    ends = 2 * layers + layers // 2
    copies = []
    for dst, at, k, start, raw_at, count in (
        (inner, 0, 0, near_at, near_at, depth),
        (inner, depth, 1, near_at, layers + near_at, depth),
        (inner, 2 * depth, 2, 0, ends, depth - 1),
        (outer, 0, 0, far_at, far_at, depth),
        (outer, depth, 1, far_at, layers + far_at, depth),
        (far, 0, 2, layers - depth + 1, ends + depth - 1, depth - 1),
    ):
        src = (phi, eps, ions)[k]
        copies.append((src.at[pl.ds(start, count)], dst.at[at : at + count, 0:band]))
        for side, raw in enumerate(raws):
            rows = slice(band + side * ROWS, band + (side + 1) * ROWS)
            copies.append((raw.at[pl.ds(raw_at, count)], dst.at[at : at + count, rows]))
    for copy in run_all(copies, sems):
        copy.wait()


def coupling_rows(z, ex, z_up, z_down, geo, alive, tiles, sub, put):
    for t, at, e, e_up, e_down in row_tiles(lambda s: ex(z, s), tiles, sub):
        not_last, not_first = geo[4, at], geo[5, at]
        right, left = roll(e, -1, 1), roll(e, 1, 1)
        inv_r2 = geo[2, at]
        zu = e + ex(z_up, at)
        zd = e + ex(z_down, at)
        has_up, has_down = geo[8, at], geo[9, at]
        ru = (e + e_up * has_up) * geo[0, at]
        rd = (e + e_down * has_down) * geo[1, at]
        au = (e + right * not_last) * inv_r2
        ad = (e + left * not_first) * inv_r2
        diag = ((zu + zd) + (ru + rd)) + (au + ad)
        inv = jnp.where(geo[3, at] * alive > 0, 1.0 / diag, 0.0)
        radials = (ru * inv * has_up, rd * inv * has_down)
        put(at, (zu * inv, zd * inv, *radials, au * inv * not_last, ad * inv * not_first), inv + inv)


def inner_coupling_kernel(sides, phi, eps, pads, *refs):
    raws, (p0, ex, w, inv2, geo) = refs[:sides], refs[sides:]
    layers, band, sector = phi.shape
    tiles = p0.shape[1] // ROWS
    r, bands = lax.axis_index("radius"), lax.axis_size("radius")
    total_r = band * bands
    sub = lax.broadcasted_iota(jnp.int32, (ROWS, sector), 0)
    lane = lax.broadcasted_iota(jnp.int32, (ROWS, sector), 1)
    half = 0.5 / total_r

    for t, first in enumerate(window_rows(sides, band)):
        at = slice(t * ROWS, (t + 1) * ROWS)
        row = sub + (r * band + first)
        rpos = ((total_r + row).astype(F32) + 0.5) / total_r
        geo[0, at] = (rpos + half) / rpos
        geo[1, at] = (rpos - half) / rpos
        geo[2, at] = 1.0 / (rpos * rpos)
        geo[3, at] = jnp.where((row >= 0) & (row < total_r), 1.0, 0.0)
        geo[4, at] = jnp.where(lane == sector - 1, 0.0, 1.0)
        geo[5, at] = jnp.where(lane == 0, 0.0, 1.0)
        geo[8, at] = jnp.where(row == total_r - 1, 0.0, 1.0)
        geo[9, at] = jnp.where(row == 0, 0.0, 1.0)
    first_pads = 2 * layers + layers // 2 + 2 * (SWEEPS - 1)
    for k in range(2):
        geo[6 + k, 0:band] = pads[k]
        for side, raw in enumerate(raws):
            geo[6 + k, band + side * ROWS : band + (side + 1) * ROWS] = raw[first_pads + k]

    @pl.loop(0, layers)
    def _(z):
        for dst, src, base in ((p0, phi, 0), (ex, eps, layers)):
            dst[z, 0:band] = src[z]
            for side, raw in enumerate(raws):
                dst[z, band + side * ROWS : band + (side + 1) * ROWS] = raw[base + z]

    @pl.loop(1, layers - 1)
    def _(z):
        def put(at, values, twice):
            for k, value in enumerate(values):
                w[k, z, at] = value
            inv2[z, at] = twice

        coupling_rows(z, lambda i, s: ex[i, s], z + 1, z - 1, geo, 1.0, tiles, sub, put)


def sweep_layer(src, src_up, src_down, w, b, tiles, sub, put):
    for t, at, p, p_up, p_down in row_tiles(src, tiles, sub):
        right, left = roll(p, -1, 1), roll(p, 1, 1)
        total = b(at) + (w(0, at) * src_up(at) + w(1, at) * src_down(at))
        total = total + (w(2, at) * p_up + w(3, at) * p_down)
        total = total + (w(4, at) * right + w(5, at) * left)
        put(at, total)


def inner_relax_kernel(sides, moved, p0, w, inv2, geo, *refs):
    rows_moved = refs[:sides]
    charge_out, swap, window_out, sums_out, state, b_out, p1, p2, p3, b, raw = refs[sides:]
    layers, band, sector = moved.shape
    depth = SWEEPS
    tiles = p0.shape[1] // ROWS
    d = lax.axis_index("drift")
    sub = lax.broadcasted_iota(jnp.int32, (ROWS, sector), 0)
    phis = (p0, p1, p2, p3)

    @pl.loop(0, layers // 2)
    def _(j):
        for half in range(2):
            z = 2 * j + half
            inside = (z > 0) & (z < layers - 1)

            def put(at, ions, z=z, inside=inside):
                value = drift_charge(ions, geo[6, at], geo[7, at], d)
                raw[z, at] = value
                b[z, at] = jnp.where(inside, value * inv2[z, at], value)

            own = slice(0, band)
            put(own, moved[z])
            charge_out[z] = raw[z, own]
            for side, packed in enumerate(rows_moved):
                above = (lax.axis_index("radius") == 0) if sides == 1 else side == 0
                two = packed[j]
                turned = roll(two, ROWS // 2, 0)
                ions = jnp.where(above, two, turned) if half == 0 else jnp.where(above, turned, two)
                put(slice(band + side * ROWS, band + (side + 1) * ROWS), ions)

    odd = lax.rem(d, 2) == 1
    for k in range(depth - 1):
        swap[k] = raw[jnp.where(odd, k, layers - depth + 1 + k)]
    sums_out[...] = jnp.zeros_like(sums_out)
    for s in range(1, depth + 1):
        src = phis[s - 1]

        @pl.loop(s, layers - s, step=2)
        def _(first, s=s, src=src):
            for z in (first, first + 1):

                def put(at, total, z=z):
                    if s < depth:
                        phis[s][z, at] = total
                    else:
                        window_out[z - depth, at] = total
                        sums_out[at] += total

                sweep_layer(
                    lambda at, z=z: src[z, at],
                    lambda at, z=z: src[z + 1, at],
                    lambda at, z=z: src[z - 1, at],
                    lambda k, at, z=z: w[k, z, at],
                    lambda at, z=z: b[z, at],
                    tiles,
                    sub,
                    put,
                )

    for s in range(1, depth):
        for k in range(2):
            state[0, s - 1, k] = phis[s][s + k]
            state[1, s - 1, k] = phis[s][layers - s - 2 + k]
    for k in range(depth):
        b_out[0, k] = b[k]
        b_out[1, k] = b[layers - depth + k]


def outer_relax_kernel(inner, outer, far, swapped, p0, ex, w, geo, state, b_in, sums_in, *refs):
    low_out, high_out, sums_out, ph, eh, wb, bb, q = refs
    layers, rows, sector = p0.shape
    depth, n = SWEEPS, layers
    zs = n + 2 * depth
    tiles = rows // ROWS
    d, drifts = lax.axis_index("drift"), lax.axis_size("drift")
    sub = lax.broadcasted_iota(jnp.int32, (ROWS, sector), 0)

    odd = lax.rem(d, 2) == 1
    for k in range(depth):
        for ref, half, to in ((ph, 0, (k, k)), (eh, depth, (k, 2 + k))):
            one, two = inner[half + k], outer[half + k]
            ref[0, to[0]] = jnp.where(odd, one, two)
            ref[1, to[1]] = jnp.where(odd, two, one)
    for k in range(2):
        eh[0, depth + k] = ex[k]
        eh[1, k] = ex[n - 2 + k]

    for k in range(depth - 1):
        rec, inj, ready = geo[6], geo[7], swapped[k]
        bb[0, k] = jnp.where(odd, ready, drift_charge(far[k], rec, inj, d - 1))
        bb[1, k + 1] = jnp.where(odd, drift_charge(inner[2 * depth + k], rec, inj, d + 1), ready)
    bb[0, depth - 1] = b_in[0, 0]
    bb[1, 0] = b_in[1, depth - 1]
    for side in range(2):

        @pl.loop(0, depth)
        def _(k, side=side):
            zg = d * n - depth + (k + 1 if side == 0 else depth + n - 1 + k)
            alive = jnp.where((zg >= 0) & (zg < drifts * n), 1.0, 0.0)

            def put(at, values, twice):
                for j, value in enumerate(values):
                    wb[j, side, k, at] = value
                bb[side, k, at] = bb[side, k, at] * twice

            coupling_rows(k + 1, lambda i, s: eh[side, i, s], k + 2, k, geo, alive, tiles, sub, put)

    def phi_at(s, e):
        if s == 0:
            if e < depth:
                return lambda at: ph[0, e, at]
            if e >= depth + n:
                return lambda at: ph[1, e - depth - n, at]
            return lambda at: p0[e - depth, at]
        z = e - depth
        if s <= z < n - s:
            if z < n // 2:
                return lambda at: state[0, s - 1, z - s, at]
            return lambda at: state[1, s - 1, z - (n - s - 2), at]
        side = 0 if e < zs // 2 else 1
        return lambda at: q[s - 1, side, (e - s) if side == 0 else e - (zs - s - depth), at]

    sums_out[...] = sums_in[...]
    for s in range(1, depth + 1):
        for side in range(2):
            for k in range(depth):
                e = s + k if side == 0 else zs - s - depth + k
                z = e - depth
                if 0 < z < n - 1:
                    w_at = lambda j, at, z=z: w[j, z, at]
                    b_at = lambda at, z=z: b_in[0, z, at] if z < n // 2 else b_in[1, z - (n - depth), at]
                else:
                    at_layer = e - 1 if side == 0 else e - (zs - depth - 1)
                    w_at = lambda j, at, side=side, i=at_layer: wb[j, side, i, at]
                    b_at = lambda at, side=side, i=at_layer: bb[side, i, at]

                def put(at, total, s=s, side=side, k=k):
                    if s < depth:
                        q[s - 1, side, k, at] = total
                    else:
                        (low_out, high_out)[side][k, at] = total
                        sums_out[at] += total

                sweep_layer(phi_at(s - 1, e), phi_at(s - 1, e + 1), phi_at(s - 1, e - 1), w_at, b_at, tiles, sub, put)


def local_kernel(low, inner, high, potential, out, run):
    _, band, _ = potential.shape
    tiles = run.shape[0] // ROWS
    run[...] = jnp.zeros_like(run)
    base = 0
    for window in (low, inner, high):

        @pl.loop(0, window.shape[0])
        def _(k, window=window, base=base):
            for t in range(tiles):
                at = slice(t * ROWS, (t + 1) * ROWS)
                value = window[k, at]
                run[at] += value
                if t < band // ROWS:
                    potential[base + k, at] = value

            def put(at, first, second):
                out[0, base + k, at] = first
                out[1, base + k, at] = second

            ratios_of(run, band, put)

        base += window.shape[0]


def ratios_of(field, band, put):
    rows, sector = field.shape
    r, bands = lax.axis_index("radius"), lax.axis_size("radius")
    total_r = band * bands
    sub = lax.broadcasted_iota(jnp.int32, (ROWS, sector), 0)
    lane = lax.broadcasted_iota(jnp.int32, (ROWS, sector), 1)
    scale = 1.0 / (8.0 * 1.09)
    for t, at, x, higher, lower in row_tiles(lambda s: field[s], rows // ROWS, sub):
        if t < band // ROWS:
            row = sub + (t * ROWS + r * band)
            rpos = ((total_r + row).astype(F32) + 0.5) / total_r
            right = jnp.where(lane == sector - 1, 0.0, roll(x, -1, 1))
            left = jnp.where(lane == 0, 0.0, roll(x, 1, 1))
            higher = jnp.where(row == total_r - 1, 0.0, higher)
            lower = jnp.where(row == 0, 0.0, lower)
            er = (lower - higher) * (0.5 * scale)
            ea = (left - right) * (0.5 * scale / rpos)
            put(at, er + 0.3 * ea, ea - 0.3 * er)


def offset_kernel(local, prefix, out, shift, stage, sems):
    layers = local.shape[1]
    copies = []

    def put(at, first, second):
        shift[0, at] = first
        shift[1, at] = second

    ratios_of(prefix, local.shape[2], put)
    parts = sems.shape[0]
    each = layers // parts
    for k in range(parts):
        for c in range(2):
            stage[c, k * each : (k + 1) * each] = local[c, k * each : (k + 1) * each] + shift[c]
        copy = pltpu.make_async_copy(
            stage.at[:, k * each : (k + 1) * each], out.at[:, k * each : (k + 1) * each], sems.at[k]
        )
        copy.start()
        copies.append(copy)
    for copy in copies:
        copy.wait()


def sums_below(sums):
    count, mine = lax.axis_size("drift"), lax.axis_index("drift")
    assert count & (count - 1) == 0
    total, below, step = sums, jnp.zeros_like(sums), 1
    while step < count:
        other = lax.ppermute(total, "drift", [(i, i ^ step) for i in range(count)])
        below = below + jnp.where((mine & step) > 0, other, 0.0)
        total = total + other
        step *= 2
    return below


def kernel(function, out_shape, in_specs, out_specs=None, scratch=(), mb=16):
    return pl.pallas_call(
        function,
        out_shape=out_shape,
        in_specs=in_specs,
        out_specs=out_specs if out_specs is not None else [IN_VMEM] * len(out_shape),
        scratch_shapes=list(scratch),
        compiler_params=pltpu.CompilerParams(vmem_limit_bytes=mb << 20),
    )


def body(ions, potential_guess, permittivity, recombination, rate_index, gap_mask, rate_table):
    layers, band, sector = ions.shape
    depth = SWEEPS
    sides = 1 if lax.axis_size("radius") == 2 else 2
    rows = band + sides * ROWS
    dma = pltpu.SemaphoreType.DMA
    ends = depth - 1
    row_block = 2 * layers + layers // 2 + 2 * ends + 2
    far_args = (potential_guess, permittivity, ions, recombination, rate_index, gap_mask, rate_table)
    phi, eps, ions_far, *pad_args = [pltpu.with_memory_space_constraint(x, pltpu.HBM) for x in far_args]

    moved = shifted(ions, "drift", 2)
    *blocks, pads = kernel(
        rows_kernel,
        [plane(row_block, ROWS, sector)] * sides + [plane(2, band, sector)],
        [ANYWHERE] * 7,
        scratch=[near(layers, ROWS, sector)] * sides
        + [
            near(band, sector),
            pltpu.VMEM((band, sector), jnp.int32),
            pltpu.VMEM((band, sector), jnp.int32),
            pltpu.SMEM(rate_table.shape, F32),
            dma((3 * sides,)),
            dma((4,)),
        ],
        mb=5,
    )(phi, eps, ions_far, *pad_args)
    if sides == 1:
        raws = [lax.ppermute(blocks[0], "radius", [(0, 1), (1, 0)])]
    else:
        raws = [shifted(blocks[0], "radius", -1), shifted(blocks[1], "radius", 1)]
    to_core, to_chip, beyond = kernel(
        functools.partial(halo_kernel, sides),
        [plane(3 * depth - 1, rows, sector), plane(2 * depth, rows, sector), plane(depth - 1, rows, sector)],
        [ANYWHERE] * 3 + [IN_VMEM] * sides,
        scratch=[dma((6 * (1 + sides),))],
        mb=6,
    )(phi, eps, ions_far, *raws)
    count = lax.axis_size("drift")
    assert count % 2 == 0
    partners = [(i, i ^ 1) for i in range(count)]
    chips = [(i, i + 1 if i % 2 else i - 1) for i in range(1, count - 1)]
    rows_moved = [shifted(raw[2 * layers : 2 * layers + layers // 2], "drift", 2) for raw in raws]
    outer = lax.ppermute(to_chip, "drift", chips)
    far = lax.ppermute(beyond, "drift", [(i - 3, i) for i in range(4, count, 2)])
    inner = lax.ppermute(to_core, "drift", partners)

    box = plane(layers, rows, sector)
    p0, ex, w, inv2, geo = kernel(
        functools.partial(inner_coupling_kernel, sides),
        [box, box, plane(6, layers, rows, sector), box, plane(10, rows, sector)],
        [IN_VMEM] * (3 + sides),
        mb=20,
    )(potential_guess, permittivity, pads, *raws)
    p0, ex, w, inv2, geo = [fetched(x) for x in (p0, ex, w, inv2, geo)]
    charge, swap, middle, sums, state, b = kernel(
        functools.partial(inner_relax_kernel, sides),
        [
            plane(layers, band, sector),
            plane(depth - 1, rows, sector),
            plane(layers - 2 * depth, rows, sector),
            plane(rows, sector),
            plane(2, depth - 1, 2, rows, sector),
            plane(2, depth, rows, sector),
        ],
        [IN_VMEM] * (5 + sides),
        scratch=[near(layers, rows, sector)] * 5,
        mb=16,
    )(moved, p0, w, inv2, geo, *rows_moved)
    swapped = lax.ppermute(swap, "drift", partners)
    low, high, sums = kernel(
        outer_relax_kernel,
        [plane(depth, rows, sector), plane(depth, rows, sector), plane(rows, sector)],
        [IN_VMEM] * 11,
        scratch=[
            near(2, depth, rows, sector),
            near(2, depth + 2, rows, sector),
            near(6, 2, depth, rows, sector),
            near(2, depth, rows, sector),
            near(depth - 1, 2, depth, rows, sector),
        ],
        mb=16,
    )(inner, outer, far, swapped, p0, ex, w, geo, fetched(state), fetched(b), fetched(sums))
    potential, local = kernel(
        local_kernel,
        [plane(layers, band, sector), plane(2, layers, band, sector)],
        [IN_VMEM] * 3,
        scratch=[near(rows, sector)],
        mb=16,
    )(low, middle, high)
    below_sums = sums_below(sums)
    distortion = kernel(
        offset_kernel,
        plane(2, layers, band, sector),
        [IN_VMEM] * 2,
        ANYWHERE,
        [near(2, band, sector), near(2, layers, band, sector), dma((4,))],
        mb=12,
    )(fetched(local), below_sums)
    return charge, potential, distortion


def solution(mesh):
    return jax.shard_map(
        body,
        mesh=mesh,
        in_specs=(
            P("drift", "radius", None),
            P("drift", "radius", None),
            P("drift", "radius", None),
            P("radius", None),
            P("radius", None),
            P("radius", None),
            P(),
        ),
        out_specs=(
            P("drift", "radius", None),
            P("drift", "radius", None),
            P(None, "drift", "radius", None),
        ),
        check_vma=False,
    )
```

```python
import functools

import jax
import jax.numpy as jnp
from jax import lax
from jax.experimental import pallas as pl
from jax.experimental.pallas import tpu as pltpu
from jax.sharding import PartitionSpec as P

SWEEPS = 4
ROWS = 8
F32 = jnp.float32
IN_VMEM = pl.BlockSpec(memory_space=pltpu.VMEM)
ANYWHERE = pl.BlockSpec(memory_space=pl.ANY)


def plane(*shape):
    return jax.ShapeDtypeStruct(shape, F32)


def near(*shape):
    return pltpu.VMEM(shape, F32)


def fetched(x):
    return pltpu.with_memory_space_constraint(x, pltpu.VMEM)


def shifted(block, axis, distance):
    count = lax.axis_size(axis)
    route = [(i, i + distance) for i in range(count) if 0 <= i + distance < count]
    return lax.ppermute(block, axis, route)


def drift_charge(ions, rec, inj, slab):
    below = 1.0 + rec * ions
    above = jnp.where(slab >= 1, ions + inj * below, 0.0)
    return above / (below + rec * above) + inj


def roll(x, amount, axis):
    return pltpu.roll(x, amount % x.shape[axis], axis)


def row_tiles(load, tiles, sub):
    x = [load(slice(t * ROWS, (t + 1) * ROWS)) for t in range(tiles)]
    up = [roll(v, -1, 0) for v in x]
    down = [roll(v, 1, 0) for v in x]
    for t in range(tiles):
        higher = jnp.where(sub == ROWS - 1, up[(t + 1) % tiles], up[t])
        lower = jnp.where(sub == 0, down[(t - 1) % tiles], down[t])
        yield t, slice(t * ROWS, (t + 1) * ROWS), x[t], higher, lower


def run_all(copies, sems):
    running = [pltpu.make_async_copy(src, dst, sems.at[k]) for k, (src, dst) in enumerate(copies)]
    for copy in running:
        copy.start()
    return running


def sides_of(count, band):
    if count == 1:
        return [pl.multiple_of(jnp.where(lax.axis_index("radius") == 0, band - ROWS, 0), ROWS)]
    return [0, band - ROWS]


def window_rows(sides, band):
    own = [t * ROWS for t in range(band // ROWS)]
    if sides == 1:
        return [*own, jnp.where(lax.axis_index("radius") == 0, band, -ROWS)]
    return [*own, band, -ROWS]


def ion_rows_kernel(ions, *rest):
    sides = (len(rest) - 1) // 2
    blocks, stages, sems = rest[:sides], rest[sides : 2 * sides], rest[-1]
    layers, band, sector = ions.shape
    starts = sides_of(sides, band)
    for copy in run_all([(ions.at[:, pl.ds(start, ROWS)], stage) for start, stage in zip(starts, stages)], sems):
        copy.wait()
    first_half = lax.broadcasted_iota(jnp.int32, (ROWS, sector), 0) < ROWS // 2
    for side, (block, stage) in enumerate(zip(blocks, stages)):
        tail = (lax.axis_index("radius") == 0) if sides == 1 else side == 1
        for j in range(layers // 2):
            one, two = stage[2 * j], stage[2 * j + 1]
            from_tail = jnp.where(first_half, roll(one, ROWS // 2, 0), two)
            from_head = jnp.where(first_half, one, roll(two, ROWS // 2, 0))
            block[j] = jnp.where(tail, from_tail, from_head)


def rows_kernel(phi, eps, ions, rec, index, gap, table, *rest):
    sides = len(rest) - 7
    blocks, pads = rest[:sides], rest[sides]
    rec_v, index_v, gap_v, table_s, sems, pad_sems = rest[sides + 1 :]
    layers, band, sector = phi.shape
    ends = SWEEPS - 1
    starts = sides_of(sides, band)
    copies = []
    for start, block in zip(starts, blocks):
        rows = pl.ds(start, ROWS)
        copies.append((phi.at[:, rows], block.at[0:layers]))
        copies.append((eps.at[:, rows], block.at[layers : 2 * layers]))
        copies.append((ions.at[0:ends, rows], block.at[2 * layers : 2 * layers + ends]))
        copies.append((ions.at[layers - ends :, rows], block.at[2 * layers + ends : 2 * layers + 2 * ends]))
    running = run_all(copies, sems)
    pad_copies = run_all([(rec, rec_v), (index, index_v), (gap, gap_v), (table, table_s)], pad_sems)
    for copy in pad_copies:
        copy.wait()
    for t in range(band // ROWS):
        at = slice(t * ROWS, (t + 1) * ROWS)
        which = index_v[at]
        picked = jnp.zeros((ROWS, sector), F32)
        for k in range(table_s.shape[0]):
            picked = jnp.where(which == k, table_s[k], picked)
        pads[0, at] = rec_v[at]
        pads[1, at] = picked * (1 - gap_v[at]).astype(F32)
    for start, block in zip(starts, blocks):
        for k in range(2):
            block[2 * layers + 2 * ends + k] = pads[k, pl.ds(start, ROWS)]
    for copy in running:
        copy.wait()


def halo_kernel(sides, phi, eps, ions, *refs):
    raws, (inner, outer_eps, outer_phi, far, sems) = refs[:sides], refs[sides:]
    layers, band, _ = phi.shape
    depth = SWEEPS
    odd = lax.rem(lax.axis_index("drift"), 2) == 1
    low, high = 0, layers - depth
    near_at, far_at = jnp.where(odd, low, high), jnp.where(odd, high, low)
    ends = 2 * layers
    copies = []
    for dst, at, k, start, raw_at, count in (
        (inner, 0, 0, near_at, near_at, depth),
        (inner, depth, 1, near_at, layers + near_at, depth),
        (inner, 2 * depth, 2, 0, ends, depth - 1),
        (outer_eps, 0, 1, far_at, layers + far_at, depth),
        (outer_phi, 0, 0, far_at, far_at, depth),
        (far, 0, 2, layers - depth + 1, ends + depth - 1, depth - 1),
    ):
        src = (phi, eps, ions)[k]
        copies.append((src.at[pl.ds(start, count)], dst.at[at : at + count, 0:band]))
        for side, raw in enumerate(raws):
            rows = slice(band + side * ROWS, band + (side + 1) * ROWS)
            copies.append((raw.at[pl.ds(raw_at, count)], dst.at[at : at + count, rows]))
    for copy in run_all(copies, sems):
        copy.wait()


def coupling_rows(z, ex, z_up, z_down, geo, alive, tiles, sub, put):
    for t, at, e, e_up, e_down in row_tiles(lambda s: ex(z, s), tiles, sub):
        not_last, not_first = geo[4, at], geo[5, at]
        right, left = roll(e, -1, 1), roll(e, 1, 1)
        inv_r2 = geo[2, at]
        zu = e + ex(z_up, at)
        zd = e + ex(z_down, at)
        has_up, has_down = geo[8, at], geo[9, at]
        ru = (e + e_up * has_up) * geo[0, at]
        rd = (e + e_down * has_down) * geo[1, at]
        au = (e + right * not_last) * inv_r2
        ad = (e + left * not_first) * inv_r2
        diag = ((zu + zd) + (ru + rd)) + (au + ad)
        inv = jnp.where(geo[3, at] * alive > 0, 1.0 / diag, 0.0)
        radials = (ru * inv * has_up, rd * inv * has_down)
        put(at, (zu * inv, zd * inv, *radials, au * inv * not_last, ad * inv * not_first), inv + inv)


def inner_coupling_kernel(sides, phi, eps, pads, *refs):
    raws, (p0, ex, w, inv2, geo) = refs[:sides], refs[sides:]
    layers, band, sector = phi.shape
    tiles = p0.shape[1] // ROWS
    r, bands = lax.axis_index("radius"), lax.axis_size("radius")
    total_r = band * bands
    sub = lax.broadcasted_iota(jnp.int32, (ROWS, sector), 0)
    lane = lax.broadcasted_iota(jnp.int32, (ROWS, sector), 1)
    half = 0.5 / total_r

    for t, first in enumerate(window_rows(sides, band)):
        at = slice(t * ROWS, (t + 1) * ROWS)
        row = sub + (r * band + first)
        rpos = ((total_r + row).astype(F32) + 0.5) / total_r
        geo[0, at] = (rpos + half) / rpos
        geo[1, at] = (rpos - half) / rpos
        geo[2, at] = 1.0 / (rpos * rpos)
        geo[3, at] = jnp.where((row >= 0) & (row < total_r), 1.0, 0.0)
        geo[4, at] = jnp.where(lane == sector - 1, 0.0, 1.0)
        geo[5, at] = jnp.where(lane == 0, 0.0, 1.0)
        geo[8, at] = jnp.where(row == total_r - 1, 0.0, 1.0)
        geo[9, at] = jnp.where(row == 0, 0.0, 1.0)
    first_pads = 2 * layers + 2 * (SWEEPS - 1)
    for k in range(2):
        geo[6 + k, 0:band] = pads[k]
        for side, raw in enumerate(raws):
            geo[6 + k, band + side * ROWS : band + (side + 1) * ROWS] = raw[first_pads + k]

    @pl.loop(0, layers)
    def _(z):
        for dst, src, base in ((p0, phi, 0), (ex, eps, layers)):
            dst[z, 0:band] = src[z]
            for side, raw in enumerate(raws):
                dst[z, band + side * ROWS : band + (side + 1) * ROWS] = raw[base + z]

    @pl.loop(1, layers - 1)
    def _(z):
        def put(at, values, twice):
            for k, value in enumerate(values):
                w[k, z, at] = value
            inv2[z, at] = twice

        coupling_rows(z, lambda i, s: ex[i, s], z + 1, z - 1, geo, 1.0, tiles, sub, put)


def sweep_layer(src, src_up, src_down, w, b, tiles, sub, put):
    for t, at, p, p_up, p_down in row_tiles(src, tiles, sub):
        right, left = roll(p, -1, 1), roll(p, 1, 1)
        total = b(at) + (w(0, at) * src_up(at) + w(1, at) * src_down(at))
        total = total + (w(2, at) * p_up + w(3, at) * p_down)
        total = total + (w(4, at) * right + w(5, at) * left)
        put(at, total)


def charge_kernel(sides, moved, inv2, geo, *refs):
    rows_moved = refs[:sides]
    raw, swap, b = refs[sides:]
    layers, band, _ = moved.shape
    ends = SWEEPS - 1
    d = lax.axis_index("drift")

    @pl.loop(0, layers // 2)
    def _(j):
        for half in range(2):
            z = 2 * j + half
            inside = (z > 0) & (z < layers - 1)

            def put(at, ions, z=z, inside=inside):
                value = drift_charge(ions, geo[6, at], geo[7, at], d)
                raw[z, at] = value
                b[z, at] = jnp.where(inside, value * inv2[z, at], value)

            put(slice(0, band), moved[z])
            for side, packed in enumerate(rows_moved):
                above = (lax.axis_index("radius") == 0) if sides == 1 else side == 0
                two = packed[j]
                turned = roll(two, ROWS // 2, 0)
                ions = jnp.where(above, two, turned) if half == 0 else jnp.where(above, turned, two)
                put(slice(band + side * ROWS, band + (side + 1) * ROWS), ions)

    odd = lax.rem(d, 2) == 1
    for k in range(ends):
        swap[k] = raw[jnp.where(odd, k, layers - ends + k)]


def inner_relax_kernel(p0, w, b, raw, charge_out, window_out, sums_out, state, p1, p2, p3, sem):
    layers, rows, sector = p0.shape
    charge_copy = pltpu.make_async_copy(raw.at[:, 0 : charge_out.shape[1]], charge_out, sem)
    charge_copy.start()
    depth = SWEEPS
    tiles = rows // ROWS
    sub = lax.broadcasted_iota(jnp.int32, (ROWS, sector), 0)
    phis = (p0, p1, p2, p3)
    sums_out[...] = jnp.zeros_like(sums_out)
    for s in range(1, depth + 1):
        src = phis[s - 1]
        for z in range(s, layers - s):

            def put(at, total, s=s, z=z):
                if s < depth:
                    phis[s][z, at] = total
                    if z - s < 2:
                        state[0, s - 1, z - s, at] = total
                    if z - (layers - s - 2) >= 0:
                        state[1, s - 1, z - (layers - s - 2), at] = total
                else:
                    window_out[z - depth, at] = total
                    sums_out[at] += total

            sweep_layer(
                lambda at, z=z, src=src: src[z, at],
                lambda at, z=z, src=src: src[z + 1, at],
                lambda at, z=z, src=src: src[z - 1, at],
                lambda k, at, z=z: w[k, z, at],
                lambda at, z=z: b[z, at],
                tiles,
                sub,
                put,
            )
    charge_copy.wait()


def outer_coupling_kernel(inner, outer_eps, far, ex, geo, wb, bb, eh):
    layers, rows, sector = ex.shape
    depth, n = SWEEPS, layers
    tiles = rows // ROWS
    d, drifts = lax.axis_index("drift"), lax.axis_size("drift")
    odd = lax.rem(d, 2) == 1
    sub = lax.broadcasted_iota(jnp.int32, (ROWS, sector), 0)

    for k in range(depth):
        one, two = inner[depth + k], outer_eps[k]
        eh[0, k] = jnp.where(odd, one, two)
        eh[1, 2 + k] = jnp.where(odd, two, one)
    for k in range(2):
        eh[0, depth + k] = ex[k]
        eh[1, k] = ex[n - 2 + k]

    for k in range(depth - 1):
        rec, inj = geo[6], geo[7]
        bb[0, k] = jnp.where(odd, 1.0, drift_charge(far[k], rec, inj, d - 1))
        bb[1, k + 1] = jnp.where(odd, drift_charge(inner[2 * depth + k], rec, inj, d + 1), 1.0)
    bb[0, depth - 1] = jnp.ones_like(bb[0, 0])
    bb[1, 0] = jnp.ones_like(bb[1, 0])
    for side in range(2):

        @pl.loop(0, depth)
        def _(k, side=side):
            zg = d * n - depth + (k + 1 if side == 0 else depth + n - 1 + k)
            alive = jnp.where((zg >= 0) & (zg < drifts * n), 1.0, 0.0)

            def put(at, values, twice):
                for j, value in enumerate(values):
                    wb[j, side, k, at] = value
                bb[side, k, at] = bb[side, k, at] * twice

            coupling_rows(k + 1, lambda i, s: eh[side, i, s], k + 2, k, geo, alive, tiles, sub, put)


def outer_relax_kernel(
    inner, outer_phi, swapped, p0, w, wb, bb_in, state, b_in, sums_in, low_out, high_out, sums_out, ph, bb, q
):
    layers, rows, sector = p0.shape
    depth, n = SWEEPS, layers
    zs = n + 2 * depth
    tiles = rows // ROWS
    odd = lax.rem(lax.axis_index("drift"), 2) == 1
    sub = lax.broadcasted_iota(jnp.int32, (ROWS, sector), 0)
    for k in range(depth):
        one, two = inner[k], outer_phi[k]
        ph[0, k] = jnp.where(odd, one, two)
        ph[1, k] = jnp.where(odd, two, one)
    for k in range(depth - 1):
        ready = swapped[k]
        bb[0, k] = bb_in[0, k] * jnp.where(odd, ready, 1.0)
        bb[1, k + 1] = bb_in[1, k + 1] * jnp.where(odd, 1.0, ready)
    bb[0, depth - 1] = bb_in[0, depth - 1] * b_in[0]
    bb[1, 0] = bb_in[1, 0] * b_in[n - 1]

    def phi_at(s, e):
        if s == 0:
            if e < depth:
                return lambda at: ph[0, e, at]
            if e >= depth + n:
                return lambda at: ph[1, e - depth - n, at]
            return lambda at: p0[e - depth, at]
        z = e - depth
        if s <= z < n - s:
            if z < n // 2:
                return lambda at: state[0, s - 1, z - s, at]
            return lambda at: state[1, s - 1, z - (n - s - 2), at]
        side = 0 if e < zs // 2 else 1
        return lambda at: q[s - 1, side, (e - s) if side == 0 else e - (zs - s - depth), at]

    sums_out[...] = sums_in[...]
    for s in range(1, depth + 1):
        for side in range(2):
            for k in range(depth):
                e = s + k if side == 0 else zs - s - depth + k
                z = e - depth
                if 0 < z < n - 1:
                    w_at = lambda j, at, z=z: w[j, z, at]
                    b_at = lambda at, z=z: b_in[z, at]
                else:
                    at_layer = e - 1 if side == 0 else e - (zs - depth - 1)
                    w_at = lambda j, at, side=side, i=at_layer: wb[j, side, i, at]
                    b_at = lambda at, side=side, i=at_layer: bb[side, i, at]

                def put(at, total, s=s, side=side, k=k):
                    if s < depth:
                        q[s - 1, side, k, at] = total
                    else:
                        (low_out, high_out)[side][k, at] = total
                        sums_out[at] += total

                sweep_layer(phi_at(s - 1, e), phi_at(s - 1, e + 1), phi_at(s - 1, e - 1), w_at, b_at, tiles, sub, put)


def local_kernel(low, inner, high, potential, out, run):
    _, band, _ = potential.shape
    tiles = run.shape[0] // ROWS
    run[...] = jnp.zeros_like(run)
    base = 0
    for window in (low, inner, high):

        @pl.loop(0, window.shape[0])
        def _(k, window=window, base=base):
            for t in range(tiles):
                at = slice(t * ROWS, (t + 1) * ROWS)
                value = window[k, at]
                run[at] += value
                if t < band // ROWS:
                    potential[base + k, at] = value

            def put(at, first, second):
                out[0, base + k, at] = first
                out[1, base + k, at] = second

            ratios_of(run, band, put)

        base += window.shape[0]


def ratios_of(field, band, put):
    rows, sector = field.shape
    r, bands = lax.axis_index("radius"), lax.axis_size("radius")
    total_r = band * bands
    sub = lax.broadcasted_iota(jnp.int32, (ROWS, sector), 0)
    lane = lax.broadcasted_iota(jnp.int32, (ROWS, sector), 1)
    scale = 1.0 / (8.0 * 1.09)
    for t, at, x, higher, lower in row_tiles(lambda s: field[s], rows // ROWS, sub):
        if t < band // ROWS:
            row = sub + (t * ROWS + r * band)
            rpos = ((total_r + row).astype(F32) + 0.5) / total_r
            right = jnp.where(lane == sector - 1, 0.0, roll(x, -1, 1))
            left = jnp.where(lane == 0, 0.0, roll(x, 1, 1))
            higher = jnp.where(row == total_r - 1, 0.0, higher)
            lower = jnp.where(row == 0, 0.0, lower)
            er = (lower - higher) * (0.5 * scale)
            ea = (left - right) * (0.5 * scale / rpos)
            put(at, er + 0.3 * ea, ea - 0.3 * er)


def offset_kernel(local, prefix, out, shift, stage, sems):
    layers = local.shape[1]
    copies = []

    def put(at, first, second):
        shift[0, at] = first
        shift[1, at] = second

    ratios_of(prefix, local.shape[2], put)
    parts = sems.shape[0]
    each = layers // parts
    for k in range(parts):
        for c in range(2):
            stage[c, k * each : (k + 1) * each] = local[c, k * each : (k + 1) * each] + shift[c]
        copy = pltpu.make_async_copy(
            stage.at[:, k * each : (k + 1) * each], out.at[:, k * each : (k + 1) * each], sems.at[k]
        )
        copy.start()
        copies.append(copy)
    for copy in copies:
        copy.wait()


def sums_below(sums):
    count, mine = lax.axis_size("drift"), lax.axis_index("drift")
    assert count & (count - 1) == 0
    total, below, step = sums, jnp.zeros_like(sums), 1
    while step < count:
        other = lax.ppermute(total, "drift", [(i, i ^ step) for i in range(count)])
        below = below + jnp.where((mine & step) > 0, other, 0.0)
        total = total + other
        step *= 2
    return below


def kernel(function, out_shape, in_specs, out_specs=None, scratch=(), mb=16):
    return pl.pallas_call(
        function,
        out_shape=out_shape,
        in_specs=in_specs,
        out_specs=out_specs if out_specs is not None else [IN_VMEM] * len(out_shape),
        scratch_shapes=list(scratch),
        compiler_params=pltpu.CompilerParams(vmem_limit_bytes=mb << 20),
    )


def body(ions, potential_guess, permittivity, recombination, rate_index, gap_mask, rate_table):
    layers, band, sector = ions.shape
    depth = SWEEPS
    sides = 1 if lax.axis_size("radius") == 2 else 2
    rows = band + sides * ROWS
    dma = pltpu.SemaphoreType.DMA
    ends = depth - 1
    row_block = 2 * layers + 2 * ends + 2
    far_args = (potential_guess, permittivity, ions, recombination, rate_index, gap_mask, rate_table)
    phi, eps, ions_far, *pad_args = [pltpu.with_memory_space_constraint(x, pltpu.HBM) for x in far_args]

    moved = shifted(ions, "drift", 2)

    def swap_rows(blocks):
        if sides == 1:
            return [lax.ppermute(blocks[0], "radius", [(0, 1), (1, 0)])]
        return [shifted(blocks[0], "radius", -1), shifted(blocks[1], "radius", 1)]

    ion_blocks = kernel(
        ion_rows_kernel,
        [plane(layers // 2, ROWS, sector)] * sides,
        [ANYWHERE],
        scratch=[near(layers, ROWS, sector)] * sides + [dma((sides,))],
        mb=3,
    )(ions_far)
    ion_raws = swap_rows(ion_blocks)
    *blocks, pads = kernel(
        rows_kernel,
        [plane(row_block, ROWS, sector)] * sides + [plane(2, band, sector)],
        [ANYWHERE] * 7,
        scratch=[
            near(band, sector),
            pltpu.VMEM((band, sector), jnp.int32),
            pltpu.VMEM((band, sector), jnp.int32),
            pltpu.SMEM(rate_table.shape, F32),
            dma((4 * sides,)),
            dma((4,)),
        ],
        mb=5,
    )(phi, eps, ions_far, *pad_args)
    raws = swap_rows(blocks)
    rows_moved = [shifted(raw, "drift", 2) for raw in ion_raws]
    to_core, eps_block, phi_block, beyond = kernel(
        functools.partial(halo_kernel, sides),
        [plane(k, rows, sector) for k in (3 * depth - 1, depth, depth, depth - 1)],
        [ANYWHERE] * 3 + [IN_VMEM] * sides,
        scratch=[dma((6 * (1 + sides),))],
        mb=6,
    )(phi, eps, ions_far, *raws)
    count = lax.axis_size("drift")
    assert count % 2 == 0
    partners = [(i, i ^ 1) for i in range(count)]
    chips = [(i, i + 1 if i % 2 else i - 1) for i in range(1, count - 1)]
    outer_eps = lax.ppermute(eps_block, "drift", chips)
    far = lax.ppermute(beyond, "drift", [(i - 3, i) for i in range(4, count, 2)])
    inner = lax.ppermute(to_core, "drift", partners)
    outer_phi = lax.ppermute(phi_block, "drift", chips)

    box = plane(layers, rows, sector)
    p0, ex, w, inv2, geo = kernel(
        functools.partial(inner_coupling_kernel, sides),
        [box, box, plane(6, layers, rows, sector), box, plane(10, rows, sector)],
        [IN_VMEM] * (3 + sides),
        mb=20,
    )(potential_guess, permittivity, pads, *raws)
    p0, ex, w, inv2, geo = [fetched(x) for x in (p0, ex, w, inv2, geo)]
    wb, bb = kernel(
        outer_coupling_kernel,
        [plane(6, 2, depth, rows, sector), plane(2, depth, rows, sector)],
        [IN_VMEM] * 5,
        scratch=[near(2, depth + 2, rows, sector)],
        mb=12,
    )(inner, outer_eps, far, ex, geo)
    wb, bb = fetched(wb), fetched(bb)
    raw, swap, b = kernel(
        functools.partial(charge_kernel, sides),
        [box, plane(depth - 1, rows, sector), box],
        [IN_VMEM] * (3 + sides),
        mb=8,
    )(moved, inv2, geo, *rows_moved)
    raw, b = fetched(raw), fetched(b)
    swapped = lax.ppermute(swap, "drift", partners)
    charge, middle, sums, state = kernel(
        inner_relax_kernel,
        [
            plane(layers, band, sector),
            plane(layers - 2 * depth, rows, sector),
            plane(rows, sector),
            plane(2, depth - 1, 2, rows, sector),
        ],
        [IN_VMEM] * 4,
        [ANYWHERE] + [IN_VMEM] * 3,
        scratch=[near(layers, rows, sector)] * 3 + [dma],
        mb=12,
    )(p0, w, b, raw)
    state, sums = fetched(state), fetched(sums)
    low, high, sums = kernel(
        outer_relax_kernel,
        [plane(depth, rows, sector), plane(depth, rows, sector), plane(rows, sector)],
        [IN_VMEM] * 10,
        scratch=[near(2, depth, rows, sector), near(2, depth, rows, sector), near(depth - 1, 2, depth, rows, sector)],
        mb=12,
    )(inner, outer_phi, swapped, p0, w, wb, bb, state, b, sums)
    potential, local = kernel(
        local_kernel,
        [plane(layers, band, sector), plane(2, layers, band, sector)],
        [IN_VMEM] * 3,
        scratch=[near(rows, sector)],
        mb=16,
    )(low, middle, high)
    below_sums = sums_below(sums)
    distortion = kernel(
        offset_kernel,
        plane(2, layers, band, sector),
        [IN_VMEM] * 2,
        ANYWHERE,
        [near(2, band, sector), near(2, layers, band, sector), dma((4,))],
        mb=12,
    )(fetched(local), below_sums)
    return charge, potential, distortion


def solution(mesh):
    return jax.shard_map(
        body,
        mesh=mesh,
        in_specs=(
            P("drift", "radius", None),
            P("drift", "radius", None),
            P("drift", "radius", None),
            P("radius", None),
            P("radius", None),
            P("radius", None),
            P(),
        ),
        out_specs=(
            P("drift", "radius", None),
            P("drift", "radius", None),
            P(None, "drift", "radius", None),
        ),
        check_vma=False,
    )
```

```python
import functools

import jax
import jax.numpy as jnp
from jax import lax
from jax.experimental import pallas as pl
from jax.experimental.pallas import tpu as pltpu
from jax.sharding import PartitionSpec as P

SWEEPS = 4
ROWS = 8
F32 = jnp.float32
IN_VMEM = pl.BlockSpec(memory_space=pltpu.VMEM)
ANYWHERE = pl.BlockSpec(memory_space=pl.ANY)


def plane(*shape):
    return jax.ShapeDtypeStruct(shape, F32)


def near(*shape):
    return pltpu.VMEM(shape, F32)


def fetched(x):
    return pltpu.with_memory_space_constraint(x, pltpu.VMEM)


def shifted(block, axis, distance):
    count = lax.axis_size(axis)
    route = [(i, i + distance) for i in range(count) if 0 <= i + distance < count]
    return lax.ppermute(block, axis, route)


def drift_charge(ions, rec, inj, slab):
    below = 1.0 + rec * ions
    above = jnp.where(slab >= 1, ions + inj * below, 0.0)
    return above / (below + rec * above) + inj


def roll(x, amount, axis):
    return pltpu.roll(x, amount % x.shape[axis], axis)


def row_tiles(load, tiles, sub):
    x = [load(slice(t * ROWS, (t + 1) * ROWS)) for t in range(tiles)]
    up = [roll(v, -1, 0) for v in x]
    down = [roll(v, 1, 0) for v in x]
    for t in range(tiles):
        higher = jnp.where(sub == ROWS - 1, up[(t + 1) % tiles], up[t])
        lower = jnp.where(sub == 0, down[(t - 1) % tiles], down[t])
        yield t, slice(t * ROWS, (t + 1) * ROWS), x[t], higher, lower


def run_all(copies, sems):
    running = [pltpu.make_async_copy(src, dst, sems.at[k]) for k, (src, dst) in enumerate(copies)]
    for copy in running:
        copy.start()
    return running


def sides_of(count, band):
    if count == 1:
        return [pl.multiple_of(jnp.where(lax.axis_index("radius") == 0, band - ROWS, 0), ROWS)]
    return [0, band - ROWS]


def window_rows(sides, band):
    own = [t * ROWS for t in range(band // ROWS)]
    if sides == 1:
        return [*own, jnp.where(lax.axis_index("radius") == 0, band, -ROWS)]
    return [*own, band, -ROWS]


def ion_rows_kernel(ions, *rest):
    sides = (len(rest) - 1) // 2
    blocks, stages, sems = rest[:sides], rest[sides : 2 * sides], rest[-1]
    layers, band, sector = ions.shape
    starts = sides_of(sides, band)
    for copy in run_all([(ions.at[:, pl.ds(start, ROWS)], stage) for start, stage in zip(starts, stages)], sems):
        copy.wait()
    first_half = lax.broadcasted_iota(jnp.int32, (ROWS, sector), 0) < ROWS // 2
    for side, (block, stage) in enumerate(zip(blocks, stages)):
        tail = (lax.axis_index("radius") == 0) if sides == 1 else side == 1
        for j in range(layers // 2):
            one, two = stage[2 * j], stage[2 * j + 1]
            from_tail = jnp.where(first_half, roll(one, ROWS // 2, 0), two)
            from_head = jnp.where(first_half, one, roll(two, ROWS // 2, 0))
            block[j] = jnp.where(tail, from_tail, from_head)


def rows_kernel(phi, eps, ions, rec, index, gap, table, *rest):
    sides = len(rest) - 7
    blocks, pads = rest[:sides], rest[sides]
    rec_v, index_v, gap_v, table_s, sems, pad_sems = rest[sides + 1 :]
    layers, band, sector = phi.shape
    ends = SWEEPS - 1
    starts = sides_of(sides, band)
    copies = []
    for start, block in zip(starts, blocks):
        rows = pl.ds(start, ROWS)
        copies.append((phi.at[:, rows], block.at[0:layers]))
        copies.append((eps.at[:, rows], block.at[layers : 2 * layers]))
        copies.append((ions.at[0:ends, rows], block.at[2 * layers : 2 * layers + ends]))
        copies.append((ions.at[layers - ends :, rows], block.at[2 * layers + ends : 2 * layers + 2 * ends]))
    running = run_all(copies, sems)
    pad_copies = run_all([(rec, rec_v), (index, index_v), (gap, gap_v), (table, table_s)], pad_sems)
    for copy in pad_copies:
        copy.wait()
    for t in range(band // ROWS):
        at = slice(t * ROWS, (t + 1) * ROWS)
        which = index_v[at]
        picked = jnp.zeros((ROWS, sector), F32)
        for k in range(table_s.shape[0]):
            picked = jnp.where(which == k, table_s[k], picked)
        pads[0, at] = rec_v[at]
        pads[1, at] = picked * (1 - gap_v[at]).astype(F32)
    for start, block in zip(starts, blocks):
        for k in range(2):
            block[2 * layers + 2 * ends + k] = pads[k, pl.ds(start, ROWS)]
    for copy in running:
        copy.wait()


def halo_kernel(sides, phi, eps, ions, *refs):
    raws, (inner, outer_eps, outer_phi, far, sems) = refs[:sides], refs[sides:]
    layers, band, _ = phi.shape
    depth = SWEEPS
    odd = lax.rem(lax.axis_index("drift"), 2) == 1
    low, high = 0, layers - depth
    near_at, far_at = jnp.where(odd, low, high), jnp.where(odd, high, low)
    ends = 2 * layers
    copies = []
    for dst, at, k, start, raw_at, count in (
        (inner, 0, 0, near_at, near_at, depth),
        (inner, depth, 1, near_at, layers + near_at, depth),
        (inner, 2 * depth, 2, 0, ends, depth - 1),
        (outer_eps, 0, 1, far_at, layers + far_at, depth),
        (outer_phi, 0, 0, far_at, far_at, depth),
        (far, 0, 2, layers - depth + 1, ends + depth - 1, depth - 1),
    ):
        src = (phi, eps, ions)[k]
        copies.append((src.at[pl.ds(start, count)], dst.at[at : at + count, 0:band]))
        for side, raw in enumerate(raws):
            rows = slice(band + side * ROWS, band + (side + 1) * ROWS)
            copies.append((raw.at[pl.ds(raw_at, count)], dst.at[at : at + count, rows]))
    for copy in run_all(copies, sems):
        copy.wait()


def coupling_rows(z, ex, z_up, z_down, geo, alive, tiles, sub, put):
    for t, at, e, e_up, e_down in row_tiles(lambda s: ex(z, s), tiles, sub):
        not_last, not_first = geo[4, at], geo[5, at]
        right, left = roll(e, -1, 1), roll(e, 1, 1)
        inv_r2 = geo[2, at]
        zu = e + ex(z_up, at)
        zd = e + ex(z_down, at)
        has_up, has_down = geo[8, at], geo[9, at]
        ru = (e + e_up * has_up) * geo[0, at]
        rd = (e + e_down * has_down) * geo[1, at]
        au = (e + right * not_last) * inv_r2
        ad = (e + left * not_first) * inv_r2
        diag = ((zu + zd) + (ru + rd)) + (au + ad)
        inv = jnp.where(geo[3, at] * alive > 0, 1.0 / diag, 0.0)
        radials = (ru * inv * has_up, rd * inv * has_down)
        put(at, (zu * inv, zd * inv, *radials, au * inv * not_last, ad * inv * not_first), inv + inv)


def inner_coupling_kernel(sides, phi, eps, pads, *refs):
    raws, (p0, ex, w, inv2, geo) = refs[:sides], refs[sides:]
    layers, band, sector = phi.shape
    tiles = p0.shape[1] // ROWS
    r, bands = lax.axis_index("radius"), lax.axis_size("radius")
    total_r = band * bands
    sub = lax.broadcasted_iota(jnp.int32, (ROWS, sector), 0)
    lane = lax.broadcasted_iota(jnp.int32, (ROWS, sector), 1)
    half = 0.5 / total_r

    for t, first in enumerate(window_rows(sides, band)):
        at = slice(t * ROWS, (t + 1) * ROWS)
        row = sub + (r * band + first)
        rpos = ((total_r + row).astype(F32) + 0.5) / total_r
        geo[0, at] = (rpos + half) / rpos
        geo[1, at] = (rpos - half) / rpos
        geo[2, at] = 1.0 / (rpos * rpos)
        geo[3, at] = jnp.where((row >= 0) & (row < total_r), 1.0, 0.0)
        geo[4, at] = jnp.where(lane == sector - 1, 0.0, 1.0)
        geo[5, at] = jnp.where(lane == 0, 0.0, 1.0)
        geo[8, at] = jnp.where(row == total_r - 1, 0.0, 1.0)
        geo[9, at] = jnp.where(row == 0, 0.0, 1.0)
    first_pads = 2 * layers + 2 * (SWEEPS - 1)
    for k in range(2):
        geo[6 + k, 0:band] = pads[k]
        for side, raw in enumerate(raws):
            geo[6 + k, band + side * ROWS : band + (side + 1) * ROWS] = raw[first_pads + k]

    @pl.loop(0, layers)
    def _(z):
        for dst, src, base in ((p0, phi, 0), (ex, eps, layers)):
            dst[z, 0:band] = src[z]
            for side, raw in enumerate(raws):
                dst[z, band + side * ROWS : band + (side + 1) * ROWS] = raw[base + z]

    @pl.loop(1, layers - 1)
    def _(z):
        def put(at, values, twice):
            for k, value in enumerate(values):
                w[k, z, at] = value
            inv2[z, at] = twice

        coupling_rows(z, lambda i, s: ex[i, s], z + 1, z - 1, geo, 1.0, tiles, sub, put)


def sweep_layer(src, src_up, src_down, w, b, tiles, sub, put):
    for t, at, p, p_up, p_down in row_tiles(src, tiles, sub):
        right, left = roll(p, -1, 1), roll(p, 1, 1)
        total = b(at) + (w(0, at) * src_up(at) + w(1, at) * src_down(at))
        total = total + (w(2, at) * p_up + w(3, at) * p_down)
        total = total + (w(4, at) * right + w(5, at) * left)
        put(at, total)


def charge_kernel(sides, moved, inv2, geo, *refs):
    rows_moved = refs[:sides]
    raw, swap, b = refs[sides:]
    layers, band, _ = moved.shape
    ends = SWEEPS - 1
    d = lax.axis_index("drift")

    @pl.loop(0, layers // 2)
    def _(j):
        for half in range(2):
            z = 2 * j + half
            inside = (z > 0) & (z < layers - 1)

            def put(at, ions, z=z, inside=inside):
                value = drift_charge(ions, geo[6, at], geo[7, at], d)
                raw[z, at] = value
                b[z, at] = jnp.where(inside, value * inv2[z, at], value)

            put(slice(0, band), moved[z])
            for side, packed in enumerate(rows_moved):
                above = (lax.axis_index("radius") == 0) if sides == 1 else side == 0
                two = packed[j]
                turned = roll(two, ROWS // 2, 0)
                ions = jnp.where(above, two, turned) if half == 0 else jnp.where(above, turned, two)
                put(slice(band + side * ROWS, band + (side + 1) * ROWS), ions)

    odd = lax.rem(d, 2) == 1
    for k in range(ends):
        swap[k] = raw[jnp.where(odd, k, layers - ends + k)]


def inner_relax_kernel(p0, w, b, raw, charge_out, window_out, sums_out, state, p1, p2, p3, sem):
    layers, rows, sector = p0.shape
    charge_copy = pltpu.make_async_copy(raw.at[:, 0 : charge_out.shape[1]], charge_out, sem)
    charge_copy.start()
    depth = SWEEPS
    tiles = rows // ROWS
    sub = lax.broadcasted_iota(jnp.int32, (ROWS, sector), 0)
    phis = (p0, p1, p2, p3)
    sums_out[...] = jnp.zeros_like(sums_out)
    for s in range(1, depth + 1):
        src = phis[s - 1]
        for z in range(s, layers - s):

            def put(at, total, s=s, z=z):
                if s < depth:
                    phis[s][z, at] = total
                    if z - s < 2:
                        state[0, s - 1, z - s, at] = total
                    if z - (layers - s - 2) >= 0:
                        state[1, s - 1, z - (layers - s - 2), at] = total
                else:
                    window_out[z - depth, at] = total
                    sums_out[at] += total

            sweep_layer(
                lambda at, z=z, src=src: src[z, at],
                lambda at, z=z, src=src: src[z + 1, at],
                lambda at, z=z, src=src: src[z - 1, at],
                lambda k, at, z=z: w[k, z, at],
                lambda at, z=z: b[z, at],
                tiles,
                sub,
                put,
            )
    charge_copy.wait()


class Wedge:
    def __init__(self, near, layers):
        d = lax.axis_index("drift")
        odd = lax.rem(d, 2)
        self.n, self.d = layers, d
        self.high = (1 - odd) if near else odd
        self.is_high = self.high == 1

    def own(self, q):
        return jnp.where(self.is_high, self.n - 1 - q, q)

    def sent(self, q, count):
        return jnp.where(self.is_high, -q - 1, count + q)

    def alive(self, q):
        z = self.d * self.n + self.own(q)
        return jnp.where((z >= 0) & (z < lax.axis_size("drift") * self.n), 1.0, 0.0)


def wedge_couplings(wedge, halo, halo_at, charge, ex, geo, wb, bb, eh):
    depth = SWEEPS
    rows, sector = eh.shape[1:]
    sub = lax.broadcasted_iota(jnp.int32, (ROWS, sector), 0)
    for q in range(-depth, 2):
        eh[depth + q] = halo[halo_at + wedge.sent(q, depth)] if q < 0 else ex[wedge.own(q)]
    for k in range(depth):
        q = k + 1 - depth
        bb[k] = charge(q) if q < 0 else jnp.ones_like(bb[0])

        def put(at, values, twice, k=k):
            for j, value in enumerate(values):
                wb[j, k, at] = value
            bb[k, at] = bb[k, at] * twice

        coupling_rows(
            k + 1, lambda i, at: eh[i, at], k + 2, k, geo, wedge.alive(q), rows // ROWS, sub, put
        )


def wedge_sweeps(wedge, halo, p0, w, wb, bb, state, b_in, q_buf, out, sums):
    depth = SWEEPS
    rows, sector = p0.shape[1:]
    sub = lax.broadcasted_iota(jnp.int32, (ROWS, sector), 0)

    def phi_at(s, q):
        if s == 0:
            if q < 0:
                spot = wedge.sent(q, depth)
                return lambda at: halo[spot, at]
            spot = wedge.own(q)
            return lambda at: p0[spot, at]
        if q >= s:
            spot = jnp.where(wedge.is_high, 1 - (q - s), q - s)
            return lambda at: state[wedge.high, s - 1, spot, at]
        return lambda at: q_buf[s - 1, q - s + depth, at]

    def coupling(q):
        if q <= 0:
            return lambda j, at: wb[j, q + depth - 1, at]
        z = wedge.own(q)
        inward, outward = wedge.high, 1 - wedge.high
        return lambda j, at: w[(inward, outward, 2, 3, 4, 5)[j], z, at]

    for s in range(1, depth + 1):
        for q in range(s - depth, s):
            if q <= 0:
                b_at = lambda at, q=q: bb[q + depth - 1, at]
            else:
                b_at = lambda at, z=wedge.own(q): b_in[z, at]

            def put(at, total, s=s, q=q):
                if s < depth:
                    q_buf[s - 1, q - s + depth, at] = total
                else:
                    out[jnp.where(wedge.is_high, depth - 1 - q, q), at] = total
                    sums[at] += total

            sources = phi_at(s - 1, q), phi_at(s - 1, q + 1), phi_at(s - 1, q - 1)
            sweep_layer(*sources, coupling(q), b_at, rows // ROWS, sub, put)


def near_kernel(inner, swapped, ex, geo, p0, w, state, b_in, sums_in, out, sums_out, wb, bb, eh, q_buf):
    wedge = Wedge(True, p0.shape[0])
    ends = SWEEPS - 1
    wedge_couplings(
        wedge, inner, SWEEPS, lambda q: swapped[wedge.sent(q, ends)], ex, geo, wb, bb, eh
    )
    bb[ends] = bb[ends] * b_in[wedge.own(0)]
    sums_out[...] = sums_in[...]
    wedge_sweeps(wedge, inner, p0, w, wb, bb, state, b_in, q_buf, out, sums_out)


def outer_coupling_kernel(inner, outer_eps, far, ex, geo, wb, bb, eh):
    wedge = Wedge(False, ex.shape[0])
    ends = SWEEPS - 1

    def charge(q):
        spot = wedge.sent(q, ends)
        ions = jnp.where(wedge.is_high, inner[2 * SWEEPS + spot], far[spot])
        return drift_charge(ions, geo[6], geo[7], jnp.where(wedge.is_high, wedge.d + 1, wedge.d - 1))

    wedge_couplings(wedge, outer_eps, 0, charge, ex, geo, wb, bb, eh)


def outer_relax_kernel(outer_phi, p0, w, wb, bb_in, state, b_in, sums_in, out, sums_out, bb, q_buf):
    wedge = Wedge(False, p0.shape[0])
    ends = SWEEPS - 1
    for k in range(ends):
        bb[k] = bb_in[k]
    bb[ends] = bb_in[ends] * b_in[wedge.own(0)]
    sums_out[...] = sums_in[...]
    wedge_sweeps(wedge, outer_phi, p0, w, wb, bb, state, b_in, q_buf, out, sums_out)


def local_kernel(near, inner, far, potential, out, run):
    _, band, _ = potential.shape
    tiles = run.shape[0] // ROWS
    run[...] = jnp.zeros_like(run)
    odd = lax.rem(lax.axis_index("drift"), 2) == 1
    base = 0
    for count, value_of in (
        (near.shape[0], lambda k, at: jnp.where(odd, near[k, at], far[k, at])),
        (inner.shape[0], lambda k, at: inner[k, at]),
        (far.shape[0], lambda k, at: jnp.where(odd, far[k, at], near[k, at])),
    ):

        @pl.loop(0, count)
        def _(k, value_of=value_of, base=base):
            for t in range(tiles):
                at = slice(t * ROWS, (t + 1) * ROWS)
                value = value_of(k, at)
                run[at] += value
                if t < band // ROWS:
                    potential[base + k, at] = value

            def put(at, first, second):
                out[0, base + k, at] = first
                out[1, base + k, at] = second

            ratios_of(run, band, put)

        base += count


def ratios_of(field, band, put):
    rows, sector = field.shape
    r, bands = lax.axis_index("radius"), lax.axis_size("radius")
    total_r = band * bands
    sub = lax.broadcasted_iota(jnp.int32, (ROWS, sector), 0)
    lane = lax.broadcasted_iota(jnp.int32, (ROWS, sector), 1)
    scale = 1.0 / (8.0 * 1.09)
    for t, at, x, higher, lower in row_tiles(lambda s: field[s], rows // ROWS, sub):
        if t < band // ROWS:
            row = sub + (t * ROWS + r * band)
            rpos = ((total_r + row).astype(F32) + 0.5) / total_r
            right = jnp.where(lane == sector - 1, 0.0, roll(x, -1, 1))
            left = jnp.where(lane == 0, 0.0, roll(x, 1, 1))
            higher = jnp.where(row == total_r - 1, 0.0, higher)
            lower = jnp.where(row == 0, 0.0, lower)
            er = (lower - higher) * (0.5 * scale)
            ea = (left - right) * (0.5 * scale / rpos)
            put(at, er + 0.3 * ea, ea - 0.3 * er)


def offset_kernel(local, prefix, out, shift, stage, sems):
    layers = local.shape[1]
    copies = []

    def put(at, first, second):
        shift[0, at] = first
        shift[1, at] = second

    ratios_of(prefix, local.shape[2], put)
    parts = sems.shape[0]
    each = layers // parts
    for k in range(parts):
        for c in range(2):
            stage[c, k * each : (k + 1) * each] = local[c, k * each : (k + 1) * each] + shift[c]
        copy = pltpu.make_async_copy(
            stage.at[:, k * each : (k + 1) * each], out.at[:, k * each : (k + 1) * each], sems.at[k]
        )
        copy.start()
        copies.append(copy)
    for copy in copies:
        copy.wait()


def sums_below(sums):
    count, mine = lax.axis_size("drift"), lax.axis_index("drift")
    assert count & (count - 1) == 0
    total, below, step = sums, jnp.zeros_like(sums), 1
    while step < count:
        other = lax.ppermute(total, "drift", [(i, i ^ step) for i in range(count)])
        below = below + jnp.where((mine & step) > 0, other, 0.0)
        total = total + other
        step *= 2
    return below


def kernel(function, out_shape, in_specs, out_specs=None, scratch=(), mb=16):
    return pl.pallas_call(
        function,
        out_shape=out_shape,
        in_specs=in_specs,
        out_specs=out_specs if out_specs is not None else [IN_VMEM] * len(out_shape),
        scratch_shapes=list(scratch),
        compiler_params=pltpu.CompilerParams(vmem_limit_bytes=mb << 20),
    )


def body(ions, potential_guess, permittivity, recombination, rate_index, gap_mask, rate_table):
    layers, band, sector = ions.shape
    depth = SWEEPS
    sides = 1 if lax.axis_size("radius") == 2 else 2
    rows = band + sides * ROWS
    dma = pltpu.SemaphoreType.DMA
    ends = depth - 1
    row_block = 2 * layers + 2 * ends + 2
    far_args = (potential_guess, permittivity, ions, recombination, rate_index, gap_mask, rate_table)
    phi, eps, ions_far, *pad_args = [pltpu.with_memory_space_constraint(x, pltpu.HBM) for x in far_args]

    moved = shifted(ions, "drift", 2)

    def swap_rows(blocks):
        if sides == 1:
            return [lax.ppermute(blocks[0], "radius", [(0, 1), (1, 0)])]
        return [shifted(blocks[0], "radius", -1), shifted(blocks[1], "radius", 1)]

    ion_blocks = kernel(
        ion_rows_kernel,
        [plane(layers // 2, ROWS, sector)] * sides,
        [ANYWHERE],
        scratch=[near(layers, ROWS, sector)] * sides + [dma((sides,))],
        mb=3,
    )(ions_far)
    ion_raws = swap_rows(ion_blocks)
    *blocks, pads = kernel(
        rows_kernel,
        [plane(row_block, ROWS, sector)] * sides + [plane(2, band, sector)],
        [ANYWHERE] * 7,
        scratch=[
            near(band, sector),
            pltpu.VMEM((band, sector), jnp.int32),
            pltpu.VMEM((band, sector), jnp.int32),
            pltpu.SMEM(rate_table.shape, F32),
            dma((4 * sides,)),
            dma((4,)),
        ],
        mb=5,
    )(phi, eps, ions_far, *pad_args)
    raws = swap_rows(blocks)
    rows_moved = [shifted(raw, "drift", 2) for raw in ion_raws]
    to_core, eps_block, phi_block, beyond = kernel(
        functools.partial(halo_kernel, sides),
        [plane(k, rows, sector) for k in (3 * depth - 1, depth, depth, depth - 1)],
        [ANYWHERE] * 3 + [IN_VMEM] * sides,
        scratch=[dma((6 * (1 + sides),))],
        mb=6,
    )(phi, eps, ions_far, *raws)
    count = lax.axis_size("drift")
    assert count % 2 == 0
    partners = [(i, i ^ 1) for i in range(count)]
    chips = [(i, i + 1 if i % 2 else i - 1) for i in range(1, count - 1)]
    outer_eps = lax.ppermute(eps_block, "drift", chips)
    far = lax.ppermute(beyond, "drift", [(i - 3, i) for i in range(4, count, 2)])
    inner = lax.ppermute(to_core, "drift", partners)
    outer_phi = lax.ppermute(phi_block, "drift", chips)

    box = plane(layers, rows, sector)
    p0, ex, w, inv2, geo = kernel(
        functools.partial(inner_coupling_kernel, sides),
        [box, box, plane(6, layers, rows, sector), box, plane(10, rows, sector)],
        [IN_VMEM] * (3 + sides),
        mb=20,
    )(potential_guess, permittivity, pads, *raws)
    p0, ex, w, inv2, geo = [fetched(x) for x in (p0, ex, w, inv2, geo)]
    wedge = plane(depth, rows, sector)
    wedge_box, wedge_couplings_box = near(depth, rows, sector), near(6, depth, rows, sector)
    wb, bb = kernel(
        outer_coupling_kernel,
        [plane(6, depth, rows, sector), wedge],
        [IN_VMEM] * 5,
        scratch=[near(depth + 2, rows, sector)],
        mb=12,
    )(inner, outer_eps, far, ex, geo)
    wb, bb = fetched(wb), fetched(bb)
    raw, swap, b = kernel(
        functools.partial(charge_kernel, sides),
        [box, plane(depth - 1, rows, sector), box],
        [IN_VMEM] * (3 + sides),
        mb=8,
    )(moved, inv2, geo, *rows_moved)
    raw, b = fetched(raw), fetched(b)
    swapped = lax.ppermute(swap, "drift", partners)
    charge, middle, sums, state = kernel(
        inner_relax_kernel,
        [
            plane(layers, band, sector),
            plane(layers - 2 * depth, rows, sector),
            plane(rows, sector),
            plane(2, depth - 1, 2, rows, sector),
        ],
        [IN_VMEM] * 4,
        [ANYWHERE] + [IN_VMEM] * 3,
        scratch=[near(layers, rows, sector)] * 3 + [dma],
        mb=12,
    )(p0, w, b, raw)
    state, sums = fetched(state), fetched(sums)
    near_out, sums = kernel(
        near_kernel,
        [wedge, plane(rows, sector)],
        [IN_VMEM] * 9,
        scratch=[wedge_couplings_box, wedge_box, near(depth + 2, rows, sector), near(depth - 1, depth, rows, sector)],
        mb=12,
    )(inner, swapped, ex, geo, p0, w, state, b, sums)
    far_out, sums = kernel(
        outer_relax_kernel,
        [wedge, plane(rows, sector)],
        [IN_VMEM] * 8,
        scratch=[wedge_box, near(depth - 1, depth, rows, sector)],
        mb=12,
    )(outer_phi, p0, w, wb, bb, state, b, fetched(sums))
    potential, local = kernel(
        local_kernel,
        [plane(layers, band, sector), plane(2, layers, band, sector)],
        [IN_VMEM] * 3,
        scratch=[near(rows, sector)],
        mb=16,
    )(near_out, middle, far_out)
    below_sums = sums_below(sums)
    distortion = kernel(
        offset_kernel,
        plane(2, layers, band, sector),
        [IN_VMEM] * 2,
        ANYWHERE,
        [near(2, band, sector), near(2, layers, band, sector), dma((4,))],
        mb=12,
    )(fetched(local), below_sums)
    return charge, potential, distortion


def solution(mesh):
    return jax.shard_map(
        body,
        mesh=mesh,
        in_specs=(
            P("drift", "radius", None),
            P("drift", "radius", None),
            P("drift", "radius", None),
            P("radius", None),
            P("radius", None),
            P("radius", None),
            P(),
        ),
        out_specs=(
            P("drift", "radius", None),
            P("drift", "radius", None),
            P(None, "drift", "radius", None),
        ),
        check_vma=False,
    )
```

```python
import functools

import jax
import jax.numpy as jnp
from jax import lax
from jax.experimental import pallas as pl
from jax.experimental.pallas import tpu as pltpu
from jax.sharding import PartitionSpec as P

SWEEPS = 4
ROWS = 8
F32 = jnp.float32
IN_VMEM = pl.BlockSpec(memory_space=pltpu.VMEM)
ANYWHERE = pl.BlockSpec(memory_space=pl.ANY)


def plane(*shape):
    return jax.ShapeDtypeStruct(shape, F32)


def near(*shape):
    return pltpu.VMEM(shape, F32)


def fetched(x):
    return pltpu.with_memory_space_constraint(x, pltpu.VMEM)


def shifted(block, axis, distance):
    count = lax.axis_size(axis)
    route = [(i, i + distance) for i in range(count) if 0 <= i + distance < count]
    return lax.ppermute(block, axis, route)


def drift_charge(ions, rec, inj, slab):
    below = 1.0 + rec * ions
    above = jnp.where(slab >= 1, ions + inj * below, 0.0)
    return above / (below + rec * above) + inj


def roll(x, amount, axis):
    return pltpu.roll(x, amount % x.shape[axis], axis)


def row_tiles(load, tiles, sub):
    x = [load(slice(t * ROWS, (t + 1) * ROWS)) for t in range(tiles)]
    up = [roll(v, -1, 0) for v in x]
    down = [roll(v, 1, 0) for v in x]
    for t in range(tiles):
        higher = jnp.where(sub == ROWS - 1, up[(t + 1) % tiles], up[t])
        lower = jnp.where(sub == 0, down[(t - 1) % tiles], down[t])
        yield t, slice(t * ROWS, (t + 1) * ROWS), x[t], higher, lower


def run_all(copies, sems):
    running = [pltpu.make_async_copy(src, dst, sems.at[k]) for k, (src, dst) in enumerate(copies)]
    for copy in running:
        copy.start()
    return running


def sides_of(count, band):
    if count == 1:
        return [pl.multiple_of(jnp.where(lax.axis_index("radius") == 0, band - ROWS, 0), ROWS)]
    return [0, band - ROWS]


def window_rows(sides, band):
    own = [t * ROWS for t in range(band // ROWS)]
    if sides == 1:
        return [*own, jnp.where(lax.axis_index("radius") == 0, band, -ROWS)]
    return [*own, band, -ROWS]


def ion_rows_kernel(ions, *rest):
    sides = (len(rest) - 1) // 2
    blocks, stages, sems = rest[:sides], rest[sides : 2 * sides], rest[-1]
    layers, band, sector = ions.shape
    starts = sides_of(sides, band)
    for copy in run_all([(ions.at[:, pl.ds(start, ROWS)], stage) for start, stage in zip(starts, stages)], sems):
        copy.wait()
    first_half = lax.broadcasted_iota(jnp.int32, (ROWS, sector), 0) < ROWS // 2
    for side, (block, stage) in enumerate(zip(blocks, stages)):
        tail = (lax.axis_index("radius") == 0) if sides == 1 else side == 1
        for j in range(layers // 2):
            one, two = stage[2 * j], stage[2 * j + 1]
            from_tail = jnp.where(first_half, roll(one, ROWS // 2, 0), two)
            from_head = jnp.where(first_half, one, roll(two, ROWS // 2, 0))
            block[j] = jnp.where(tail, from_tail, from_head)


def rows_kernel(phi, eps, ions, rec, index, gap, table, *rest):
    sides = len(rest) - 7
    blocks, pads = rest[:sides], rest[sides]
    rec_v, index_v, gap_v, table_s, sems, pad_sems = rest[sides + 1 :]
    layers, band, sector = phi.shape
    ends = SWEEPS - 1
    starts = sides_of(sides, band)
    copies = []
    for start, block in zip(starts, blocks):
        rows = pl.ds(start, ROWS)
        copies.append((phi.at[:, rows], block.at[0:layers]))
        copies.append((eps.at[:, rows], block.at[layers : 2 * layers]))
        copies.append((ions.at[0:ends, rows], block.at[2 * layers : 2 * layers + ends]))
        copies.append((ions.at[layers - ends :, rows], block.at[2 * layers + ends : 2 * layers + 2 * ends]))
    running = run_all(copies, sems)
    pad_copies = run_all([(rec, rec_v), (index, index_v), (gap, gap_v), (table, table_s)], pad_sems)
    for copy in pad_copies:
        copy.wait()
    for t in range(band // ROWS):
        at = slice(t * ROWS, (t + 1) * ROWS)
        which = index_v[at]
        picked = jnp.zeros((ROWS, sector), F32)
        for k in range(table_s.shape[0]):
            picked = jnp.where(which == k, table_s[k], picked)
        pads[0, at] = rec_v[at]
        pads[1, at] = picked * (1 - gap_v[at]).astype(F32)
    for start, block in zip(starts, blocks):
        for k in range(2):
            block[2 * layers + 2 * ends + k] = pads[k, pl.ds(start, ROWS)]
    for copy in running:
        copy.wait()


def halo_kernel(sides, phi, eps, ions, *refs):
    raws, (inner, outer_eps, outer_phi, far, sems) = refs[:sides], refs[sides:]
    layers, band, _ = phi.shape
    depth = SWEEPS
    odd = lax.rem(lax.axis_index("drift"), 2) == 1
    low, high = 0, layers - depth
    near_at, far_at = jnp.where(odd, low, high), jnp.where(odd, high, low)
    ends = 2 * layers
    copies = []
    for dst, at, k, start, raw_at, count in (
        (inner, 0, 0, near_at, near_at, depth),
        (inner, depth, 1, near_at, layers + near_at, depth),
        (inner, 2 * depth, 2, 0, ends, depth - 1),
        (far, 0, 2, layers - depth + 1, ends + depth - 1, depth - 1),
    ):
        src = (phi, eps, ions)[k]
        copies.append((src.at[pl.ds(start, count)], dst.at[at : at + count, 0:band]))
        for side, raw in enumerate(raws):
            rows = slice(band + side * ROWS, band + (side + 1) * ROWS)
            copies.append((raw.at[pl.ds(raw_at, count)], dst.at[at : at + count, rows]))
    for dst, src in ((outer_eps, eps), (outer_phi, phi)):
        for k in range(depth):
            copies.append((src.at[far_at + k], dst.at[k * band : (k + 1) * band]))
    running = run_all(copies, sems)
    sector = phi.shape[2]
    first_half = lax.broadcasted_iota(jnp.int32, (ROWS, sector), 0) < ROWS // 2
    for side, raw in enumerate(raws):
        above = (lax.axis_index("radius") == 0) if sides == 1 else side == 0
        for dst, base in ((outer_eps, layers), (outer_phi, 0)):
            for j in range(depth // 2):
                one, two = raw[base + far_at + 2 * j], raw[base + far_at + 2 * j + 1]
                from_above = jnp.where(first_half, one, roll(two, ROWS // 2, 0))
                from_below = jnp.where(first_half, roll(one, ROWS // 2, 0), two)
                at = depth * band + (side * (depth // 2) + j) * ROWS
                dst[at : at + ROWS] = jnp.where(above, from_above, from_below)
    for copy in running:
        copy.wait()


def unpack_halo(packed, halo, band):
    depth = SWEEPS
    sides = (halo.shape[1] - band) // ROWS
    for k in range(depth):
        halo[k, 0:band] = packed[k * band : (k + 1) * band]
        for side in range(sides):
            above = (lax.axis_index("radius") == 0) if sides == 1 else side == 0
            at = depth * band + (side * (depth // 2) + k // 2) * ROWS
            two = packed[at : at + ROWS]
            turned = roll(two, ROWS // 2, 0)
            rows = slice(band + side * ROWS, band + (side + 1) * ROWS)
            halo[k, rows] = jnp.where(above, two, turned) if k % 2 == 0 else jnp.where(above, turned, two)


def coupling_rows(z, ex, z_up, z_down, geo, alive, tiles, sub, put):
    for t, at, e, e_up, e_down in row_tiles(lambda s: ex(z, s), tiles, sub):
        not_last, not_first = geo[4, at], geo[5, at]
        right, left = roll(e, -1, 1), roll(e, 1, 1)
        inv_r2 = geo[2, at]
        zu = e + ex(z_up, at)
        zd = e + ex(z_down, at)
        has_up, has_down = geo[8, at], geo[9, at]
        ru = (e + e_up * has_up) * geo[0, at]
        rd = (e + e_down * has_down) * geo[1, at]
        au = (e + right * not_last) * inv_r2
        ad = (e + left * not_first) * inv_r2
        diag = ((zu + zd) + (ru + rd)) + (au + ad)
        inv = jnp.where(geo[3, at] * alive > 0, 1.0 / diag, 0.0)
        radials = (ru * inv * has_up, rd * inv * has_down)
        put(at, (zu * inv, zd * inv, *radials, au * inv * not_last, ad * inv * not_first), inv + inv)


def inner_coupling_kernel(sides, phi, eps, pads, *refs):
    raws, (p0, ex, w, inv2, geo) = refs[:sides], refs[sides:]
    layers, band, sector = phi.shape
    tiles = p0.shape[1] // ROWS
    r, bands = lax.axis_index("radius"), lax.axis_size("radius")
    total_r = band * bands
    sub = lax.broadcasted_iota(jnp.int32, (ROWS, sector), 0)
    lane = lax.broadcasted_iota(jnp.int32, (ROWS, sector), 1)
    half = 0.5 / total_r

    for t, first in enumerate(window_rows(sides, band)):
        at = slice(t * ROWS, (t + 1) * ROWS)
        row = sub + (r * band + first)
        rpos = ((total_r + row).astype(F32) + 0.5) / total_r
        geo[0, at] = (rpos + half) / rpos
        geo[1, at] = (rpos - half) / rpos
        geo[2, at] = 1.0 / (rpos * rpos)
        geo[3, at] = jnp.where((row >= 0) & (row < total_r), 1.0, 0.0)
        geo[4, at] = jnp.where(lane == sector - 1, 0.0, 1.0)
        geo[5, at] = jnp.where(lane == 0, 0.0, 1.0)
        geo[8, at] = jnp.where(row == total_r - 1, 0.0, 1.0)
        geo[9, at] = jnp.where(row == 0, 0.0, 1.0)
    first_pads = 2 * layers + 2 * (SWEEPS - 1)
    for k in range(2):
        geo[6 + k, 0:band] = pads[k]
        for side, raw in enumerate(raws):
            geo[6 + k, band + side * ROWS : band + (side + 1) * ROWS] = raw[first_pads + k]

    @pl.loop(0, layers)
    def _(z):
        for dst, src, base in ((p0, phi, 0), (ex, eps, layers)):
            dst[z, 0:band] = src[z]
            for side, raw in enumerate(raws):
                dst[z, band + side * ROWS : band + (side + 1) * ROWS] = raw[base + z]

    @pl.loop(1, layers - 1)
    def _(z):
        def put(at, values, twice):
            for k, value in enumerate(values):
                w[k, z, at] = value
            inv2[z, at] = twice

        coupling_rows(z, lambda i, s: ex[i, s], z + 1, z - 1, geo, 1.0, tiles, sub, put)


def sweep_layer(src, src_up, src_down, w, b, tiles, sub, put):
    for t, at, p, p_up, p_down in row_tiles(src, tiles, sub):
        right, left = roll(p, -1, 1), roll(p, 1, 1)
        total = b(at) + (w(0, at) * src_up(at) + w(1, at) * src_down(at))
        total = total + (w(2, at) * p_up + w(3, at) * p_down)
        total = total + (w(4, at) * right + w(5, at) * left)
        put(at, total)


def charge_kernel(sides, moved, inv2, geo, *refs):
    rows_moved = refs[:sides]
    raw, swap, b = refs[sides:]
    layers, band, _ = moved.shape
    ends = SWEEPS - 1
    d = lax.axis_index("drift")

    @pl.loop(0, layers // 2)
    def _(j):
        for half in range(2):
            z = 2 * j + half
            inside = (z > 0) & (z < layers - 1)

            def put(at, ions, z=z, inside=inside):
                value = drift_charge(ions, geo[6, at], geo[7, at], d)
                raw[z, at] = value
                b[z, at] = jnp.where(inside, value * inv2[z, at], value)

            put(slice(0, band), moved[z])
            for side, packed in enumerate(rows_moved):
                above = (lax.axis_index("radius") == 0) if sides == 1 else side == 0
                two = packed[j]
                turned = roll(two, ROWS // 2, 0)
                ions = jnp.where(above, two, turned) if half == 0 else jnp.where(above, turned, two)
                put(slice(band + side * ROWS, band + (side + 1) * ROWS), ions)

    odd = lax.rem(d, 2) == 1
    for k in range(ends):
        swap[k] = raw[jnp.where(odd, k, layers - ends + k)]


def inner_relax_kernel(p0, w, b, raw, charge_out, window_out, sums_out, state, p1, p2, p3, sem):
    layers, rows, sector = p0.shape
    charge_copy = pltpu.make_async_copy(raw.at[:, 0 : charge_out.shape[1]], charge_out, sem)
    charge_copy.start()
    depth = SWEEPS
    tiles = rows // ROWS
    sub = lax.broadcasted_iota(jnp.int32, (ROWS, sector), 0)
    phis = (p0, p1, p2, p3)
    sums_out[...] = jnp.zeros_like(sums_out)
    for s in range(1, depth + 1):
        src = phis[s - 1]
        for z in range(s, layers - s):

            def put(at, total, s=s, z=z):
                if s < depth:
                    phis[s][z, at] = total
                    if z - s < 2:
                        state[0, s - 1, z - s, at] = total
                    if z - (layers - s - 2) >= 0:
                        state[1, s - 1, z - (layers - s - 2), at] = total
                else:
                    window_out[z - depth, at] = total
                    sums_out[at] += total

            sweep_layer(
                lambda at, z=z, src=src: src[z, at],
                lambda at, z=z, src=src: src[z + 1, at],
                lambda at, z=z, src=src: src[z - 1, at],
                lambda k, at, z=z: w[k, z, at],
                lambda at, z=z: b[z, at],
                tiles,
                sub,
                put,
            )
    charge_copy.wait()


class Wedge:
    def __init__(self, near, layers):
        d = lax.axis_index("drift")
        odd = lax.rem(d, 2)
        self.n, self.d = layers, d
        self.high = (1 - odd) if near else odd
        self.is_high = self.high == 1

    def own(self, q):
        return jnp.where(self.is_high, self.n - 1 - q, q)

    def sent(self, q, count):
        return jnp.where(self.is_high, -q - 1, count + q)

    def alive(self, q):
        z = self.d * self.n + self.own(q)
        return jnp.where((z >= 0) & (z < lax.axis_size("drift") * self.n), 1.0, 0.0)


def wedge_couplings(wedge, halo, halo_at, charge, ex, geo, wb, bb, eh):
    depth = SWEEPS
    rows, sector = eh.shape[1:]
    sub = lax.broadcasted_iota(jnp.int32, (ROWS, sector), 0)
    for q in range(-depth, 2):
        eh[depth + q] = halo[halo_at + wedge.sent(q, depth)] if q < 0 else ex[wedge.own(q)]
    for k in range(depth):
        q = k + 1 - depth
        bb[k] = charge(q) if q < 0 else jnp.ones_like(bb[0])

        def put(at, values, twice, k=k):
            for j, value in enumerate(values):
                wb[j, k, at] = value
            bb[k, at] = bb[k, at] * twice

        coupling_rows(
            k + 1, lambda i, at: eh[i, at], k + 2, k, geo, wedge.alive(q), rows // ROWS, sub, put
        )


def wedge_sweeps(wedge, halo, p0, w, wb, bb, state, b_in, q_buf, out, sums):
    depth = SWEEPS
    rows, sector = p0.shape[1:]
    sub = lax.broadcasted_iota(jnp.int32, (ROWS, sector), 0)

    def phi_at(s, q):
        if s == 0:
            if q < 0:
                spot = wedge.sent(q, depth)
                return lambda at: halo[spot, at]
            spot = wedge.own(q)
            return lambda at: p0[spot, at]
        if q >= s:
            spot = jnp.where(wedge.is_high, 1 - (q - s), q - s)
            return lambda at: state[wedge.high, s - 1, spot, at]
        return lambda at: q_buf[s - 1, q - s + depth, at]

    def coupling(q):
        if q <= 0:
            return lambda j, at: wb[j, q + depth - 1, at]
        z = wedge.own(q)
        inward, outward = wedge.high, 1 - wedge.high
        return lambda j, at: w[(inward, outward, 2, 3, 4, 5)[j], z, at]

    for s in range(1, depth + 1):
        for q in range(s - depth, s):
            if q <= 0:
                b_at = lambda at, q=q: bb[q + depth - 1, at]
            else:
                b_at = lambda at, z=wedge.own(q): b_in[z, at]

            def put(at, total, s=s, q=q):
                if s < depth:
                    q_buf[s - 1, q - s + depth, at] = total
                else:
                    out[jnp.where(wedge.is_high, depth - 1 - q, q), at] = total
                    sums[at] += total

            sources = phi_at(s - 1, q), phi_at(s - 1, q + 1), phi_at(s - 1, q - 1)
            sweep_layer(*sources, coupling(q), b_at, rows // ROWS, sub, put)


def near_kernel(inner, swapped, ex, geo, p0, w, state, b_in, sums_in, out, sums_out, wb, bb, eh, q_buf):
    wedge = Wedge(True, p0.shape[0])
    ends = SWEEPS - 1
    wedge_couplings(
        wedge, inner, SWEEPS, lambda q: swapped[wedge.sent(q, ends)], ex, geo, wb, bb, eh
    )
    bb[ends] = bb[ends] * b_in[wedge.own(0)]
    sums_out[...] = sums_in[...]
    wedge_sweeps(wedge, inner, p0, w, wb, bb, state, b_in, q_buf, out, sums_out)


def outer_coupling_kernel(band, inner, outer_eps, far, ex, geo, wb, bb, eh, halo):
    wedge = Wedge(False, ex.shape[0])
    ends = SWEEPS - 1

    def charge(q):
        spot = wedge.sent(q, ends)
        ions = jnp.where(wedge.is_high, inner[2 * SWEEPS + spot], far[spot])
        return drift_charge(ions, geo[6], geo[7], jnp.where(wedge.is_high, wedge.d + 1, wedge.d - 1))

    unpack_halo(outer_eps, halo, band)
    wedge_couplings(wedge, halo, 0, charge, ex, geo, wb, bb, eh)


def outer_relax_kernel(band, outer_phi, p0, w, wb, bb_in, state, b_in, sums_in, out, sums_out, bb, q_buf, halo):
    wedge = Wedge(False, p0.shape[0])
    ends = SWEEPS - 1
    for k in range(ends):
        bb[k] = bb_in[k]
    bb[ends] = bb_in[ends] * b_in[wedge.own(0)]
    sums_out[...] = sums_in[...]
    unpack_halo(outer_phi, halo, band)
    wedge_sweeps(wedge, halo, p0, w, wb, bb, state, b_in, q_buf, out, sums_out)


def local_kernel(near, inner, far, potential, out, run):
    _, band, _ = potential.shape
    tiles = run.shape[0] // ROWS
    run[...] = jnp.zeros_like(run)
    odd = lax.rem(lax.axis_index("drift"), 2) == 1
    base = 0
    for count, value_of in (
        (near.shape[0], lambda k, at: jnp.where(odd, near[k, at], far[k, at])),
        (inner.shape[0], lambda k, at: inner[k, at]),
        (far.shape[0], lambda k, at: jnp.where(odd, far[k, at], near[k, at])),
    ):

        @pl.loop(0, count)
        def _(k, value_of=value_of, base=base):
            for t in range(tiles):
                at = slice(t * ROWS, (t + 1) * ROWS)
                value = value_of(k, at)
                run[at] += value
                if t < band // ROWS:
                    potential[base + k, at] = value

            def put(at, first, second):
                out[0, base + k, at] = first
                out[1, base + k, at] = second

            ratios_of(run, band, put)

        base += count


def ratios_of(field, band, put):
    rows, sector = field.shape
    r, bands = lax.axis_index("radius"), lax.axis_size("radius")
    total_r = band * bands
    sub = lax.broadcasted_iota(jnp.int32, (ROWS, sector), 0)
    lane = lax.broadcasted_iota(jnp.int32, (ROWS, sector), 1)
    scale = 1.0 / (8.0 * 1.09)
    for t, at, x, higher, lower in row_tiles(lambda s: field[s], rows // ROWS, sub):
        if t < band // ROWS:
            row = sub + (t * ROWS + r * band)
            rpos = ((total_r + row).astype(F32) + 0.5) / total_r
            right = jnp.where(lane == sector - 1, 0.0, roll(x, -1, 1))
            left = jnp.where(lane == 0, 0.0, roll(x, 1, 1))
            higher = jnp.where(row == total_r - 1, 0.0, higher)
            lower = jnp.where(row == 0, 0.0, lower)
            er = (lower - higher) * (0.5 * scale)
            ea = (left - right) * (0.5 * scale / rpos)
            put(at, er + 0.3 * ea, ea - 0.3 * er)


def offset_kernel(local, prefix, out, shift, stage, sems):
    layers = local.shape[1]
    copies = []

    def put(at, first, second):
        shift[0, at] = first
        shift[1, at] = second

    ratios_of(prefix, local.shape[2], put)
    parts = sems.shape[0]
    each = layers // parts
    for k in range(parts):
        for c in range(2):
            stage[c, k * each : (k + 1) * each] = local[c, k * each : (k + 1) * each] + shift[c]
        copy = pltpu.make_async_copy(
            stage.at[:, k * each : (k + 1) * each], out.at[:, k * each : (k + 1) * each], sems.at[k]
        )
        copy.start()
        copies.append(copy)
    for copy in copies:
        copy.wait()


def sums_below(sums):
    count, mine = lax.axis_size("drift"), lax.axis_index("drift")
    assert count & (count - 1) == 0
    total, below, step = sums, jnp.zeros_like(sums), 1
    while step < count:
        other = lax.ppermute(total, "drift", [(i, i ^ step) for i in range(count)])
        below = below + jnp.where((mine & step) > 0, other, 0.0)
        total = total + other
        step *= 2
    return below


def kernel(function, out_shape, in_specs, out_specs=None, scratch=(), mb=16):
    return pl.pallas_call(
        function,
        out_shape=out_shape,
        in_specs=in_specs,
        out_specs=out_specs if out_specs is not None else [IN_VMEM] * len(out_shape),
        scratch_shapes=list(scratch),
        compiler_params=pltpu.CompilerParams(vmem_limit_bytes=mb << 20),
    )


def body(ions, potential_guess, permittivity, recombination, rate_index, gap_mask, rate_table):
    layers, band, sector = ions.shape
    depth = SWEEPS
    sides = 1 if lax.axis_size("radius") == 2 else 2
    rows = band + sides * ROWS
    dma = pltpu.SemaphoreType.DMA
    ends = depth - 1
    row_block = 2 * layers + 2 * ends + 2
    far_args = (potential_guess, permittivity, ions, recombination, rate_index, gap_mask, rate_table)
    phi, eps, ions_far, *pad_args = [pltpu.with_memory_space_constraint(x, pltpu.HBM) for x in far_args]

    moved = shifted(ions, "drift", 2)

    def swap_rows(blocks):
        if sides == 1:
            return [lax.ppermute(blocks[0], "radius", [(0, 1), (1, 0)])]
        return [shifted(blocks[0], "radius", -1), shifted(blocks[1], "radius", 1)]

    ion_blocks = kernel(
        ion_rows_kernel,
        [plane(layers // 2, ROWS, sector)] * sides,
        [ANYWHERE],
        scratch=[near(layers, ROWS, sector)] * sides + [dma((sides,))],
        mb=3,
    )(ions_far)
    ion_raws = swap_rows(ion_blocks)
    *blocks, pads = kernel(
        rows_kernel,
        [plane(row_block, ROWS, sector)] * sides + [plane(2, band, sector)],
        [ANYWHERE] * 7,
        scratch=[
            near(band, sector),
            pltpu.VMEM((band, sector), jnp.int32),
            pltpu.VMEM((band, sector), jnp.int32),
            pltpu.SMEM(rate_table.shape, F32),
            dma((4 * sides,)),
            dma((4,)),
        ],
        mb=5,
    )(phi, eps, ions_far, *pad_args)
    raws = swap_rows(blocks)
    rows_moved = [shifted(raw, "drift", 2) for raw in ion_raws]
    packed = depth * band + sides * (depth // 2) * ROWS
    to_core, eps_block, phi_block, beyond = kernel(
        functools.partial(halo_kernel, sides),
        [
            plane(3 * depth - 1, rows, sector),
            plane(packed, sector),
            plane(packed, sector),
            plane(depth - 1, rows, sector),
        ],
        [ANYWHERE] * 3 + [IN_VMEM] * sides,
        scratch=[dma((4 * (1 + sides) + 2 * depth,))],
        mb=6,
    )(phi, eps, ions_far, *raws)
    count = lax.axis_size("drift")
    assert count % 2 == 0
    partners = [(i, i ^ 1) for i in range(count)]
    chips = [(i, i + 1 if i % 2 else i - 1) for i in range(1, count - 1)]
    outer_eps = lax.ppermute(eps_block, "drift", chips)
    far = lax.ppermute(beyond, "drift", [(i - 3, i) for i in range(4, count, 2)])
    inner = lax.ppermute(to_core, "drift", partners)
    outer_phi = lax.ppermute(phi_block, "drift", chips)

    box = plane(layers, rows, sector)
    p0, ex, w, inv2, geo = kernel(
        functools.partial(inner_coupling_kernel, sides),
        [box, box, plane(6, layers, rows, sector), box, plane(10, rows, sector)],
        [IN_VMEM] * (3 + sides),
        mb=20,
    )(potential_guess, permittivity, pads, *raws)
    p0, ex, w, inv2, geo = [fetched(x) for x in (p0, ex, w, inv2, geo)]
    wedge = plane(depth, rows, sector)
    wedge_box, wedge_couplings_box = near(depth, rows, sector), near(6, depth, rows, sector)
    wb, bb = kernel(
        functools.partial(outer_coupling_kernel, band),
        [plane(6, depth, rows, sector), wedge],
        [IN_VMEM] * 5,
        scratch=[near(depth + 2, rows, sector), wedge_box],
        mb=12,
    )(inner, outer_eps, far, ex, geo)
    wb, bb = fetched(wb), fetched(bb)
    raw, swap, b = kernel(
        functools.partial(charge_kernel, sides),
        [box, plane(depth - 1, rows, sector), box],
        [IN_VMEM] * (3 + sides),
        mb=8,
    )(moved, inv2, geo, *rows_moved)
    raw, b = fetched(raw), fetched(b)
    swapped = lax.ppermute(swap, "drift", partners)
    charge, middle, sums, state = kernel(
        inner_relax_kernel,
        [
            plane(layers, band, sector),
            plane(layers - 2 * depth, rows, sector),
            plane(rows, sector),
            plane(2, depth - 1, 2, rows, sector),
        ],
        [IN_VMEM] * 4,
        [ANYWHERE] + [IN_VMEM] * 3,
        scratch=[near(layers, rows, sector)] * 3 + [dma],
        mb=12,
    )(p0, w, b, raw)
    state, sums = fetched(state), fetched(sums)
    near_out, sums = kernel(
        near_kernel,
        [wedge, plane(rows, sector)],
        [IN_VMEM] * 9,
        scratch=[wedge_couplings_box, wedge_box, near(depth + 2, rows, sector), near(depth - 1, depth, rows, sector)],
        mb=12,
    )(inner, swapped, ex, geo, p0, w, state, b, sums)
    far_out, sums = kernel(
        functools.partial(outer_relax_kernel, band),
        [wedge, plane(rows, sector)],
        [IN_VMEM] * 8,
        scratch=[wedge_box, near(depth - 1, depth, rows, sector), wedge_box],
        mb=12,
    )(outer_phi, p0, w, wb, bb, state, b, fetched(sums))
    potential, local = kernel(
        local_kernel,
        [plane(layers, band, sector), plane(2, layers, band, sector)],
        [IN_VMEM] * 3,
        scratch=[near(rows, sector)],
        mb=16,
    )(near_out, middle, far_out)
    below_sums = sums_below(sums)
    distortion = kernel(
        offset_kernel,
        plane(2, layers, band, sector),
        [IN_VMEM] * 2,
        ANYWHERE,
        [near(2, band, sector), near(2, layers, band, sector), dma((4,))],
        mb=12,
    )(fetched(local), below_sums)
    return charge, potential, distortion


def solution(mesh):
    return jax.shard_map(
        body,
        mesh=mesh,
        in_specs=(
            P("drift", "radius", None),
            P("drift", "radius", None),
            P("drift", "radius", None),
            P("radius", None),
            P("radius", None),
            P("radius", None),
            P(),
        ),
        out_specs=(
            P("drift", "radius", None),
            P("drift", "radius", None),
            P(None, "drift", "radius", None),
        ),
        check_vma=False,
    )
```

```python
import functools

import jax
import jax.numpy as jnp
from jax import lax
from jax.experimental import pallas as pl
from jax.experimental.pallas import tpu as pltpu
from jax.sharding import PartitionSpec as P

SWEEPS = 4
ROWS = 8
F32 = jnp.float32
IN_VMEM = pl.BlockSpec(memory_space=pltpu.VMEM)
ANYWHERE = pl.BlockSpec(memory_space=pl.ANY)


def plane(*shape):
    return jax.ShapeDtypeStruct(shape, F32)


def near(*shape):
    return pltpu.VMEM(shape, F32)


def fetched(x):
    return pltpu.with_memory_space_constraint(x, pltpu.VMEM)


def shifted(block, axis, distance):
    count = lax.axis_size(axis)
    route = [(i, i + distance) for i in range(count) if 0 <= i + distance < count]
    return lax.ppermute(block, axis, route)


def drift_charge(ions, rec, inj, slab):
    below = 1.0 + rec * ions
    above = jnp.where(slab >= 1, ions + inj * below, 0.0)
    return above / (below + rec * above) + inj


def roll(x, amount, axis):
    return pltpu.roll(x, amount % x.shape[axis], axis)


def row_tiles(load, tiles, sub):
    x = [load(slice(t * ROWS, (t + 1) * ROWS)) for t in range(tiles)]
    up = [roll(v, -1, 0) for v in x]
    down = [roll(v, 1, 0) for v in x]
    for t in range(tiles):
        higher = jnp.where(sub == ROWS - 1, up[(t + 1) % tiles], up[t])
        lower = jnp.where(sub == 0, down[(t - 1) % tiles], down[t])
        yield t, slice(t * ROWS, (t + 1) * ROWS), x[t], higher, lower


def run_all(copies, sems):
    running = [pltpu.make_async_copy(src, dst, sems.at[k]) for k, (src, dst) in enumerate(copies)]
    for copy in running:
        copy.start()
    return running


def sides_of(count, band):
    if count == 1:
        return [pl.multiple_of(jnp.where(lax.axis_index("radius") == 0, band - ROWS, 0), ROWS)]
    return [0, band - ROWS]


def window_rows(sides, band):
    own = [t * ROWS for t in range(band // ROWS)]
    if sides == 1:
        return [*own, jnp.where(lax.axis_index("radius") == 0, band, -ROWS)]
    return [*own, band, -ROWS]


def ion_rows_kernel(ions, *rest):
    sides = (len(rest) - 1) // 2
    blocks, stages, sems = rest[:sides], rest[sides : 2 * sides], rest[-1]
    layers, band, sector = ions.shape
    starts = sides_of(sides, band)
    for copy in run_all([(ions.at[:, pl.ds(start, ROWS)], stage) for start, stage in zip(starts, stages)], sems):
        copy.wait()
    first_half = lax.broadcasted_iota(jnp.int32, (ROWS, sector), 0) < ROWS // 2
    for side, (block, stage) in enumerate(zip(blocks, stages)):
        tail = (lax.axis_index("radius") == 0) if sides == 1 else side == 1
        for j in range(layers // 2):
            one, two = stage[2 * j], stage[2 * j + 1]
            from_tail = jnp.where(first_half, roll(one, ROWS // 2, 0), two)
            from_head = jnp.where(first_half, one, roll(two, ROWS // 2, 0))
            block[j] = jnp.where(tail, from_tail, from_head)


def rows_kernel(phi, eps, ions, rec, index, gap, table, *rest):
    sides = len(rest) - 7
    blocks, pads = rest[:sides], rest[sides]
    rec_v, index_v, gap_v, table_s, sems, pad_sems = rest[sides + 1 :]
    layers, band, sector = phi.shape
    ends = SWEEPS - 1
    starts = sides_of(sides, band)
    copies = []
    for start, block in zip(starts, blocks):
        rows = pl.ds(start, ROWS)
        copies.append((phi.at[:, rows], block.at[0:layers]))
        copies.append((eps.at[:, rows], block.at[layers : 2 * layers]))
        copies.append((ions.at[0:ends, rows], block.at[2 * layers : 2 * layers + ends]))
        copies.append((ions.at[layers - ends :, rows], block.at[2 * layers + ends : 2 * layers + 2 * ends]))
    running = run_all(copies, sems)
    pad_copies = run_all([(rec, rec_v), (index, index_v), (gap, gap_v), (table, table_s)], pad_sems)
    for copy in pad_copies:
        copy.wait()
    for t in range(band // ROWS):
        at = slice(t * ROWS, (t + 1) * ROWS)
        which = index_v[at]
        picked = jnp.zeros((ROWS, sector), F32)
        for k in range(table_s.shape[0]):
            picked = jnp.where(which == k, table_s[k], picked)
        pads[0, at] = rec_v[at]
        pads[1, at] = picked * (1 - gap_v[at]).astype(F32)
    for start, block in zip(starts, blocks):
        for k in range(2):
            block[2 * layers + 2 * ends + k] = pads[k, pl.ds(start, ROWS)]
    for copy in running:
        copy.wait()


def halo_kernel(sides, phi, eps, ions, *refs):
    raws, (inner, outer_eps, outer_phi, far, sems) = refs[:sides], refs[sides:]
    layers, band, _ = phi.shape
    depth = SWEEPS
    odd = lax.rem(lax.axis_index("drift"), 2) == 1
    low, high = 0, layers - depth
    near_at, far_at = jnp.where(odd, low, high), jnp.where(odd, high, low)
    ends = 2 * layers
    copies = []
    for dst, at, k, start, raw_at, count in (
        (inner, 0, 0, near_at, near_at, depth),
        (inner, depth, 1, near_at, layers + near_at, depth),
        (inner, 2 * depth, 2, 0, ends, depth - 1),
        (far, 0, 2, layers - depth + 1, ends + depth - 1, depth - 1),
    ):
        src = (phi, eps, ions)[k]
        copies.append((src.at[pl.ds(start, count)], dst.at[at : at + count, 0:band]))
        for side, raw in enumerate(raws):
            rows = slice(band + side * ROWS, band + (side + 1) * ROWS)
            copies.append((raw.at[pl.ds(raw_at, count)], dst.at[at : at + count, rows]))
    for dst, src in ((outer_eps, eps), (outer_phi, phi)):
        for k in range(depth):
            copies.append((src.at[far_at + k], dst.at[k * band : (k + 1) * band]))
    running = run_all(copies, sems)
    sector = phi.shape[2]
    first_half = lax.broadcasted_iota(jnp.int32, (ROWS, sector), 0) < ROWS // 2
    for side, raw in enumerate(raws):
        above = (lax.axis_index("radius") == 0) if sides == 1 else side == 0
        for dst, base in ((outer_eps, layers), (outer_phi, 0)):
            for j in range(depth // 2):
                one, two = raw[base + far_at + 2 * j], raw[base + far_at + 2 * j + 1]
                from_above = jnp.where(first_half, one, roll(two, ROWS // 2, 0))
                from_below = jnp.where(first_half, roll(one, ROWS // 2, 0), two)
                at = depth * band + (side * (depth // 2) + j) * ROWS
                dst[at : at + ROWS] = jnp.where(above, from_above, from_below)
    for copy in running:
        copy.wait()


def unpack_halo(packed, halo, band):
    depth = SWEEPS
    sides = (halo.shape[1] - band) // ROWS
    for k in range(depth):
        halo[k, 0:band] = packed[k * band : (k + 1) * band]
        for side in range(sides):
            above = (lax.axis_index("radius") == 0) if sides == 1 else side == 0
            at = depth * band + (side * (depth // 2) + k // 2) * ROWS
            two = packed[at : at + ROWS]
            turned = roll(two, ROWS // 2, 0)
            rows = slice(band + side * ROWS, band + (side + 1) * ROWS)
            halo[k, rows] = jnp.where(above, two, turned) if k % 2 == 0 else jnp.where(above, turned, two)


def coupling_rows(z, ex, z_up, z_down, geo, alive, tiles, sub, put):
    for t, at, e, e_up, e_down in row_tiles(lambda s: ex(z, s), tiles, sub):
        not_last, not_first = geo[4, at], geo[5, at]
        right, left = roll(e, -1, 1), roll(e, 1, 1)
        inv_r2 = geo[2, at]
        zu = e + ex(z_up, at)
        zd = e + ex(z_down, at)
        has_up, has_down = geo[8, at], geo[9, at]
        ru = (e + e_up * has_up) * geo[0, at]
        rd = (e + e_down * has_down) * geo[1, at]
        au = (e + right * not_last) * inv_r2
        ad = (e + left * not_first) * inv_r2
        diag = ((zu + zd) + (ru + rd)) + (au + ad)
        inv = jnp.where(geo[3, at] * alive > 0, 1.0 / diag, 0.0)
        radials = (ru * inv * has_up, rd * inv * has_down)
        put(at, (zu * inv, zd * inv, *radials, au * inv * not_last, ad * inv * not_first), inv + inv)


def inner_coupling_kernel(sides, phi, eps, pads, *refs):
    raws, (p0, ex, w, inv2, geo) = refs[:sides], refs[sides:]
    layers, band, sector = phi.shape
    tiles = p0.shape[1] // ROWS
    r, bands = lax.axis_index("radius"), lax.axis_size("radius")
    total_r = band * bands
    sub = lax.broadcasted_iota(jnp.int32, (ROWS, sector), 0)
    lane = lax.broadcasted_iota(jnp.int32, (ROWS, sector), 1)
    half = 0.5 / total_r

    for t, first in enumerate(window_rows(sides, band)):
        at = slice(t * ROWS, (t + 1) * ROWS)
        row = sub + (r * band + first)
        rpos = ((total_r + row).astype(F32) + 0.5) / total_r
        geo[0, at] = (rpos + half) / rpos
        geo[1, at] = (rpos - half) / rpos
        geo[2, at] = 1.0 / (rpos * rpos)
        geo[3, at] = jnp.where((row >= 0) & (row < total_r), 1.0, 0.0)
        geo[4, at] = jnp.where(lane == sector - 1, 0.0, 1.0)
        geo[5, at] = jnp.where(lane == 0, 0.0, 1.0)
        geo[8, at] = jnp.where(row == total_r - 1, 0.0, 1.0)
        geo[9, at] = jnp.where(row == 0, 0.0, 1.0)
    first_pads = 2 * layers + 2 * (SWEEPS - 1)
    for k in range(2):
        geo[6 + k, 0:band] = pads[k]
        for side, raw in enumerate(raws):
            geo[6 + k, band + side * ROWS : band + (side + 1) * ROWS] = raw[first_pads + k]

    @pl.loop(0, layers)
    def _(z):
        for dst, src, base in ((p0, phi, 0), (ex, eps, layers)):
            dst[z, 0:band] = src[z]
            for side, raw in enumerate(raws):
                dst[z, band + side * ROWS : band + (side + 1) * ROWS] = raw[base + z]

    @pl.loop(1, layers - 1)
    def _(z):
        def put(at, values, twice):
            for k, value in enumerate(values):
                w[k, z, at] = value
            inv2[z, at] = twice

        coupling_rows(z, lambda i, s: ex[i, s], z + 1, z - 1, geo, 1.0, tiles, sub, put)


def sweep_layer(src, src_up, src_down, w, b, tiles, sub, put):
    for t, at, p, p_up, p_down in row_tiles(src, tiles, sub):
        right, left = roll(p, -1, 1), roll(p, 1, 1)
        total = b(at) + (w(0, at) * src_up(at) + w(1, at) * src_down(at))
        total = total + (w(2, at) * p_up + w(3, at) * p_down)
        total = total + (w(4, at) * right + w(5, at) * left)
        put(at, total)


def charge_kernel(sides, moved, inv2, geo, *refs):
    rows_moved = refs[:sides]
    raw, swap, b = refs[sides:]
    layers, band, _ = moved.shape
    ends = SWEEPS - 1
    d = lax.axis_index("drift")

    @pl.loop(0, layers // 2)
    def _(j):
        for half in range(2):
            z = 2 * j + half
            inside = (z > 0) & (z < layers - 1)

            def put(at, ions, z=z, inside=inside):
                value = drift_charge(ions, geo[6, at], geo[7, at], d)
                raw[z, at] = value
                b[z, at] = jnp.where(inside, value * inv2[z, at], value)

            put(slice(0, band), moved[z])
            for side, packed in enumerate(rows_moved):
                above = (lax.axis_index("radius") == 0) if sides == 1 else side == 0
                two = packed[j]
                turned = roll(two, ROWS // 2, 0)
                ions = jnp.where(above, two, turned) if half == 0 else jnp.where(above, turned, two)
                put(slice(band + side * ROWS, band + (side + 1) * ROWS), ions)

    odd = lax.rem(d, 2) == 1
    for k in range(ends):
        swap[k] = raw[jnp.where(odd, k, layers - ends + k)]


def inner_relax_kernel(p0, w, b, raw, charge_out, window_out, sums_out, state, p1, p2, p3, sem):
    layers, rows, sector = p0.shape
    charge_copy = pltpu.make_async_copy(raw.at[:, 0 : charge_out.shape[1]], charge_out, sem)
    charge_copy.start()
    depth = SWEEPS
    tiles = rows // ROWS
    sub = lax.broadcasted_iota(jnp.int32, (ROWS, sector), 0)
    phis = (p0, p1, p2, p3)
    sums_out[...] = jnp.zeros_like(sums_out)
    for s in range(1, depth + 1):
        src = phis[s - 1]
        for z in range(s, layers - s):

            def put(at, total, s=s, z=z):
                if s < depth:
                    phis[s][z, at] = total
                    if z - s < 2:
                        state[0, s - 1, z - s, at] = total
                    if z - (layers - s - 2) >= 0:
                        state[1, s - 1, z - (layers - s - 2), at] = total
                else:
                    window_out[z - depth, at] = total
                    sums_out[at] += total

            sweep_layer(
                lambda at, z=z, src=src: src[z, at],
                lambda at, z=z, src=src: src[z + 1, at],
                lambda at, z=z, src=src: src[z - 1, at],
                lambda k, at, z=z: w[k, z, at],
                lambda at, z=z: b[z, at],
                tiles,
                sub,
                put,
            )
    charge_copy.wait()


class Wedge:
    def __init__(self, near, layers):
        d = lax.axis_index("drift")
        odd = lax.rem(d, 2)
        self.n, self.d = layers, d
        self.high = (1 - odd) if near else odd
        self.is_high = self.high == 1

    def own(self, q):
        return jnp.where(self.is_high, self.n - 1 - q, q)

    def sent(self, q, count):
        return jnp.where(self.is_high, -q - 1, count + q)

    def alive(self, q):
        z = self.d * self.n + self.own(q)
        return jnp.where((z >= 0) & (z < lax.axis_size("drift") * self.n), 1.0, 0.0)


def wedge_couplings(wedge, halo, halo_at, charge, ex, geo, wb, bb, eh):
    depth = SWEEPS
    rows, sector = eh.shape[1:]
    sub = lax.broadcasted_iota(jnp.int32, (ROWS, sector), 0)
    for q in range(-depth, 2):
        eh[depth + q] = halo[halo_at + wedge.sent(q, depth)] if q < 0 else ex[wedge.own(q)]
    for k in range(depth):
        q = k + 1 - depth
        bb[k] = charge(q) if q < 0 else jnp.ones_like(bb[0])

        def put(at, values, twice, k=k):
            for j, value in enumerate(values):
                wb[j, k, at] = value
            bb[k, at] = bb[k, at] * twice

        coupling_rows(
            k + 1, lambda i, at: eh[i, at], k + 2, k, geo, wedge.alive(q), rows // ROWS, sub, put
        )


def wedge_sweeps(wedge, halo, p0, w, wb, bb, state, b_in, q_buf, out, sums):
    depth = SWEEPS
    rows, sector = p0.shape[1:]
    sub = lax.broadcasted_iota(jnp.int32, (ROWS, sector), 0)

    def phi_at(s, q):
        if s == 0:
            if q < 0:
                spot = wedge.sent(q, depth)
                return lambda at: halo[spot, at]
            spot = wedge.own(q)
            return lambda at: p0[spot, at]
        if q >= s:
            spot = jnp.where(wedge.is_high, 1 - (q - s), q - s)
            return lambda at: state[wedge.high, s - 1, spot, at]
        return lambda at: q_buf[s - 1, q - s + depth, at]

    def coupling(q):
        if q <= 0:
            return lambda j, at: wb[j, q + depth - 1, at]
        z = wedge.own(q)
        inward, outward = wedge.high, 1 - wedge.high
        return lambda j, at: w[(inward, outward, 2, 3, 4, 5)[j], z, at]

    for s in range(1, depth + 1):
        for q in range(s - depth, s):
            if q <= 0:
                b_at = lambda at, q=q: bb[q + depth - 1, at]
            else:
                b_at = lambda at, z=wedge.own(q): b_in[z, at]

            def put(at, total, s=s, q=q):
                if s < depth:
                    q_buf[s - 1, q - s + depth, at] = total
                else:
                    out[jnp.where(wedge.is_high, depth - 1 - q, q), at] = total
                    sums[at] += total

            sources = phi_at(s - 1, q), phi_at(s - 1, q + 1), phi_at(s - 1, q - 1)
            sweep_layer(*sources, coupling(q), b_at, rows // ROWS, sub, put)


def near_coupling_kernel(inner, ex, geo, wb, bb, eh):
    wedge = Wedge(True, ex.shape[0])
    wedge_couplings(wedge, inner, SWEEPS, lambda q: jnp.ones_like(bb[0]), ex, geo, wb, bb, eh)


def near_kernel(inner, swapped, p0, w, wb, bb_in, state, b_in, sums_in, out, sums_out, bb, q_buf):
    wedge = Wedge(True, p0.shape[0])
    ends = SWEEPS - 1
    for k in range(ends):
        bb[k] = bb_in[k] * swapped[wedge.sent(k - ends, ends)]
    bb[ends] = bb_in[ends] * b_in[wedge.own(0)]
    sums_out[...] = sums_in[...]
    wedge_sweeps(wedge, inner, p0, w, wb, bb, state, b_in, q_buf, out, sums_out)


def outer_coupling_kernel(band, inner, outer_eps, far, ex, geo, wb, bb, eh, halo):
    wedge = Wedge(False, ex.shape[0])
    ends = SWEEPS - 1

    def charge(q):
        spot = wedge.sent(q, ends)
        ions = jnp.where(wedge.is_high, inner[2 * SWEEPS + spot], far[spot])
        return drift_charge(ions, geo[6], geo[7], jnp.where(wedge.is_high, wedge.d + 1, wedge.d - 1))

    unpack_halo(outer_eps, halo, band)
    wedge_couplings(wedge, halo, 0, charge, ex, geo, wb, bb, eh)


def outer_relax_kernel(band, outer_phi, p0, w, wb, bb_in, state, b_in, sums_in, out, sums_out, bb, q_buf, halo):
    wedge = Wedge(False, p0.shape[0])
    ends = SWEEPS - 1
    for k in range(ends):
        bb[k] = bb_in[k]
    bb[ends] = bb_in[ends] * b_in[wedge.own(0)]
    sums_out[...] = sums_in[...]
    unpack_halo(outer_phi, halo, band)
    wedge_sweeps(wedge, halo, p0, w, wb, bb, state, b_in, q_buf, out, sums_out)


def local_kernel(near, inner, far, potential, out, run):
    _, band, _ = potential.shape
    tiles = run.shape[0] // ROWS
    run[...] = jnp.zeros_like(run)
    odd = lax.rem(lax.axis_index("drift"), 2) == 1
    base = 0
    for count, value_of in (
        (near.shape[0], lambda k, at: jnp.where(odd, near[k, at], far[k, at])),
        (inner.shape[0], lambda k, at: inner[k, at]),
        (far.shape[0], lambda k, at: jnp.where(odd, far[k, at], near[k, at])),
    ):

        @pl.loop(0, count)
        def _(k, value_of=value_of, base=base):
            for t in range(tiles):
                at = slice(t * ROWS, (t + 1) * ROWS)
                value = value_of(k, at)
                run[at] += value
                if t < band // ROWS:
                    potential[base + k, at] = value

            def put(at, first, second):
                out[0, base + k, at] = first
                out[1, base + k, at] = second

            ratios_of(run, band, put)

        base += count


def ratios_of(field, band, put):
    rows, sector = field.shape
    r, bands = lax.axis_index("radius"), lax.axis_size("radius")
    total_r = band * bands
    sub = lax.broadcasted_iota(jnp.int32, (ROWS, sector), 0)
    lane = lax.broadcasted_iota(jnp.int32, (ROWS, sector), 1)
    scale = 1.0 / (8.0 * 1.09)
    for t, at, x, higher, lower in row_tiles(lambda s: field[s], rows // ROWS, sub):
        if t < band // ROWS:
            row = sub + (t * ROWS + r * band)
            rpos = ((total_r + row).astype(F32) + 0.5) / total_r
            right = jnp.where(lane == sector - 1, 0.0, roll(x, -1, 1))
            left = jnp.where(lane == 0, 0.0, roll(x, 1, 1))
            higher = jnp.where(row == total_r - 1, 0.0, higher)
            lower = jnp.where(row == 0, 0.0, lower)
            er = (lower - higher) * (0.5 * scale)
            ea = (left - right) * (0.5 * scale / rpos)
            put(at, er + 0.3 * ea, ea - 0.3 * er)


def offset_kernel(local, prefix, out, shift, stage, sems):
    layers = local.shape[1]
    copies = []

    def put(at, first, second):
        shift[0, at] = first
        shift[1, at] = second

    ratios_of(prefix, local.shape[2], put)
    parts = sems.shape[0]
    each = layers // parts
    for k in range(parts):
        for c in range(2):
            stage[c, k * each : (k + 1) * each] = local[c, k * each : (k + 1) * each] + shift[c]
        copy = pltpu.make_async_copy(
            stage.at[:, k * each : (k + 1) * each], out.at[:, k * each : (k + 1) * each], sems.at[k]
        )
        copy.start()
        copies.append(copy)
    for copy in copies:
        copy.wait()


def sums_below(sums):
    count, mine = lax.axis_size("drift"), lax.axis_index("drift")
    assert count & (count - 1) == 0
    total, below, step = sums, jnp.zeros_like(sums), 1
    while step < count:
        other = lax.ppermute(total, "drift", [(i, i ^ step) for i in range(count)])
        below = below + jnp.where((mine & step) > 0, other, 0.0)
        total = total + other
        step *= 2
    return below


def kernel(function, out_shape, in_specs, out_specs=None, scratch=(), mb=16):
    return pl.pallas_call(
        function,
        out_shape=out_shape,
        in_specs=in_specs,
        out_specs=out_specs if out_specs is not None else [IN_VMEM] * len(out_shape),
        scratch_shapes=list(scratch),
        compiler_params=pltpu.CompilerParams(vmem_limit_bytes=mb << 20),
    )


def body(ions, potential_guess, permittivity, recombination, rate_index, gap_mask, rate_table):
    layers, band, sector = ions.shape
    depth = SWEEPS
    sides = 1 if lax.axis_size("radius") == 2 else 2
    rows = band + sides * ROWS
    dma = pltpu.SemaphoreType.DMA
    ends = depth - 1
    row_block = 2 * layers + 2 * ends + 2
    far_args = (potential_guess, permittivity, ions, recombination, rate_index, gap_mask, rate_table)
    phi, eps, ions_far, *pad_args = [pltpu.with_memory_space_constraint(x, pltpu.HBM) for x in far_args]

    moved = shifted(ions, "drift", 2)

    def swap_rows(blocks):
        if sides == 1:
            return [lax.ppermute(blocks[0], "radius", [(0, 1), (1, 0)])]
        return [shifted(blocks[0], "radius", -1), shifted(blocks[1], "radius", 1)]

    ion_blocks = kernel(
        ion_rows_kernel,
        [plane(layers // 2, ROWS, sector)] * sides,
        [ANYWHERE],
        scratch=[near(layers, ROWS, sector)] * sides + [dma((sides,))],
        mb=3,
    )(ions_far)
    ion_raws = swap_rows(ion_blocks)
    *blocks, pads = kernel(
        rows_kernel,
        [plane(row_block, ROWS, sector)] * sides + [plane(2, band, sector)],
        [ANYWHERE] * 7,
        scratch=[
            near(band, sector),
            pltpu.VMEM((band, sector), jnp.int32),
            pltpu.VMEM((band, sector), jnp.int32),
            pltpu.SMEM(rate_table.shape, F32),
            dma((4 * sides,)),
            dma((4,)),
        ],
        mb=5,
    )(phi, eps, ions_far, *pad_args)
    raws = swap_rows(blocks)
    rows_moved = [shifted(raw, "drift", 2) for raw in ion_raws]
    packed = depth * band + sides * (depth // 2) * ROWS
    to_core, eps_block, phi_block, beyond = kernel(
        functools.partial(halo_kernel, sides),
        [
            plane(3 * depth - 1, rows, sector),
            plane(packed, sector),
            plane(packed, sector),
            plane(depth - 1, rows, sector),
        ],
        [ANYWHERE] * 3 + [IN_VMEM] * sides,
        scratch=[dma((4 * (1 + sides) + 2 * depth,))],
        mb=6,
    )(phi, eps, ions_far, *raws)
    count = lax.axis_size("drift")
    assert count % 2 == 0
    partners = [(i, i ^ 1) for i in range(count)]
    chips = [(i, i + 1 if i % 2 else i - 1) for i in range(1, count - 1)]
    outer_eps = lax.ppermute(eps_block, "drift", chips)
    far = lax.ppermute(beyond, "drift", [(i - 3, i) for i in range(4, count, 2)])
    inner = lax.ppermute(to_core, "drift", partners)
    outer_phi = lax.ppermute(phi_block, "drift", chips)

    box = plane(layers, rows, sector)
    p0, ex, w, inv2, geo = kernel(
        functools.partial(inner_coupling_kernel, sides),
        [box, box, plane(6, layers, rows, sector), box, plane(10, rows, sector)],
        [IN_VMEM] * (3 + sides),
        mb=20,
    )(potential_guess, permittivity, pads, *raws)
    p0, ex, w, inv2, geo = [fetched(x) for x in (p0, ex, w, inv2, geo)]
    wedge = plane(depth, rows, sector)
    wedge_box = near(depth, rows, sector)
    near_w, near_b = kernel(
        near_coupling_kernel,
        [plane(6, depth, rows, sector), wedge],
        [IN_VMEM] * 3,
        scratch=[near(depth + 2, rows, sector)],
        mb=12,
    )(inner, ex, geo)
    near_w, near_b = fetched(near_w), fetched(near_b)
    wb, bb = kernel(
        functools.partial(outer_coupling_kernel, band),
        [plane(6, depth, rows, sector), wedge],
        [IN_VMEM] * 5,
        scratch=[near(depth + 2, rows, sector), wedge_box],
        mb=12,
    )(inner, outer_eps, far, ex, geo)
    wb, bb = fetched(wb), fetched(bb)
    raw, swap, b = kernel(
        functools.partial(charge_kernel, sides),
        [box, plane(depth - 1, rows, sector), box],
        [IN_VMEM] * (3 + sides),
        mb=8,
    )(moved, inv2, geo, *rows_moved)
    raw, b = fetched(raw), fetched(b)
    swapped = lax.ppermute(swap, "drift", partners)
    charge, middle, sums, state = kernel(
        inner_relax_kernel,
        [
            plane(layers, band, sector),
            plane(layers - 2 * depth, rows, sector),
            plane(rows, sector),
            plane(2, depth - 1, 2, rows, sector),
        ],
        [IN_VMEM] * 4,
        [ANYWHERE] + [IN_VMEM] * 3,
        scratch=[near(layers, rows, sector)] * 3 + [dma],
        mb=12,
    )(p0, w, b, raw)
    state, sums = fetched(state), fetched(sums)
    near_out, sums = kernel(
        near_kernel,
        [wedge, plane(rows, sector)],
        [IN_VMEM] * 9,
        scratch=[wedge_box, near(depth - 1, depth, rows, sector)],
        mb=12,
    )(inner, swapped, p0, w, near_w, near_b, state, b, sums)
    far_out, sums = kernel(
        functools.partial(outer_relax_kernel, band),
        [wedge, plane(rows, sector)],
        [IN_VMEM] * 8,
        scratch=[wedge_box, near(depth - 1, depth, rows, sector), wedge_box],
        mb=12,
    )(outer_phi, p0, w, wb, bb, state, b, fetched(sums))
    potential, local = kernel(
        local_kernel,
        [plane(layers, band, sector), plane(2, layers, band, sector)],
        [IN_VMEM] * 3,
        scratch=[near(rows, sector)],
        mb=16,
    )(near_out, middle, far_out)
    below_sums = sums_below(sums)
    distortion = kernel(
        offset_kernel,
        plane(2, layers, band, sector),
        [IN_VMEM] * 2,
        ANYWHERE,
        [near(2, band, sector), near(2, layers, band, sector), dma((4,))],
        mb=12,
    )(fetched(local), below_sums)
    return charge, potential, distortion


def solution(mesh):
    return jax.shard_map(
        body,
        mesh=mesh,
        in_specs=(
            P("drift", "radius", None),
            P("drift", "radius", None),
            P("drift", "radius", None),
            P("radius", None),
            P("radius", None),
            P("radius", None),
            P(),
        ),
        out_specs=(
            P("drift", "radius", None),
            P("drift", "radius", None),
            P(None, "drift", "radius", None),
        ),
        check_vma=False,
    )
```
